256 devices in a mesh: member: 8 (over z_hi, core), lat: 32 (over y, z_lo, x).
Axes of the slice: x: 4, y: 4, z: 8 (z_hi: 4, z_lo: 2; z = z_hi * 2 + z_lo), core: 2. Of those that a mesh axis runs over, the one named last changes fastest.
Arguments:
- ensemble: bfloat16 [16, 64, 128, 256], P('member', None, 'lat'), may hold values from -6 to 6
- cotangent: bfloat16 [16, 64, 128, 256], P('member', None, 'lat'), may hold values from -6 to 6
- conv_in: bfloat16 [3, 3, 64, 128], replicated, may hold values from -0.25 to 0.25
- pool_weight: bfloat16 [256, 128], replicated, may hold values from -1 to 1
- conv_out: bfloat16 [3, 3, 128, 64], replicated, may hold values from -0.1875 to 0.1875
Outputs:
- encoded: bfloat16 [16, 64, 128, 256], P('member', None, 'lat')
- d_input: bfloat16 [16, 64, 128, 256], P('member', None, 'lat')
- grad_conv_in: float32 [3, 3, 64, 128], replicated
- grad_pool: float32 [256, 128], replicated
- grad_conv_out: float32 [3, 3, 128, 64], replicated
The draws below stay inside these ranges and needn't reach their ends.
All inputs are finite; a program needn't handle non-finite values.
Results may differ from the reference program's by a relative error of at most 0.0085.
Values may be sent and summed in bfloat16 or wider, within the bound.
No kernel may reach another device: no remote copies, remote signals or barrier semaphores. Data moves between devices by JAX's collectives and lax.ppermute only.
A program may use at most 64 MiB of HBM per device.

```python
import math
import jax
import jax.numpy as jnp
from jax import lax

V = 64
C = 128
LON = 256
MEMBERS = 16
NLAT = 128


def levels(own_key, shape, cuts, least, high):
    factor_of = 1.0
    for position, blocks in cuts:
        draws = jax.random.uniform(jax.random.fold_in(jax.random.fold_in(own_key, 6), position), (blocks,), jnp.float32, least / len(cuts), high / len(cuts))
        factor_of = factor_of * jnp.repeat(jnp.exp(draws), shape[position] // blocks).reshape((-1,) + (1,) * (len(shape) - 1 - position))
    return factor_of


def normal_values(rng, extent, scale, reach, shards=(), kind=jnp.bfloat16):
    values = scale * jax.random.normal(rng, extent, jnp.float32)
    if shards:
        values = values * levels(rng, extent, shards, -0.22, 0.18)
    return jnp.clip(values, -reach, reach).astype(kind)


def setup_inputs(seed: int = 0) -> dict:
    key_list = jax.random.split(jax.random.key(seed), 6)
    return {
        "ensemble": normal_values(key_list[0], (MEMBERS, V, NLAT, LON), 1.0, 6.0, ((0, 8), (2, 32))),
        "cotangent": normal_values(key_list[1], (MEMBERS, V, NLAT, LON), 1.0, 6.0, ((0, 8), (2, 32))),
        "conv_in": normal_values(key_list[2], (3, 3, V, C), (9 * V) ** -0.5, 0.25),
        "pool_weight": normal_values(key_list[3], (2 * C, C), (C // 4) ** -0.5, 1.0),
        "conv_out": normal_values(key_list[4], (3, 3, C, V), (9 * C) ** -0.5, 0.1875),
    }


def wrap_longitude(field):
    return jnp.concatenate([field[..., -1:], field, field[..., :1]], axis=3)

def pad_rows(field):
    return jnp.pad(field, ((0, 0), (0, 0), (1, 1), (0, 0)))

def convolve(padded_rows, kernel):
    return lax.conv_general_dilated(wrap_longitude(padded_rows), kernel, (1, 1), 'VALID', dimension_numbers=('NCHW', 'HWIO', 'NCHW'), preferred_element_type=jnp.float32)

def flipped(kernel):
    return jnp.transpose(kernel[::-1, ::-1], (0, 1, 3, 2))

def kernel_grad(padded_rows, output_grad):
    return lax.conv_general_dilated(wrap_longitude(padded_rows), output_grad, (1, 1), 'VALID', dimension_numbers=('CNHW', 'IOHW', 'HWNC'), preferred_element_type=jnp.float32)

def silu_slope(values):
    sigma = jax.nn.sigmoid(values)
    return sigma * (1.0 + values * (1.0 - sigma))

def reference(ensemble, cotangent, conv_in, pool_weight, conv_out):
    ens_rows = pad_rows(ensemble)
    pre = convolve(ens_rows, conv_in)
    active = jax.nn.silu(pre).astype(jnp.bfloat16)
    active_wide = active.astype(jnp.float32)
    average = lax.optimization_barrier(jnp.mean(active_wide, axis=0))
    spread = jnp.sqrt(lax.optimization_barrier(jnp.mean((active_wide - average) ** 2, axis=0)) + 0.1)
    stats = jnp.concatenate([average, spread], axis=0)
    pool_wide = pool_weight.astype(jnp.float32)
    shared = jnp.einsum('kc,khw->chw', pool_wide, stats, precision=lax.Precision.HIGHEST)
    zed = active_wide + shared
    hidden = jax.nn.silu(zed).astype(jnp.bfloat16)
    hid_rows = pad_rows(hidden)
    encoded = (ensemble.astype(jnp.float32) + convolve(hid_rows, conv_out)).astype(jnp.bfloat16)
    d_hidden = convolve(pad_rows(cotangent), flipped(conv_out))
    d_zed = (d_hidden * silu_slope(zed)).astype(jnp.bfloat16)
    grad_out = kernel_grad(hid_rows, cotangent)
    d_shared = lax.optimization_barrier(jnp.sum(d_zed.astype(jnp.float32), axis=0))
    d_stats = jnp.einsum('kc,chw->khw', pool_wide, d_shared, precision=lax.Precision.HIGHEST)
    grad_pool = jnp.einsum('khw,chw->kc', stats, d_shared, precision=lax.Precision.HIGHEST)
    d_active = d_zed.astype(jnp.float32) + d_stats[:C] / MEMBERS + d_stats[C:] * (active_wide - average) / (MEMBERS * spread)
    d_pre = (d_active * silu_slope(pre)).astype(jnp.bfloat16)
    d_input = (cotangent.astype(jnp.float32) + convolve(pad_rows(d_pre), flipped(conv_in))).astype(jnp.bfloat16)
    grad_in = kernel_grad(ens_rows, d_pre)
    grad_scale = 1.0 / math.sqrt(MEMBERS * NLAT * LON)
    return (encoded, d_input, grad_in * grad_scale, grad_pool * grad_scale, grad_out * grad_scale)
```

```python
import math

import jax
import jax.numpy as jnp
from jax import lax
from jax.experimental import pallas as pl
from jax.experimental.pallas import tpu as pltpu
from jax.sharding import PartitionSpec as P

BF = jnp.bfloat16
F32 = jnp.float32
BOTH = ("member", "lat")
WIDE = 80


def ring(count, shift):
    return [(i, (i + shift) % count) for i in range(count)]


def sigmoid(v):
    return 1.0 / (1.0 + jnp.exp(-v))


def split3(v):
    a = v.astype(BF)
    r = v - a.astype(F32)
    b = r.astype(BF)
    c = (r - b.astype(F32)).astype(BF)
    return a, b, c


def dot(a, b):
    return jnp.dot(a, b, preferred_element_type=F32)


def dot_t(a, b, dims):
    return lax.dot_general(a, b, (dims, ((), ())), preferred_element_type=F32)


def dot_rows(a, b):
    return dot_t(a, b, ((0,), (0,)))


def tile_kernel(
    lat_ref, own_ref, top_ref, bot_ref, w1_ref, w2_ref, pool_ref,
    out_ref, grads_ref,
    pre_s, dh_s, act_s, xo_s, hq_s, dpo_s, sum_s, var_s, shared_s, ca_s, cs_s,
):
    srcs, rows, width, _ = own_ref.shape
    inner = rows + 2
    cols = xo_s.shape[2]
    nlat = lat_ref[1]
    members = 2 * srcs
    channels = pre_s.shape[-1]
    shape = (inner, WIDE, channels)

    def up(v, n):
        return pltpu.roll(v, WIDE - n, 1) if n else v

    parity = lax.broadcasted_iota(jnp.int32, shape, 1) % 2

    def pair_sum(v):
        return v + jnp.where(parity == 0, up(v, 1), pltpu.roll(v, 1, 1))

    row_id = lax.broadcasted_iota(jnp.int32, shape, 0) + lat_ref[0] * rows - 1
    inside = jnp.logical_and(row_id >= 0, row_id < nlat)

    sum_s[...] = jnp.zeros(shape, F32)

    def first(s, carry):
        x = jnp.concatenate([top_ref[s], own_ref[s], bot_ref[s]], axis=0).astype(F32)
        x = jnp.concatenate([x, jnp.zeros((rows + 4, WIDE - width, 128), F32)], axis=1)
        x1, x2, x3 = up(x, 2), up(x, 4), up(x, 6)
        xs = jnp.concatenate([x, x1, x2], axis=-1).astype(BF)
        xo_s[s] = jnp.concatenate([v[1 : 1 + inner, :cols] for v in (x1, x2, x3)], axis=-1).astype(BF)
        acc = dot(xs[0:inner].reshape(inner * WIDE, 384), w1_ref[0])
        acc += dot(xs[1 : 1 + inner].reshape(inner * WIDE, 384), w1_ref[1])
        acc += dot(xs[2 : 2 + inner].reshape(inner * WIDE, 384), w1_ref[2])
        pre = acc[:, :channels].reshape(shape)
        pre_s[s] = pre
        dh_s[s] = acc[:, channels:].reshape(shape)
        act = (pre * sigmoid(pre)).astype(BF).astype(F32)
        act_s[s] = act
        sum_s[...] += act
        return carry

    lax.fori_loop(0, srcs, first, 0)
    average = pair_sum(sum_s[...]) * (1.0 / members)
    sum_s[...] = average
    var_s[...] = jnp.zeros(shape, F32)

    def second(s, carry):
        d = act_s[s] - sum_s[...]
        var_s[...] += d * d
        return carry

    lax.fori_loop(0, srcs, second, 0)
    spread = jnp.sqrt(pair_sum(var_s[...]) * (1.0 / members) + 0.1)
    var_s[...] = spread
    stats = jnp.concatenate([sum_s[...], spread], axis=-1).reshape(inner * WIDE, 2 * channels)
    s1, s2, s3 = split3(stats)
    pool = pool_ref[...]
    shared_s[...] = (dot(s1, pool) + dot(s2, pool) + dot(s3, pool)).reshape(shape)
    ca_s[...] = jnp.zeros(shape, F32)

    def third(s, carry):
        zed = act_s[s] + shared_s[...]
        sig = sigmoid(zed)
        hid = jnp.where(inside, (zed * sig).astype(BF).astype(F32), 0.0)
        dz = (dh_s[s] * (sig * (1.0 + zed * (1.0 - sig)))).astype(BF).astype(F32)
        dh_s[s] = dz
        ca_s[...] += dz
        hq_s[s] = jnp.concatenate([up(hid, 2 * q)[:, :cols] for q in range(3)], axis=-1).astype(BF)
        return carry

    lax.fori_loop(0, srcs, third, 0)
    d_shared = pair_sum(ca_s[...])
    d1, d2, d3 = split3(d_shared.reshape(inner * WIDE, channels))
    last = ((1,), (1,))
    d_stats = dot_t(d1, pool, last) + dot_t(d2, pool, last) + dot_t(d3, pool, last)
    ca_s[...] = (d_stats[:, :channels] * (1.0 / members)).reshape(shape)
    cs_s[...] = d_stats[:, channels:].reshape(shape) / (members * var_s[...])
    r_id = lax.broadcasted_iota(jnp.int32, shape, 0)
    c_id = lax.broadcasted_iota(jnp.int32, shape, 1)
    mine = (r_id >= 1) & (r_id <= rows) & (c_id >= 2) & (c_id < 2 + cols) & (parity == 0)
    e1, e2, e3 = split3(jnp.where(mine, d_shared, 0.0).reshape(inner * WIDE, channels))
    g_pool = dot_rows(s1, e1) + dot_rows(s1, e2) + dot_rows(s2, e1) + dot_rows(s2, e2) + dot_rows(s1, e3) + dot_rows(s3, e1)

    def fourth(s, carry):
        pre = pre_s[s]
        sig = sigmoid(pre)
        d_act = dh_s[s] + ca_s[...] + cs_s[...] * (act_s[s] - sum_s[...])
        dp = jnp.where(inside, d_act * (sig * (1.0 + pre * (1.0 - sig))), 0.0).astype(BF).astype(F32)
        dq = jnp.concatenate([up(dp, 2 * q)[:, :cols] for q in range(3)], axis=-1).astype(BF)
        dpo_s[s] = dq[1 : 1 + rows, :, channels : 2 * channels]
        hq = hq_s[s]
        both = jnp.concatenate([hq, dq], axis=-1)
        acc = dot(both[0:rows].reshape(rows * cols, 6 * channels), w2_ref[0])
        acc += dot(both[1 : 1 + rows].reshape(rows * cols, 6 * channels), w2_ref[1])
        acc += dot(both[2 : 2 + rows].reshape(rows * cols, 6 * channels), w2_ref[2])
        own = xo_s[s, 1 : 1 + rows, :, 128:256].astype(F32)
        out_ref[s] = (own + acc.reshape(rows, cols, 128)).astype(BF)
        return carry

    lax.fori_loop(0, srcs, fourth, 0)

    total = srcs * rows * cols
    dpo = dpo_s[...].reshape(total, channels)
    own = xo_s[:, 1 : 1 + rows, :, 128:256].reshape(total, 128)
    half = channels // 2
    for p in range(3):
        g_in = dot_rows(dpo, xo_s[:, p : p + rows].reshape(total, 384))
        g_out = dot_rows(own, hq_s[:, p : p + rows].reshape(total, 384))
        for q in range(3):
            t = 3 * p + q
            grads_ref[t * half : (t + 1) * half, :] = g_in[:, q * 128 : (q + 1) * 128].T[:half].astype(BF)
            grads_ref[(9 + t) * half : (10 + t) * half, :] = g_out[half:, q * 128 : (q + 1) * 128].astype(BF)
    used = 18 * half + 2 * channels
    grads_ref[18 * half : used, :] = g_pool.astype(BF)
    if used < grads_ref.shape[0]:
        grads_ref[used:, :] = jnp.zeros((grads_ref.shape[0] - used, 128), BF)


def sum_kernel(parts_ref, out_ref):
    total = jnp.sum(parts_ref[...].astype(F32), axis=0)
    out_ref[...] = jnp.broadcast_to(total[None], out_ref.shape).astype(BF)


def on_device(ensemble, cotangent, conv_in, pool_weight, conv_out):
    mem_local, var_count, rows, lon = ensemble.shape
    groups = lax.axis_size("member")
    bands = lax.axis_size("lat")
    channels = conv_in.shape[-1]
    cols = lon // groups
    width = (cols + 4) * mem_local
    both = jnp.concatenate([ensemble, cotangent], axis=1)
    both = both.transpose(2, 3, 0, 1)
    wrapped = jnp.concatenate([both[:, -2:], both, both[:, :2]], axis=1)
    chunks = jnp.stack(
        [wrapped[:, k * cols : k * cols + cols + 4].reshape(rows, width, 128) for k in range(groups)]
    )
    own = lax.all_to_all(chunks, "member", split_axis=0, concat_axis=0, tiled=True)
    top = lax.ppermute(own[:, rows - 2 :], "lat", [(i, i + 1) for i in range(bands - 1)])
    bot = lax.ppermute(own[:, :2], "lat", [(i + 1, i) for i in range(bands - 1)])

    flip_in = jnp.transpose(conv_in[::-1, ::-1], (0, 1, 3, 2))
    flip_out = jnp.transpose(conv_out[::-1, ::-1], (0, 1, 3, 2))
    z1 = jnp.zeros_like(conv_in)
    z2 = jnp.zeros_like(conv_out)
    w1 = jnp.concatenate(
        [jnp.concatenate([conv_in, z1], axis=3), jnp.concatenate([z1, flip_out], axis=3)], axis=2
    ).reshape(3, 384, 256)
    w2 = jnp.concatenate(
        [
            jnp.concatenate([conv_out, z2], axis=3).reshape(3, 384, 128),
            jnp.concatenate([z2, flip_in], axis=3).reshape(3, 384, 128),
        ],
        axis=1,
    )
    lat = jnp.stack([lax.axis_index("lat"), jnp.int32(bands * rows)]).astype(jnp.int32)
    inner = rows + 2
    plane = (inner, WIDE, channels)
    vm = pltpu.VMEM
    count = groups * bands
    used = 18 * (channels // 2) + 2 * channels
    per = -(-used // (8 * count)) * 8
    vspec = pl.BlockSpec(memory_space=pltpu.VMEM)
    out, grads = pl.pallas_call(
        tile_kernel,
        out_shape=(
            jax.ShapeDtypeStruct((groups, rows, cols * mem_local, 128), BF),
            jax.ShapeDtypeStruct((count * per, channels), BF),
        ),
        in_specs=[pl.BlockSpec(memory_space=pltpu.SMEM)] + [vspec] * 6,
        out_specs=(vspec, vspec),
        scratch_shapes=[
            vm((groups,) + plane, F32),
            vm((groups,) + plane, F32),
            vm((groups,) + plane, F32),
            vm((groups, inner, cols * mem_local, 384), BF),
            vm((groups, inner, cols * mem_local, 384), BF),
            vm((groups, rows, cols * mem_local, channels), BF),
            vm(plane, F32),
            vm(plane, F32),
            vm(plane, F32),
            vm(plane, F32),
            vm(plane, F32),
        ],
        compiler_params=pltpu.CompilerParams(vmem_limit_bytes=56 * 1024 * 1024),
        name="tile",
    )(lat, own, top, bot, w1, w2, pool_weight)

    grads = grads.reshape(count, per, channels)
    parts = lax.all_to_all(grads, BOTH, split_axis=0, concat_axis=0, tiled=True)
    shared = pl.pallas_call(
        sum_kernel,
        out_shape=jax.ShapeDtypeStruct((count, per, channels), BF),
        in_specs=[vspec],
        out_specs=vspec,
        name="total",
    )(parts)
    full = lax.all_to_all(shared, BOTH, split_axis=0, concat_axis=0, tiled=True)
    members = mem_local * groups
    scale = 1.0 / math.sqrt(members * bands * rows * lon)
    full = full.reshape(count * per, channels).astype(F32) * scale
    half = channels // 2
    grad_in = full[: 9 * half].reshape(3, 3, half, channels)
    grad_out = full[9 * half : 18 * half].reshape(3, 3, half, channels).transpose(0, 1, 3, 2)
    grad_pool = full[18 * half : used]

    back = lax.all_to_all(out, "member", split_axis=0, concat_axis=0, tiled=True)
    back = back.reshape(groups, rows, cols, mem_local, 128).transpose(3, 4, 1, 0, 2)
    back = back.reshape(mem_local, 128, rows, lon)
    return back[:, :var_count], back[:, var_count:], grad_in, grad_pool, grad_out


def solution(mesh):
    return jax.shard_map(
        on_device,
        mesh=mesh,
        in_specs=(P("member", None, "lat", None), P("member", None, "lat", None), P(), P(), P()),
        out_specs=(P("member", None, "lat", None), P("member", None, "lat", None), P(), P(), P()),
        check_vma=False,
    )
```

```python
import math

import jax
import jax.numpy as jnp
from jax import lax
from jax.experimental import pallas as pl
from jax.experimental.pallas import tpu as pltpu
from jax.sharding import PartitionSpec as P

BF = jnp.bfloat16
F32 = jnp.float32
BOTH = ("member", "lat")
WIDE = 80


def ring(count, shift):
    return [(i, (i + shift) % count) for i in range(count)]


def sigmoid(v):
    return 1.0 / (1.0 + jnp.exp(-v))


def split3(v):
    a = v.astype(BF)
    r = v - a.astype(F32)
    b = r.astype(BF)
    c = (r - b.astype(F32)).astype(BF)
    return a, b, c


def dot(a, b):
    return jnp.dot(a, b, preferred_element_type=F32)


def dot_t(a, b, dims):
    return lax.dot_general(a, b, (dims, ((), ())), preferred_element_type=F32)


def dot_rows(a, b):
    return dot_t(a, b, ((0,), (0,)))


def pack_kernel(me_ref, ens_ref, cot_ref, *refs):
    outs, plane = refs[:-1], refs[-1]
    groups = len(outs)
    mem_local, _, rows, lon = ens_ref.shape
    width = outs[0].shape[1]
    for m in range(mem_local):
        for r in range(rows):
            both = jnp.concatenate([ens_ref[m, :, r, :], cot_ref[m, :, r, :]], axis=0).astype(F32).T
            plane[r, pl.ds(4 + m, lon, stride=2), :] = both
            plane[r, pl.ds(m, 2, stride=2), :] = both[lon - 2 :]
            plane[r, pl.ds(4 + 2 * lon + m, 2, stride=2), :] = both[:2]
    for s in range(groups):
        k = lax.rem(me_ref[0] + s, groups)
        for r in range(rows):
            outs[s][r] = plane[r, pl.ds(pl.multiple_of(k * (width - 8), 8), width), :].astype(BF)


def edges_kernel(*refs):
    tiles, (head_ref, tail_ref) = refs[:-2], refs[-2:]
    for s, tile in enumerate(tiles):
        head_ref[s] = tile[:2]
        tail_ref[s] = tile[tile.shape[0] - 2 :]


def unpack_kernel(me_ref, *refs):
    tiles, (enc_ref, din_ref, plane) = refs[:-3], refs[-3:]
    groups = len(tiles)
    mem_local, half, rows, lon = enc_ref.shape
    width = tiles[0].shape[1]
    for s in range(groups):
        k = lax.rem(me_ref[0] + s, groups)
        for r in range(rows):
            plane[r, pl.ds(pl.multiple_of(k * width, 8), width), :] = tiles[s][r].astype(F32)
    for m in range(mem_local):
        for r in range(rows):
            both = plane[r, pl.ds(m, lon, stride=2), :].T.astype(BF)
            enc_ref[m, :, r, :] = both[:half]
            din_ref[m, :, r, :] = both[half:]


def tile_kernel(
    lat_ref, t0, t1, t2, t3, t4, t5, t6, t7, top_ref, bot_ref, w1_ref, w2_ref, pool_ref,
    o0, o1, o2, o3, o4, o5, o6, o7, grads_ref,
    own_ref, out_ref, pre_s, dh_s, act_s, xo_s, hq_s, dpo_s, sum_s, var_s, shared_s, ca_s, cs_s,
):
    srcs, rows, width, _ = own_ref.shape
    inner = rows + 2
    cols = xo_s.shape[2]
    nlat = lat_ref[1]
    for s, tile in enumerate((t0, t1, t2, t3, t4, t5, t6, t7)):
        own_ref[s] = tile[...]
    members = 2 * srcs
    channels = pre_s.shape[-1]
    shape = (inner, WIDE, channels)

    def up(v, n):
        return pltpu.roll(v, WIDE - n, 1) if n else v

    parity = lax.broadcasted_iota(jnp.int32, shape, 1) % 2

    def pair_sum(v):
        return v + jnp.where(parity == 0, up(v, 1), pltpu.roll(v, 1, 1))

    row_id = lax.broadcasted_iota(jnp.int32, shape, 0) + lat_ref[0] * rows - 1
    inside = jnp.logical_and(row_id >= 0, row_id < nlat)

    sum_s[...] = jnp.zeros(shape, F32)

    def first(s, carry):
        x = jnp.concatenate([top_ref[s], own_ref[s], bot_ref[s]], axis=0).astype(F32)
        x = jnp.concatenate([x, jnp.zeros((rows + 4, WIDE - width, 128), F32)], axis=1)
        x1, x2, x3 = up(x, 2), up(x, 4), up(x, 6)
        xs = jnp.concatenate([x, x1, x2], axis=-1).astype(BF)
        xo_s[s] = jnp.concatenate([v[1 : 1 + inner, :cols] for v in (x1, x2, x3)], axis=-1).astype(BF)
        acc = dot(xs[0:inner].reshape(inner * WIDE, 384), w1_ref[0])
        acc += dot(xs[1 : 1 + inner].reshape(inner * WIDE, 384), w1_ref[1])
        acc += dot(xs[2 : 2 + inner].reshape(inner * WIDE, 384), w1_ref[2])
        pre = acc[:, :channels].reshape(shape)
        pre_s[s] = pre
        dh_s[s] = acc[:, channels:].reshape(shape)
        act = (pre * sigmoid(pre)).astype(BF).astype(F32)
        act_s[s] = act
        sum_s[...] += act
        return carry

    lax.fori_loop(0, srcs, first, 0)
    average = pair_sum(sum_s[...]) * (1.0 / members)
    sum_s[...] = average
    var_s[...] = jnp.zeros(shape, F32)

    def second(s, carry):
        d = act_s[s] - sum_s[...]
        var_s[...] += d * d
        return carry

    lax.fori_loop(0, srcs, second, 0)
    spread = jnp.sqrt(pair_sum(var_s[...]) * (1.0 / members) + 0.1)
    var_s[...] = spread
    stats = jnp.concatenate([sum_s[...], spread], axis=-1).reshape(inner * WIDE, 2 * channels)
    s1, s2, s3 = split3(stats)
    pool = pool_ref[...]
    shared_s[...] = (dot(s1, pool) + dot(s2, pool) + dot(s3, pool)).reshape(shape)
    ca_s[...] = jnp.zeros(shape, F32)

    def third(s, carry):
        zed = act_s[s] + shared_s[...]
        sig = sigmoid(zed)
        hid = jnp.where(inside, (zed * sig).astype(BF).astype(F32), 0.0)
        dz = (dh_s[s] * (sig * (1.0 + zed * (1.0 - sig)))).astype(BF).astype(F32)
        dh_s[s] = dz
        ca_s[...] += dz
        hq_s[s] = jnp.concatenate([up(hid, 2 * q)[:, :cols] for q in range(3)], axis=-1).astype(BF)
        return carry

    lax.fori_loop(0, srcs, third, 0)
    d_shared = pair_sum(ca_s[...])
    d1, d2, d3 = split3(d_shared.reshape(inner * WIDE, channels))
    last = ((1,), (1,))
    d_stats = dot_t(d1, pool, last) + dot_t(d2, pool, last) + dot_t(d3, pool, last)
    ca_s[...] = (d_stats[:, :channels] * (1.0 / members)).reshape(shape)
    cs_s[...] = d_stats[:, channels:].reshape(shape) / (members * var_s[...])
    r_id = lax.broadcasted_iota(jnp.int32, shape, 0)
    c_id = lax.broadcasted_iota(jnp.int32, shape, 1)
    mine = (r_id >= 1) & (r_id <= rows) & (c_id >= 2) & (c_id < 2 + cols) & (parity == 0)
    e1, e2, e3 = split3(jnp.where(mine, d_shared, 0.0).reshape(inner * WIDE, channels))
    g_pool = dot_rows(s1, e1) + dot_rows(s1, e2) + dot_rows(s2, e1) + dot_rows(s2, e2) + dot_rows(s1, e3) + dot_rows(s3, e1)

    def fourth(s, carry):
        pre = pre_s[s]
        sig = sigmoid(pre)
        d_act = dh_s[s] + ca_s[...] + cs_s[...] * (act_s[s] - sum_s[...])
        dp = jnp.where(inside, d_act * (sig * (1.0 + pre * (1.0 - sig))), 0.0).astype(BF).astype(F32)
        dq = jnp.concatenate([up(dp, 2 * q)[:, :cols] for q in range(3)], axis=-1).astype(BF)
        dpo_s[s] = dq[1 : 1 + rows, :, channels : 2 * channels]
        hq = hq_s[s]
        both = jnp.concatenate([hq, dq], axis=-1)
        acc = dot(both[0:rows].reshape(rows * cols, 6 * channels), w2_ref[0])
        acc += dot(both[1 : 1 + rows].reshape(rows * cols, 6 * channels), w2_ref[1])
        acc += dot(both[2 : 2 + rows].reshape(rows * cols, 6 * channels), w2_ref[2])
        own = xo_s[s, 1 : 1 + rows, :, 128:256].astype(F32)
        out_ref[s] = (own + acc.reshape(rows, cols, 128)).astype(BF)
        return carry

    lax.fori_loop(0, srcs, fourth, 0)
    for s, piece in enumerate((o0, o1, o2, o3, o4, o5, o6, o7)):
        piece[...] = out_ref[s]

    total = srcs * rows * cols
    dpo = dpo_s[...].reshape(total, channels)
    own = xo_s[:, 1 : 1 + rows, :, 128:256].reshape(total, 128)
    half = channels // 2
    for p in range(3):
        g_in = dot_rows(dpo, xo_s[:, p : p + rows].reshape(total, 384))
        g_out = dot_rows(own, hq_s[:, p : p + rows].reshape(total, 384))
        for q in range(3):
            t = 3 * p + q
            grads_ref[t * half : (t + 1) * half, :] = g_in[:, q * 128 : (q + 1) * 128].T[:half].astype(BF)
            grads_ref[(9 + t) * half : (10 + t) * half, :] = g_out[half:, q * 128 : (q + 1) * 128].astype(BF)
    used = 18 * half + 2 * channels
    grads_ref[18 * half : used, :] = g_pool.astype(BF)
    if used < grads_ref.shape[0]:
        grads_ref[used:, :] = jnp.zeros((grads_ref.shape[0] - used, 128), BF)


def sum_kernel(parts_ref, out_ref):
    total = jnp.sum(parts_ref[...].astype(F32), axis=0)
    out_ref[...] = jnp.broadcast_to(total[None], out_ref.shape).astype(BF)


def on_device(ensemble, cotangent, conv_in, pool_weight, conv_out):
    mem_local, var_count, rows, lon = ensemble.shape
    groups = lax.axis_size("member")
    bands = lax.axis_size("lat")
    channels = conv_in.shape[-1]
    cols = lon // groups
    width = (cols + 4) * mem_local
    vspec = pl.BlockSpec(memory_space=pltpu.VMEM)
    sspec = pl.BlockSpec(memory_space=pltpu.SMEM)
    vm = pltpu.VMEM
    me = lax.axis_index("member").astype(jnp.int32).reshape(1)
    tiles = pl.pallas_call(
        pack_kernel,
        out_shape=[jax.ShapeDtypeStruct((rows, width, 128), BF)] * groups,
        in_specs=[sspec, vspec, vspec],
        out_specs=[vspec] * groups,
        scratch_shapes=[vm((rows, 2 * lon + 8, 128), F32)],
        name="pack",
    )(me, ensemble, cotangent)
    tiles = [tiles[0]] + [lax.ppermute(tiles[s], "member", ring(groups, s)) for s in range(1, groups)]
    head, tail = pl.pallas_call(
        edges_kernel,
        out_shape=[jax.ShapeDtypeStruct((groups, 2, width, 128), BF)] * 2,
        in_specs=[vspec] * groups,
        out_specs=[vspec] * 2,
        name="edges",
    )(*tiles)
    top = lax.ppermute(tail, "lat", [(i, i + 1) for i in range(bands - 1)])
    bot = lax.ppermute(head, "lat", [(i + 1, i) for i in range(bands - 1)])

    flip_in = jnp.transpose(conv_in[::-1, ::-1], (0, 1, 3, 2))
    flip_out = jnp.transpose(conv_out[::-1, ::-1], (0, 1, 3, 2))
    z1 = jnp.zeros_like(conv_in)
    z2 = jnp.zeros_like(conv_out)
    w1 = jnp.concatenate(
        [jnp.concatenate([conv_in, z1], axis=3), jnp.concatenate([z1, flip_out], axis=3)], axis=2
    ).reshape(3, 384, 256)
    w2 = jnp.concatenate(
        [
            jnp.concatenate([conv_out, z2], axis=3).reshape(3, 384, 128),
            jnp.concatenate([z2, flip_in], axis=3).reshape(3, 384, 128),
        ],
        axis=1,
    )
    lat = jnp.stack([lax.axis_index("lat"), jnp.int32(bands * rows)]).astype(jnp.int32)
    inner = rows + 2
    plane = (inner, WIDE, channels)
    count = groups * bands
    used = 18 * (channels // 2) + 2 * channels
    per = -(-used // (8 * count)) * 8
    *pieces, grads = pl.pallas_call(
        tile_kernel,
        out_shape=[jax.ShapeDtypeStruct((rows, cols * mem_local, 128), BF)] * groups
        + [jax.ShapeDtypeStruct((count * per, channels), BF)],
        in_specs=[sspec] + [vspec] * (groups + 5),
        out_specs=[vspec] * (groups + 1),
        scratch_shapes=[
            vm((groups, rows, width, 128), BF),
            vm((groups, rows, cols * mem_local, 128), BF),
            vm((groups,) + plane, F32),
            vm((groups,) + plane, F32),
            vm((groups,) + plane, F32),
            vm((groups, inner, cols * mem_local, 384), BF),
            vm((groups, inner, cols * mem_local, 384), BF),
            vm((groups, rows, cols * mem_local, channels), BF),
            vm(plane, F32),
            vm(plane, F32),
            vm(plane, F32),
            vm(plane, F32),
            vm(plane, F32),
        ],
        compiler_params=pltpu.CompilerParams(vmem_limit_bytes=56 * 1024 * 1024),
        name="tile",
    )(lat, *tiles, top, bot, w1, w2, pool_weight)

    grads = grads.reshape(count, per, channels)
    parts = lax.all_to_all(grads, BOTH, split_axis=0, concat_axis=0, tiled=True)
    shared = pl.pallas_call(
        sum_kernel,
        out_shape=jax.ShapeDtypeStruct((count, per, channels), BF),
        in_specs=[vspec],
        out_specs=vspec,
        name="total",
    )(parts)
    full = lax.all_to_all(shared, BOTH, split_axis=0, concat_axis=0, tiled=True)
    members = mem_local * groups
    scale = 1.0 / math.sqrt(members * bands * rows * lon)
    full = full.reshape(count * per, channels).astype(F32) * scale
    half = channels // 2
    grad_in = full[: 9 * half].reshape(3, 3, half, channels)
    grad_out = full[9 * half : 18 * half].reshape(3, 3, half, channels).transpose(0, 1, 3, 2)
    grad_pool = full[18 * half : used]

    pieces = [pieces[0]] + [
        lax.ppermute(pieces[s], "member", ring(groups, -s)) for s in range(1, groups)
    ]
    encoded, d_input = pl.pallas_call(
        unpack_kernel,
        out_shape=[jax.ShapeDtypeStruct(ensemble.shape, BF)] * 2,
        in_specs=[sspec] + [vspec] * groups,
        out_specs=[vspec] * 2,
        scratch_shapes=[vm((rows, 2 * lon, 128), F32)],
        name="unpack",
    )(me, *pieces)
    return encoded, d_input, grad_in, grad_pool, grad_out


def solution(mesh):
    return jax.shard_map(
        on_device,
        mesh=mesh,
        in_specs=(P("member", None, "lat", None), P("member", None, "lat", None), P(), P(), P()),
        out_specs=(P("member", None, "lat", None), P("member", None, "lat", None), P(), P(), P()),
        check_vma=False,
    )
```

```python
import functools
import math

import jax
import jax.numpy as jnp
from jax import lax
from jax.experimental import pallas as pl
from jax.experimental.pallas import tpu as pltpu
from jax.sharding import PartitionSpec as P

BF = jnp.bfloat16
F32 = jnp.float32
BOTH = ("member", "lat")
WIDE = 80


SLOTS = ((0, 0), (0, 1), (1, 0), (3, 0), (2, 0), (2, 1), (1, 1), (3, 1))
SPLIT = 4


def peer(device, slot, groups, sign=1):
    step, core = slot
    chips = groups // 2
    return 2 * ((device // 2 + chips + sign * step) % chips) + (device % 2 + core) % 2


def swap(value, slot, groups, sign):
    pairs = [(i, peer(i, slot, groups, sign)) for i in range(groups)]
    return lax.ppermute(value, "member", pairs)


def row_blocks(start, rows, count, pitch):
    step = math.gcd(rows, count, start)
    for off in range(0, rows, step):
        block, chunk = divmod(start + off, count)
        yield off, step, pl.ds(chunk * pitch + block, step, stride=pitch)


def sigmoid(v):
    return 1.0 / (1.0 + jnp.exp(-v))


def split3(v):
    a = v.astype(BF)
    r = v - a.astype(F32)
    b = r.astype(BF)
    c = (r - b.astype(F32)).astype(BF)
    return a, b, c


def dot(a, b):
    return jnp.dot(a, b, preferred_element_type=F32)


def dot_t(a, b, dims):
    return lax.dot_general(a, b, (dims, ((), ())), preferred_element_type=F32)


def dot_rows(a, b):
    return dot_t(a, b, ((0,), (0,)))


def pack_kernel(me_ref, ens_ref, cot_ref, *refs):
    outs, plane = refs[:-1], refs[-1]
    groups = len(outs)
    mem_local, _, rows, lon = ens_ref.shape
    width = outs[0].shape[1]
    for m in range(mem_local):
        for r in range(rows):
            both = jnp.concatenate([ens_ref[m, :, r, :], cot_ref[m, :, r, :]], axis=0).astype(F32).T
            plane[r, pl.ds(4 + m, lon, stride=2), :] = both
            plane[r, pl.ds(m, 2, stride=2), :] = both[lon - 2 :]
            plane[r, pl.ds(4 + 2 * lon + m, 2, stride=2), :] = both[:2]
    for s in range(groups):
        k = peer(me_ref[0], SLOTS[s], groups)
        for r in range(rows):
            outs[s][r] = plane[r, pl.ds(pl.multiple_of(k * (width - 8), 8), width), :].astype(BF)


def edges_kernel(n, *refs):
    tiles, (head_ref, tail_ref, sems) = refs[:n], refs[-3:]
    copies = []
    for s, tile in enumerate(tiles):
        copies.append(pltpu.make_async_copy(tile.at[pl.ds(0, 2)], head_ref.at[s], sems.at[2 * s]))
        copies.append(pltpu.make_async_copy(tile.at[pl.ds(tile.shape[0] - 2, 2)], tail_ref.at[s], sems.at[2 * s + 1]))
    for copy in copies:
        copy.start()
    for copy in copies:
        copy.wait()


def unpack_kernel(me_ref, *refs):
    tiles, (enc_ref, din_ref, plane) = refs[:-3], refs[-3:]
    groups = len(tiles)
    mem_local, half, rows, lon = enc_ref.shape
    width = tiles[0].shape[1]
    for s in range(groups):
        k = peer(me_ref[0], SLOTS[s], groups)
        for r in range(rows):
            plane[r, pl.ds(pl.multiple_of(k * width, 8), width), :] = tiles[s][r].astype(F32)
    for m in range(mem_local):
        for r in range(rows):
            both = plane[r, pl.ds(m, lon, stride=2), :].T.astype(BF)
            enc_ref[m, :, r, :] = both[:half]
            din_ref[m, :, r, :] = both[half:]


def tile_kernel(
    lat_ref, t0, t1, t2, t3, t4, t5, t6, t7, top0, top1, bot0, bot1, w1_ref, w2_ref, pool_ref,
    o0, o1, o2, o3, o4, o5, o6, o7, grads_ref,
    own_ref, top_ref, bot_ref, out_ref, pre_s, dh_s, act_s, xo_s, hq_s, dpo_s, sum_s, var_s, shared_s, ca_s, cs_s, chunk_s,
):
    srcs, rows, width, _ = own_ref.shape
    inner = rows + 2
    cols = xo_s.shape[2]
    nlat = lat_ref[1]
    for s, tile in enumerate((t0, t1, t2, t3, t4, t5, t6, t7)):
        own_ref[s] = tile[...]
    for ref, top, bot in ((0, top0, bot0), (SPLIT, top1, bot1)):
        top_ref[ref : ref + top.shape[0]] = top[...]
        bot_ref[ref : ref + bot.shape[0]] = bot[...]
    members = 2 * srcs
    channels = pre_s.shape[-1]
    shape = (inner, WIDE, channels)

    def up(v, n):
        return pltpu.roll(v, WIDE - n, 1) if n else v

    parity = lax.broadcasted_iota(jnp.int32, shape, 1) % 2

    def pair_sum(v):
        return v + jnp.where(parity == 0, up(v, 1), pltpu.roll(v, 1, 1))

    row_id = lax.broadcasted_iota(jnp.int32, shape, 0) + lat_ref[0] * rows - 1
    inside = jnp.logical_and(row_id >= 0, row_id < nlat)

    sum_s[...] = jnp.zeros(shape, F32)

    def first(s, carry):
        x = jnp.concatenate([top_ref[s], own_ref[s], bot_ref[s]], axis=0).astype(F32)
        x = jnp.concatenate([x, jnp.zeros((rows + 4, WIDE - width, 128), F32)], axis=1)
        x1, x2, x3 = up(x, 2), up(x, 4), up(x, 6)
        xs = jnp.concatenate([x, x1, x2], axis=-1).astype(BF)
        xo_s[s] = jnp.concatenate([v[1 : 1 + inner, :cols] for v in (x1, x2, x3)], axis=-1).astype(BF)
        acc = dot(xs[0:inner].reshape(inner * WIDE, 384), w1_ref[0])
        acc += dot(xs[1 : 1 + inner].reshape(inner * WIDE, 384), w1_ref[1])
        acc += dot(xs[2 : 2 + inner].reshape(inner * WIDE, 384), w1_ref[2])
        pre = acc[:, :channels].reshape(shape)
        pre_s[s] = pre
        dh_s[s] = acc[:, channels:].reshape(shape)
        act = (pre * sigmoid(pre)).astype(BF).astype(F32)
        act_s[s] = act
        sum_s[...] += act
        return carry

    lax.fori_loop(0, srcs, first, 0)
    average = pair_sum(sum_s[...]) * (1.0 / members)
    sum_s[...] = average
    var_s[...] = jnp.zeros(shape, F32)

    def second(s, carry):
        d = act_s[s] - sum_s[...]
        var_s[...] += d * d
        return carry

    lax.fori_loop(0, srcs, second, 0)
    spread = jnp.sqrt(pair_sum(var_s[...]) * (1.0 / members) + 0.1)
    var_s[...] = spread
    stats = jnp.concatenate([sum_s[...], spread], axis=-1).reshape(inner * WIDE, 2 * channels)
    s1, s2, s3 = split3(stats)
    pool = pool_ref[...]
    shared_s[...] = (dot(s1, pool) + dot(s2, pool) + dot(s3, pool)).reshape(shape)
    ca_s[...] = jnp.zeros(shape, F32)

    def third(s, carry):
        zed = act_s[s] + shared_s[...]
        sig = sigmoid(zed)
        hid = jnp.where(inside, (zed * sig).astype(BF).astype(F32), 0.0)
        dz = (dh_s[s] * (sig * (1.0 + zed * (1.0 - sig)))).astype(BF).astype(F32)
        dh_s[s] = dz
        ca_s[...] += dz
        hq_s[s] = jnp.concatenate([up(hid, 2 * q)[:, :cols] for q in range(3)], axis=-1).astype(BF)
        return carry

    lax.fori_loop(0, srcs, third, 0)
    d_shared = pair_sum(ca_s[...])
    d1, d2, d3 = split3(d_shared.reshape(inner * WIDE, channels))
    last = ((1,), (1,))
    d_stats = dot_t(d1, pool, last) + dot_t(d2, pool, last) + dot_t(d3, pool, last)
    ca_s[...] = (d_stats[:, :channels] * (1.0 / members)).reshape(shape)
    cs_s[...] = d_stats[:, channels:].reshape(shape) / (members * var_s[...])
    r_id = lax.broadcasted_iota(jnp.int32, shape, 0)
    c_id = lax.broadcasted_iota(jnp.int32, shape, 1)
    mine = (r_id >= 1) & (r_id <= rows) & (c_id >= 2) & (c_id < 2 + cols) & (parity == 0)
    e1, e2, e3 = split3(jnp.where(mine, d_shared, 0.0).reshape(inner * WIDE, channels))
    g_pool = dot_rows(s1, e1) + dot_rows(s1, e2) + dot_rows(s2, e1) + dot_rows(s2, e2) + dot_rows(s1, e3) + dot_rows(s3, e1)

    def fourth(s, carry):
        pre = pre_s[s]
        sig = sigmoid(pre)
        d_act = dh_s[s] + ca_s[...] + cs_s[...] * (act_s[s] - sum_s[...])
        dp = jnp.where(inside, d_act * (sig * (1.0 + pre * (1.0 - sig))), 0.0).astype(BF).astype(F32)
        dq = jnp.concatenate([up(dp, 2 * q)[:, :cols] for q in range(3)], axis=-1).astype(BF)
        dpo_s[s] = dq[1 : 1 + rows, :, channels : 2 * channels]
        hq = hq_s[s]
        both = jnp.concatenate([hq, dq], axis=-1)
        acc = dot(both[0:rows].reshape(rows * cols, 6 * channels), w2_ref[0])
        acc += dot(both[1 : 1 + rows].reshape(rows * cols, 6 * channels), w2_ref[1])
        acc += dot(both[2 : 2 + rows].reshape(rows * cols, 6 * channels), w2_ref[2])
        own = xo_s[s, 1 : 1 + rows, :, 128:256].astype(F32)
        out_ref[s] = (own + acc.reshape(rows, cols, 128)).astype(BF)
        return carry

    lax.fori_loop(0, srcs, fourth, 0)
    for s, piece in enumerate((o0, o1, o2, o3, o4, o5, o6, o7)):
        piece[...] = out_ref[s]

    total = srcs * rows * cols
    dpo = dpo_s[...].reshape(total, channels)
    own = xo_s[:, 1 : 1 + rows, :, 128:256].reshape(total, 128)
    half = channels // 2
    count, per, _ = grads_ref.shape
    pitch = chunk_s.shape[0] // count

    def put(start, value):
        for off, step, where in row_blocks(start, value.shape[0], count, pitch):
            chunk_s[where, :] = value[off : off + step]

    for p in range(3):
        g_in = dot_rows(dpo, xo_s[:, p : p + rows].reshape(total, 384))
        g_out = dot_rows(own, hq_s[:, p : p + rows].reshape(total, 384))
        for q in range(3):
            t = 3 * p + q
            put(t * half, g_in[:, q * 128 : (q + 1) * 128].T[:half])
            put((9 + t) * half, g_out[half:, q * 128 : (q + 1) * 128])
    used = 18 * half + 2 * channels
    put(18 * half, g_pool)
    if used < count * per:
        put(used, jnp.zeros((count * per - used, 128), F32))
    grads_ref[...] = chunk_s[...].reshape(count, pitch, 128)[:, :per].astype(BF)


def sum_kernel(parts_ref, out_ref):
    total = jnp.sum(parts_ref[...].astype(F32), axis=0)
    out_ref[...] = jnp.broadcast_to(total[None], out_ref.shape).astype(BF)


def finish_kernel(scale, full_ref, in_ref, out_ref, pool_ref, chunk_s):
    count, per, _ = full_ref.shape
    pitch = chunk_s.shape[0] // count
    pad = jnp.zeros((count, pitch - per, 128), F32)
    full = full_ref[...].astype(F32) * scale
    chunk_s[...] = (jnp.concatenate([full, pad], axis=1) if pitch > per else full).reshape(count * pitch, 128)
    start = 0
    for ref in (in_ref, out_ref, pool_ref):
        size = ref.shape[0]
        for off, step, where in row_blocks(start, size, count, pitch):
            ref[off : off + step] = chunk_s[where, :]
        start += size


def on_device(ensemble, cotangent, conv_in, pool_weight, conv_out):
    mem_local, var_count, rows, lon = ensemble.shape
    groups = lax.axis_size("member")
    bands = lax.axis_size("lat")
    channels = conv_in.shape[-1]
    cols = lon // groups
    width = (cols + 4) * mem_local
    vspec = pl.BlockSpec(memory_space=pltpu.VMEM)
    sspec = pl.BlockSpec(memory_space=pltpu.SMEM)
    vm = pltpu.VMEM
    me = lax.axis_index("member").astype(jnp.int32).reshape(1)
    tiles = pl.pallas_call(
        pack_kernel,
        out_shape=[jax.ShapeDtypeStruct((rows, width, 128), BF)] * groups,
        in_specs=[sspec, vspec, vspec],
        out_specs=[vspec] * groups,
        scratch_shapes=[vm((rows, 2 * lon + 8, 128), F32)],
        name="pack",
    )(me, ensemble, cotangent)
    tiles = [tiles[0]] + [swap(tiles[s], SLOTS[s], groups, 1) for s in range(1, groups)]
    tops, bots = [], []
    for group in (tiles[:SPLIT], tiles[SPLIT:]):
        n = len(group)
        after = tops[:1]
        head, tail = pl.pallas_call(
            functools.partial(edges_kernel, n),
            out_shape=[jax.ShapeDtypeStruct((n, 2, width, 128), BF)] * 2,
            in_specs=[pl.BlockSpec(memory_space=pl.ANY)] * (n + len(after)),
            out_specs=[pl.BlockSpec(memory_space=pl.ANY)] * 2,
            scratch_shapes=[pltpu.SemaphoreType.DMA((2 * n,))],
            name="edges",
        )(*group, *after)
        tops.append(tail)
        bots.append(head)
    tops = [lax.ppermute(tail, "lat", [(i, i + 1) for i in range(bands - 1)]) for tail in tops]
    bots = [lax.ppermute(head, "lat", [(i + 1, i) for i in range(bands - 1)]) for head in bots]

    flip_in = jnp.transpose(conv_in[::-1, ::-1], (0, 1, 3, 2))
    flip_out = jnp.transpose(conv_out[::-1, ::-1], (0, 1, 3, 2))
    z1 = jnp.zeros_like(conv_in)
    z2 = jnp.zeros_like(conv_out)
    w1 = jnp.concatenate(
        [jnp.concatenate([conv_in, z1], axis=3), jnp.concatenate([z1, flip_out], axis=3)], axis=2
    ).reshape(3, 384, 256)
    w2 = jnp.concatenate(
        [
            jnp.concatenate([conv_out, z2], axis=3).reshape(3, 384, 128),
            jnp.concatenate([z2, flip_in], axis=3).reshape(3, 384, 128),
        ],
        axis=1,
    )
    lat = jnp.stack([lax.axis_index("lat"), jnp.int32(bands * rows)]).astype(jnp.int32)
    inner = rows + 2
    plane = (inner, WIDE, channels)
    count = groups * bands
    used = 18 * (channels // 2) + 2 * channels
    per = -(-used // count)
    pitch = -(-per // 8) * 8
    grads_shape = jax.ShapeDtypeStruct((count, per, channels), BF)
    *pieces, grads = pl.pallas_call(
        tile_kernel,
        out_shape=[jax.ShapeDtypeStruct((rows, cols * mem_local, 128), BF)] * groups
        + [grads_shape],
        in_specs=[sspec] + [vspec] * (groups + 7),
        out_specs=[vspec] * (groups + 1),
        scratch_shapes=[
            vm((groups, rows, width, 128), BF),
            vm((groups, 2, width, 128), BF),
            vm((groups, 2, width, 128), BF),
            vm((groups, rows, cols * mem_local, 128), BF),
            vm((groups,) + plane, F32),
            vm((groups,) + plane, F32),
            vm((groups,) + plane, F32),
            vm((groups, inner, cols * mem_local, 384), BF),
            vm((groups, inner, cols * mem_local, 384), BF),
            vm((groups, rows, cols * mem_local, channels), BF),
            vm(plane, F32),
            vm(plane, F32),
            vm(plane, F32),
            vm(plane, F32),
            vm(plane, F32),
            vm((count * pitch, channels), F32),
        ],
        compiler_params=pltpu.CompilerParams(vmem_limit_bytes=56 * 1024 * 1024),
        name="tile",
    )(lat, *tiles, *tops, *bots, w1, w2, pool_weight)

    pieces = [pieces[0]] + [swap(pieces[s], SLOTS[s], groups, -1) for s in range(1, groups)]
    parts = lax.all_to_all(grads, BOTH, split_axis=0, concat_axis=0, tiled=True)
    parts, *pieces = lax.optimization_barrier((parts, *pieces))
    shared = pl.pallas_call(
        sum_kernel,
        out_shape=grads_shape,
        in_specs=[vspec],
        out_specs=vspec,
        name="total",
    )(parts)
    full = lax.all_to_all(shared, BOTH, split_axis=0, concat_axis=0, tiled=True)
    members = mem_local * groups
    scale = 1.0 / math.sqrt(members * bands * rows * lon)
    half = channels // 2
    grad_in, grad_out, grad_pool = pl.pallas_call(
        functools.partial(finish_kernel, scale),
        out_shape=[jax.ShapeDtypeStruct((n, channels), F32) for n in (9 * half, 9 * half, 2 * channels)],
        in_specs=[vspec],
        out_specs=[vspec] * 3,
        scratch_shapes=[vm((count * pitch, channels), F32)],
        name="finish",
    )(full)
    grad_in = grad_in.reshape(3, 3, half, channels)
    grad_out = grad_out.reshape(3, 3, half, channels).transpose(0, 1, 3, 2)

    encoded, d_input = pl.pallas_call(
        unpack_kernel,
        out_shape=[jax.ShapeDtypeStruct(ensemble.shape, BF)] * 2,
        in_specs=[sspec] + [vspec] * groups,
        out_specs=[vspec] * 2,
        scratch_shapes=[vm((rows, 2 * lon, 128), F32)],
        name="unpack",
    )(me, *pieces)
    return encoded, d_input, grad_in, grad_pool, grad_out


def solution(mesh):
    return jax.shard_map(
        on_device,
        mesh=mesh,
        in_specs=(P("member", None, "lat", None), P("member", None, "lat", None), P(), P(), P()),
        out_specs=(P("member", None, "lat", None), P("member", None, "lat", None), P(), P(), P()),
        check_vma=False,
    )
```

```python
import functools
import math

import jax
import jax.numpy as jnp
from jax import lax
from jax.experimental import pallas as pl
from jax.experimental.pallas import tpu as pltpu
from jax.sharding import PartitionSpec as P

BF = jnp.bfloat16
F32 = jnp.float32
BOTH = ("member", "lat")
WIDE = 80


SLOTS = ((0, 0), (0, 1), (1, 0), (3, 0), (2, 0), (2, 1), (1, 1), (3, 1))
SPLIT = 4


def peer(device, slot, groups, sign=1):
    step, core = slot
    chips = groups // 2
    return 2 * ((device // 2 + chips + sign * step) % chips) + (device % 2 + core) % 2


def swap(value, slot, groups, sign):
    pairs = [(i, peer(i, slot, groups, sign)) for i in range(groups)]
    return lax.ppermute(value, "member", pairs)


def row_blocks(start, rows, count, pitch):
    step = math.gcd(rows, count, start)
    for off in range(0, rows, step):
        block, chunk = divmod(start + off, count)
        yield off, step, pl.ds(chunk * pitch + block, step, stride=pitch)


def sigmoid(v):
    return 1.0 / (1.0 + jnp.exp(-v))


def split3(v):
    a = v.astype(BF)
    r = v - a.astype(F32)
    b = r.astype(BF)
    c = (r - b.astype(F32)).astype(BF)
    return a, b, c


def dot(a, b):
    return jnp.dot(a, b, preferred_element_type=F32)


def dot_t(a, b, dims):
    return lax.dot_general(a, b, (dims, ((), ())), preferred_element_type=F32)


def dot_rows(a, b):
    return dot_t(a, b, ((0,), (0,)))


def pack_kernel(me_ref, ens_ref, cot_ref, *refs):
    outs, plane = refs[:-1], refs[-1]
    groups = len(outs)
    mem_local, _, rows, lon = ens_ref.shape
    width = outs[0].shape[1]
    for m in range(mem_local):
        for r in range(rows):
            both = jnp.concatenate([ens_ref[m, :, r, :], cot_ref[m, :, r, :]], axis=0).astype(F32).T
            plane[r, pl.ds(4 + m, lon, stride=2), :] = both
            plane[r, pl.ds(m, 2, stride=2), :] = both[lon - 2 :]
            plane[r, pl.ds(4 + 2 * lon + m, 2, stride=2), :] = both[:2]
    for s in range(groups):
        k = peer(me_ref[0], SLOTS[s], groups)
        for r in range(rows):
            outs[s][r] = plane[r, pl.ds(pl.multiple_of(k * (width - 8), 8), width), :].astype(BF)


def edges_kernel(*refs):
    tiles, (head_ref, tail_ref) = refs[:-2], refs[-2:]
    for s, tile in enumerate(tiles):
        head_ref[s] = tile[:2]
        tail_ref[s] = tile[tile.shape[0] - 2 :]


def unpack_kernel(me_ref, *refs):
    tiles, (enc_ref, din_ref, plane) = refs[:-3], refs[-3:]
    groups = len(tiles)
    mem_local, half, rows, lon = enc_ref.shape
    width = tiles[0].shape[1]
    for s in range(groups):
        k = peer(me_ref[0], SLOTS[s], groups)
        for r in range(rows):
            plane[r, pl.ds(pl.multiple_of(k * width, 8), width), :] = tiles[s][r].astype(F32)
    for m in range(mem_local):
        for r in range(rows):
            both = plane[r, pl.ds(m, lon, stride=2), :].T.astype(BF)
            enc_ref[m, :, r, :] = both[:half]
            din_ref[m, :, r, :] = both[half:]


def tile_kernel(
    lat_ref, t0, t1, t2, t3, t4, t5, t6, t7, top_ref, bot_ref, w1_ref, w2_ref, pool_ref,
    o0, o1, o2, o3, o4, o5, o6, o7, grads_ref,
    own_ref, out_ref, pre_s, dh_s, act_s, xo_s, hq_s, dpo_s, sum_s, var_s, shared_s, ca_s, cs_s, chunk_s,
):
    srcs, rows, width, _ = own_ref.shape
    inner = rows + 2
    cols = xo_s.shape[2]
    nlat = lat_ref[1]
    for s, tile in enumerate((t0, t1, t2, t3, t4, t5, t6, t7)):
        own_ref[s] = tile[...]
    members = 2 * srcs
    channels = pre_s.shape[-1]
    shape = (inner, WIDE, channels)

    def up(v, n):
        return pltpu.roll(v, WIDE - n, 1) if n else v

    parity = lax.broadcasted_iota(jnp.int32, shape, 1) % 2

    def pair_sum(v):
        return v + jnp.where(parity == 0, up(v, 1), pltpu.roll(v, 1, 1))

    row_id = lax.broadcasted_iota(jnp.int32, shape, 0) + lat_ref[0] * rows - 1
    inside = jnp.logical_and(row_id >= 0, row_id < nlat)

    sum_s[...] = jnp.zeros(shape, F32)

    def first(s, carry):
        x = jnp.concatenate([top_ref[s], own_ref[s], bot_ref[s]], axis=0).astype(F32)
        x = jnp.concatenate([x, jnp.zeros((rows + 4, WIDE - width, 128), F32)], axis=1)
        x1, x2, x3 = up(x, 2), up(x, 4), up(x, 6)
        xs = jnp.concatenate([x, x1, x2], axis=-1).astype(BF)
        xo_s[s] = jnp.concatenate([v[1 : 1 + inner, :cols] for v in (x1, x2, x3)], axis=-1).astype(BF)
        acc = dot(xs[0:inner].reshape(inner * WIDE, 384), w1_ref[0])
        acc += dot(xs[1 : 1 + inner].reshape(inner * WIDE, 384), w1_ref[1])
        acc += dot(xs[2 : 2 + inner].reshape(inner * WIDE, 384), w1_ref[2])
        pre = acc[:, :channels].reshape(shape)
        pre_s[s] = pre
        dh_s[s] = acc[:, channels:].reshape(shape)
        act = (pre * sigmoid(pre)).astype(BF).astype(F32)
        act_s[s] = act
        sum_s[...] += act
        return carry

    lax.fori_loop(0, srcs, first, 0)
    average = pair_sum(sum_s[...]) * (1.0 / members)
    sum_s[...] = average
    var_s[...] = jnp.zeros(shape, F32)

    def second(s, carry):
        d = act_s[s] - sum_s[...]
        var_s[...] += d * d
        return carry

    lax.fori_loop(0, srcs, second, 0)
    spread = jnp.sqrt(pair_sum(var_s[...]) * (1.0 / members) + 0.1)
    var_s[...] = spread
    stats = jnp.concatenate([sum_s[...], spread], axis=-1).reshape(inner * WIDE, 2 * channels)
    s1, s2, s3 = split3(stats)
    pool = pool_ref[...]
    shared_s[...] = (dot(s1, pool) + dot(s2, pool) + dot(s3, pool)).reshape(shape)
    ca_s[...] = jnp.zeros(shape, F32)

    def third(s, carry):
        zed = act_s[s] + shared_s[...]
        sig = sigmoid(zed)
        hid = jnp.where(inside, (zed * sig).astype(BF).astype(F32), 0.0)
        dz = (dh_s[s] * (sig * (1.0 + zed * (1.0 - sig)))).astype(BF).astype(F32)
        dh_s[s] = dz
        ca_s[...] += dz
        hq_s[s] = jnp.concatenate([up(hid, 2 * q)[:, :cols] for q in range(3)], axis=-1).astype(BF)
        return carry

    lax.fori_loop(0, srcs, third, 0)
    d_shared = pair_sum(ca_s[...])
    d1, d2, d3 = split3(d_shared.reshape(inner * WIDE, channels))
    last = ((1,), (1,))
    d_stats = dot_t(d1, pool, last) + dot_t(d2, pool, last) + dot_t(d3, pool, last)
    ca_s[...] = (d_stats[:, :channels] * (1.0 / members)).reshape(shape)
    cs_s[...] = d_stats[:, channels:].reshape(shape) / (members * var_s[...])
    r_id = lax.broadcasted_iota(jnp.int32, shape, 0)
    c_id = lax.broadcasted_iota(jnp.int32, shape, 1)
    mine = (r_id >= 1) & (r_id <= rows) & (c_id >= 2) & (c_id < 2 + cols) & (parity == 0)
    e1, e2, e3 = split3(jnp.where(mine, d_shared, 0.0).reshape(inner * WIDE, channels))
    g_pool = dot_rows(s1, e1) + dot_rows(s1, e2) + dot_rows(s2, e1) + dot_rows(s2, e2) + dot_rows(s1, e3) + dot_rows(s3, e1)

    def fourth(s, carry):
        pre = pre_s[s]
        sig = sigmoid(pre)
        d_act = dh_s[s] + ca_s[...] + cs_s[...] * (act_s[s] - sum_s[...])
        dp = jnp.where(inside, d_act * (sig * (1.0 + pre * (1.0 - sig))), 0.0).astype(BF).astype(F32)
        dq = jnp.concatenate([up(dp, 2 * q)[:, :cols] for q in range(3)], axis=-1).astype(BF)
        dpo_s[s] = dq[1 : 1 + rows, :, channels : 2 * channels]
        hq = hq_s[s]
        both = jnp.concatenate([hq, dq], axis=-1)
        acc = dot(both[0:rows].reshape(rows * cols, 6 * channels), w2_ref[0])
        acc += dot(both[1 : 1 + rows].reshape(rows * cols, 6 * channels), w2_ref[1])
        acc += dot(both[2 : 2 + rows].reshape(rows * cols, 6 * channels), w2_ref[2])
        own = xo_s[s, 1 : 1 + rows, :, 128:256].astype(F32)
        out_ref[s] = (own + acc.reshape(rows, cols, 128)).astype(BF)
        return carry

    lax.fori_loop(0, srcs, fourth, 0)
    for s, piece in enumerate((o0, o1, o2, o3, o4, o5, o6, o7)):
        piece[...] = out_ref[s]

    total = srcs * rows * cols
    dpo = dpo_s[...].reshape(total, channels)
    own = xo_s[:, 1 : 1 + rows, :, 128:256].reshape(total, 128)
    half = channels // 2
    count, per, _ = grads_ref.shape
    pitch = chunk_s.shape[0] // count

    def put(start, value):
        for off, step, where in row_blocks(start, value.shape[0], count, pitch):
            chunk_s[where, :] = value[off : off + step]

    for p in range(3):
        g_in = dot_rows(dpo, xo_s[:, p : p + rows].reshape(total, 384))
        g_out = dot_rows(own, hq_s[:, p : p + rows].reshape(total, 384))
        for q in range(3):
            t = 3 * p + q
            put(t * half, g_in[:, q * 128 : (q + 1) * 128].T[:half])
            put((9 + t) * half, g_out[half:, q * 128 : (q + 1) * 128])
    used = 18 * half + 2 * channels
    put(18 * half, g_pool)
    if used < count * per:
        put(used, jnp.zeros((count * per - used, 128), F32))
    grads_ref[...] = chunk_s[...].reshape(count, pitch, 128)[:, :per].astype(BF)


def sum_kernel(parts_ref, out_ref):
    total = jnp.sum(parts_ref[...].astype(F32), axis=0)
    out_ref[...] = jnp.broadcast_to(total[None], out_ref.shape).astype(BF)


def finish_kernel(scale, full_ref, in_ref, out_ref, pool_ref, chunk_s):
    count, per, _ = full_ref.shape
    pitch = chunk_s.shape[0] // count
    pad = jnp.zeros((count, pitch - per, 128), F32)
    full = full_ref[...].astype(F32) * scale
    chunk_s[...] = (jnp.concatenate([full, pad], axis=1) if pitch > per else full).reshape(count * pitch, 128)
    start = 0
    for ref in (in_ref, out_ref, pool_ref):
        size = ref.shape[0]
        for off, step, where in row_blocks(start, size, count, pitch):
            ref[off : off + step] = chunk_s[where, :]
        start += size


def on_device(ensemble, cotangent, conv_in, pool_weight, conv_out):
    mem_local, var_count, rows, lon = ensemble.shape
    groups = lax.axis_size("member")
    bands = lax.axis_size("lat")
    channels = conv_in.shape[-1]
    cols = lon // groups
    width = (cols + 4) * mem_local
    vspec = pl.BlockSpec(memory_space=pltpu.VMEM)
    sspec = pl.BlockSpec(memory_space=pltpu.SMEM)
    vm = pltpu.VMEM
    me = lax.axis_index("member").astype(jnp.int32).reshape(1)
    tiles = pl.pallas_call(
        pack_kernel,
        out_shape=[jax.ShapeDtypeStruct((rows, width, 128), BF)] * groups,
        in_specs=[sspec, vspec, vspec],
        out_specs=[vspec] * groups,
        scratch_shapes=[vm((rows, 2 * lon + 8, 128), F32)],
        name="pack",
    )(me, ensemble, cotangent)
    tiles = [tiles[0]] + [swap(tiles[s], SLOTS[s], groups, 1) for s in range(1, groups)]
    head, tail = pl.pallas_call(
        edges_kernel,
        out_shape=[jax.ShapeDtypeStruct((groups, 2, width, 128), BF)] * 2,
        in_specs=[vspec] * groups,
        out_specs=[vspec] * 2,
        name="edges",
    )(*tiles)
    top = lax.ppermute(tail, "lat", [(i, i + 1) for i in range(bands - 1)])
    bot = lax.ppermute(head, "lat", [(i + 1, i) for i in range(bands - 1)])

    flip_in = jnp.transpose(conv_in[::-1, ::-1], (0, 1, 3, 2))
    flip_out = jnp.transpose(conv_out[::-1, ::-1], (0, 1, 3, 2))
    z1 = jnp.zeros_like(conv_in)
    z2 = jnp.zeros_like(conv_out)
    w1 = jnp.concatenate(
        [jnp.concatenate([conv_in, z1], axis=3), jnp.concatenate([z1, flip_out], axis=3)], axis=2
    ).reshape(3, 384, 256)
    w2 = jnp.concatenate(
        [
            jnp.concatenate([conv_out, z2], axis=3).reshape(3, 384, 128),
            jnp.concatenate([z2, flip_in], axis=3).reshape(3, 384, 128),
        ],
        axis=1,
    )
    lat = jnp.stack([lax.axis_index("lat"), jnp.int32(bands * rows)]).astype(jnp.int32)
    inner = rows + 2
    plane = (inner, WIDE, channels)
    count = groups * bands
    used = 18 * (channels // 2) + 2 * channels
    per = -(-used // (8 * count)) * 8
    pitch = -(-per // 8) * 8
    grads_shape = jax.ShapeDtypeStruct((count, per, channels), BF)
    *pieces, grads = pl.pallas_call(
        tile_kernel,
        out_shape=[jax.ShapeDtypeStruct((rows, cols * mem_local, 128), BF)] * groups
        + [grads_shape],
        in_specs=[sspec] + [vspec] * (groups + 5),
        out_specs=[vspec] * (groups + 1),
        scratch_shapes=[
            vm((groups, rows, width, 128), BF),
            vm((groups, rows, cols * mem_local, 128), BF),
            vm((groups,) + plane, F32),
            vm((groups,) + plane, F32),
            vm((groups,) + plane, F32),
            vm((groups, inner, cols * mem_local, 384), BF),
            vm((groups, inner, cols * mem_local, 384), BF),
            vm((groups, rows, cols * mem_local, channels), BF),
            vm(plane, F32),
            vm(plane, F32),
            vm(plane, F32),
            vm(plane, F32),
            vm(plane, F32),
            vm((count * pitch, channels), F32),
        ],
        compiler_params=pltpu.CompilerParams(vmem_limit_bytes=56 * 1024 * 1024),
        name="tile",
    )(lat, *tiles, top, bot, w1, w2, pool_weight)

    early = [pieces[0]] + [swap(pieces[s], SLOTS[s], groups, -1) for s in range(1, SPLIT)]
    parts = lax.all_to_all(grads, BOTH, split_axis=0, concat_axis=0, tiled=True)
    parts, early, late = lax.optimization_barrier((parts, early, pieces[SPLIT:]))
    shared = pl.pallas_call(
        sum_kernel,
        out_shape=grads_shape,
        in_specs=[vspec],
        out_specs=vspec,
        name="total",
    )(parts)
    late = [swap(piece, SLOTS[s], groups, -1) for s, piece in enumerate(late, SPLIT)]
    full = lax.all_to_all(shared, BOTH, split_axis=0, concat_axis=0, tiled=True)
    members = mem_local * groups
    scale = 1.0 / math.sqrt(members * bands * rows * lon)
    half = channels // 2
    grad_in, grad_out, grad_pool = pl.pallas_call(
        functools.partial(finish_kernel, scale),
        out_shape=[jax.ShapeDtypeStruct((n, channels), F32) for n in (9 * half, 9 * half, 2 * channels)],
        in_specs=[vspec],
        out_specs=[vspec] * 3,
        scratch_shapes=[vm((count * pitch, channels), F32)],
        name="finish",
    )(full)
    grad_in = grad_in.reshape(3, 3, half, channels)
    grad_out = grad_out.reshape(3, 3, half, channels).transpose(0, 1, 3, 2)

    encoded, d_input = pl.pallas_call(
        unpack_kernel,
        out_shape=[jax.ShapeDtypeStruct(ensemble.shape, BF)] * 2,
        in_specs=[sspec] + [vspec] * groups,
        out_specs=[vspec] * 2,
        scratch_shapes=[vm((rows, 2 * lon, 128), F32)],
        name="unpack",
    )(me, *early, *late)
    return encoded, d_input, grad_in, grad_pool, grad_out


def solution(mesh):
    return jax.shard_map(
        on_device,
        mesh=mesh,
        in_specs=(P("member", None, "lat", None), P("member", None, "lat", None), P(), P(), P()),
        out_specs=(P("member", None, "lat", None), P("member", None, "lat", None), P(), P(), P()),
        check_vma=False,
    )
```

```python
import functools
import math

import jax
import jax.numpy as jnp
from jax import lax
from jax.experimental import pallas as pl
from jax.experimental.pallas import tpu as pltpu
from jax.sharding import PartitionSpec as P

BF = jnp.bfloat16
F32 = jnp.float32
WIDE = 80


SLOTS = ((0, 0), (0, 1), (1, 0), (3, 0), (2, 0), (2, 1), (1, 1), (3, 1))


def peer(device, slot, groups, sign=1):
    step, core = slot
    chips = groups // 2
    return 2 * ((device // 2 + chips + sign * step) % chips) + (device % 2 + core) % 2


def swap(value, slot, groups, sign):
    pairs = [(i, peer(i, slot, groups, sign)) for i in range(groups)]
    return lax.ppermute(value, "member", pairs)


def sigmoid(v):
    return 1.0 / (1.0 + jnp.exp(-v))


def split3(v):
    a = v.astype(BF)
    r = v - a.astype(F32)
    b = r.astype(BF)
    c = (r - b.astype(F32)).astype(BF)
    return a, b, c


def dot(a, b):
    return jnp.dot(a, b, preferred_element_type=F32)


def dot_t(a, b, dims):
    return lax.dot_general(a, b, (dims, ((), ())), preferred_element_type=F32)


def dot_rows(a, b):
    return dot_t(a, b, ((0,), (0,)))


def pack_kernel(me_ref, ens_ref, cot_ref, *refs):
    outs, plane = refs[:-1], refs[-1]
    groups = len(outs)
    mem_local, _, rows, lon = ens_ref.shape
    width = outs[0].shape[1]
    for m in range(mem_local):
        for r in range(rows):
            both = jnp.concatenate([ens_ref[m, :, r, :], cot_ref[m, :, r, :]], axis=0).astype(F32).T
            plane[r, pl.ds(4 + m, lon, stride=2), :] = both
            plane[r, pl.ds(m, 2, stride=2), :] = both[lon - 2 :]
            plane[r, pl.ds(4 + 2 * lon + m, 2, stride=2), :] = both[:2]
    for s in range(groups):
        k = peer(me_ref[0], SLOTS[s], groups)
        for r in range(rows):
            outs[s][r] = plane[r, pl.ds(pl.multiple_of(k * (width - 8), 8), width), :].astype(BF)


def edges_kernel(*refs):
    tiles, (head_ref, tail_ref) = refs[:-2], refs[-2:]
    for s, tile in enumerate(tiles):
        head_ref[s] = tile[:2]
        tail_ref[s] = tile[tile.shape[0] - 2 :]


def unpack_kernel(me_ref, *refs):
    tiles, (enc_ref, din_ref, plane) = refs[:-3], refs[-3:]
    groups = len(tiles)
    mem_local, half, rows, lon = enc_ref.shape
    width = tiles[0].shape[1]
    for s in range(groups):
        k = peer(me_ref[0], SLOTS[s], groups)
        for r in range(rows):
            plane[r, pl.ds(pl.multiple_of(k * width, 8), width), :] = tiles[s][r].astype(F32)
    for m in range(mem_local):
        for r in range(rows):
            both = plane[r, pl.ds(m, lon, stride=2), :].T.astype(BF)
            enc_ref[m, :, r, :] = both[:half]
            din_ref[m, :, r, :] = both[half:]


def tile_kernel(
    lat_ref, t0, t1, t2, t3, t4, t5, t6, t7, top_ref, bot_ref, w1_ref, w2_ref, pool_ref,
    o0, o1, o2, o3, o4, o5, o6, o7, grads_ref,
    own_ref, out_ref, pre_s, dh_s, act_s, xo_s, hq_s, dpo_s, sum_s, var_s, shared_s, ca_s, cs_s,
):
    srcs, rows, width, _ = own_ref.shape
    inner = rows + 2
    cols = xo_s.shape[2]
    nlat = lat_ref[1]
    for s, tile in enumerate((t0, t1, t2, t3, t4, t5, t6, t7)):
        own_ref[s] = tile[...]
    members = 2 * srcs
    channels = pre_s.shape[-1]
    shape = (inner, WIDE, channels)

    def up(v, n):
        return pltpu.roll(v, WIDE - n, 1) if n else v

    parity = lax.broadcasted_iota(jnp.int32, shape, 1) % 2

    def pair_sum(v):
        return v + jnp.where(parity == 0, up(v, 1), pltpu.roll(v, 1, 1))

    row_id = lax.broadcasted_iota(jnp.int32, shape, 0) + lat_ref[0] * rows - 1
    inside = jnp.logical_and(row_id >= 0, row_id < nlat)

    sum_s[...] = jnp.zeros(shape, F32)

    def first(s, carry):
        x = jnp.concatenate([top_ref[s], own_ref[s], bot_ref[s]], axis=0).astype(F32)
        x = jnp.concatenate([x, jnp.zeros((rows + 4, WIDE - width, 128), F32)], axis=1)
        x1, x2, x3 = up(x, 2), up(x, 4), up(x, 6)
        xs = jnp.concatenate([x, x1, x2], axis=-1).astype(BF)
        xo_s[s] = jnp.concatenate([v[1 : 1 + inner, :cols] for v in (x1, x2, x3)], axis=-1).astype(BF)
        acc = dot(xs[0:inner].reshape(inner * WIDE, 384), w1_ref[0])
        acc += dot(xs[1 : 1 + inner].reshape(inner * WIDE, 384), w1_ref[1])
        acc += dot(xs[2 : 2 + inner].reshape(inner * WIDE, 384), w1_ref[2])
        pre = acc[:, :channels].reshape(shape)
        pre_s[s] = pre
        dh_s[s] = acc[:, channels:].reshape(shape)
        act = (pre * sigmoid(pre)).astype(BF).astype(F32)
        act_s[s] = act
        sum_s[...] += act
        return carry

    lax.fori_loop(0, srcs, first, 0)
    average = pair_sum(sum_s[...]) * (1.0 / members)
    sum_s[...] = average
    var_s[...] = jnp.zeros(shape, F32)

    def second(s, carry):
        d = act_s[s] - sum_s[...]
        var_s[...] += d * d
        return carry

    lax.fori_loop(0, srcs, second, 0)
    spread = jnp.sqrt(pair_sum(var_s[...]) * (1.0 / members) + 0.1)
    var_s[...] = spread
    stats = jnp.concatenate([sum_s[...], spread], axis=-1).reshape(inner * WIDE, 2 * channels)
    s1, s2, s3 = split3(stats)
    pool = pool_ref[...]
    shared_s[...] = (dot(s1, pool) + dot(s2, pool) + dot(s3, pool)).reshape(shape)
    ca_s[...] = jnp.zeros(shape, F32)

    def third(s, carry):
        zed = act_s[s] + shared_s[...]
        sig = sigmoid(zed)
        hid = jnp.where(inside, (zed * sig).astype(BF).astype(F32), 0.0)
        dz = (dh_s[s] * (sig * (1.0 + zed * (1.0 - sig)))).astype(BF).astype(F32)
        dh_s[s] = dz
        ca_s[...] += dz
        hq_s[s] = jnp.concatenate([up(hid, 2 * q)[:, :cols] for q in range(3)], axis=-1).astype(BF)
        return carry

    lax.fori_loop(0, srcs, third, 0)
    d_shared = pair_sum(ca_s[...])
    d1, d2, d3 = split3(d_shared.reshape(inner * WIDE, channels))
    last = ((1,), (1,))
    d_stats = dot_t(d1, pool, last) + dot_t(d2, pool, last) + dot_t(d3, pool, last)
    ca_s[...] = (d_stats[:, :channels] * (1.0 / members)).reshape(shape)
    cs_s[...] = d_stats[:, channels:].reshape(shape) / (members * var_s[...])
    r_id = lax.broadcasted_iota(jnp.int32, shape, 0)
    c_id = lax.broadcasted_iota(jnp.int32, shape, 1)
    mine = (r_id >= 1) & (r_id <= rows) & (c_id >= 2) & (c_id < 2 + cols) & (parity == 0)
    e1, e2, e3 = split3(jnp.where(mine, d_shared, 0.0).reshape(inner * WIDE, channels))
    g_pool = dot_rows(s1, e1) + dot_rows(s1, e2) + dot_rows(s2, e1) + dot_rows(s2, e2) + dot_rows(s1, e3) + dot_rows(s3, e1)

    def fourth(s, carry):
        pre = pre_s[s]
        sig = sigmoid(pre)
        d_act = dh_s[s] + ca_s[...] + cs_s[...] * (act_s[s] - sum_s[...])
        dp = jnp.where(inside, d_act * (sig * (1.0 + pre * (1.0 - sig))), 0.0).astype(BF).astype(F32)
        dq = jnp.concatenate([up(dp, 2 * q)[:, :cols] for q in range(3)], axis=-1).astype(BF)
        dpo_s[s] = dq[1 : 1 + rows, :, channels : 2 * channels]
        hq = hq_s[s]
        both = jnp.concatenate([hq, dq], axis=-1)
        acc = dot(both[0:rows].reshape(rows * cols, 6 * channels), w2_ref[0])
        acc += dot(both[1 : 1 + rows].reshape(rows * cols, 6 * channels), w2_ref[1])
        acc += dot(both[2 : 2 + rows].reshape(rows * cols, 6 * channels), w2_ref[2])
        own = xo_s[s, 1 : 1 + rows, :, 128:256].astype(F32)
        out_ref[s] = (own + acc.reshape(rows, cols, 128)).astype(BF)
        return carry

    lax.fori_loop(0, srcs, fourth, 0)
    for s, piece in enumerate((o0, o1, o2, o3, o4, o5, o6, o7)):
        piece[...] = out_ref[s]

    total = srcs * rows * cols
    dpo = dpo_s[...].reshape(total, channels)
    own = xo_s[:, 1 : 1 + rows, :, 128:256].reshape(total, 128)
    half = channels // 2
    for p in range(3):
        g_in = dot_rows(dpo, xo_s[:, p : p + rows].reshape(total, 384))
        g_out = dot_rows(own, hq_s[:, p : p + rows].reshape(total, 384))
        for q in range(3):
            t = 3 * p + q
            grads_ref[t * half : (t + 1) * half, :] = g_in[:, q * 128 : (q + 1) * 128].T[:half].astype(BF)
            grads_ref[(9 + t) * half : (10 + t) * half, :] = g_out[half:, q * 128 : (q + 1) * 128].astype(BF)
    used = 18 * half + 2 * channels
    grads_ref[18 * half : used, :] = g_pool.astype(BF)
    if used < grads_ref.shape[0]:
        grads_ref[used:, :] = jnp.zeros((grads_ref.shape[0] - used, 128), BF)


def sum_kernel(parts_ref, out_ref):
    total = jnp.sum(parts_ref[...].astype(F32), axis=0)
    out_ref[...] = jnp.broadcast_to(total[None], out_ref.shape).astype(out_ref.dtype)


def finish_kernel(scale, full_ref, in_ref, out_ref, pool_ref):
    start = 0
    for ref in (in_ref, out_ref, pool_ref):
        size = ref.shape[0]
        ref[...] = full_ref[start : start + size].astype(F32) * scale
        start += size


def on_device(ensemble, cotangent, conv_in, pool_weight, conv_out):
    mem_local, var_count, rows, lon = ensemble.shape
    groups = lax.axis_size("member")
    bands = lax.axis_size("lat")
    channels = conv_in.shape[-1]
    cols = lon // groups
    width = (cols + 4) * mem_local
    vspec = pl.BlockSpec(memory_space=pltpu.VMEM)
    sspec = pl.BlockSpec(memory_space=pltpu.SMEM)
    vm = pltpu.VMEM
    me = lax.axis_index("member").astype(jnp.int32).reshape(1)
    tiles = pl.pallas_call(
        pack_kernel,
        out_shape=[jax.ShapeDtypeStruct((rows, width, 128), BF)] * groups,
        in_specs=[sspec, vspec, vspec],
        out_specs=[vspec] * groups,
        scratch_shapes=[vm((rows, 2 * lon + 8, 128), F32)],
        name="pack",
    )(me, ensemble, cotangent)
    tiles = [tiles[0]] + [swap(tiles[s], SLOTS[s], groups, 1) for s in range(1, groups)]
    head, tail = pl.pallas_call(
        edges_kernel,
        out_shape=[jax.ShapeDtypeStruct((groups, 2, width, 128), BF)] * 2,
        in_specs=[vspec] * groups,
        out_specs=[vspec] * 2,
        name="edges",
    )(*tiles)
    top = lax.ppermute(tail, "lat", [(i, i + 1) for i in range(bands - 1)])
    bot = lax.ppermute(head, "lat", [(i + 1, i) for i in range(bands - 1)])

    flip_in = jnp.transpose(conv_in[::-1, ::-1], (0, 1, 3, 2))
    flip_out = jnp.transpose(conv_out[::-1, ::-1], (0, 1, 3, 2))
    z1 = jnp.zeros_like(conv_in)
    z2 = jnp.zeros_like(conv_out)
    w1 = jnp.concatenate(
        [jnp.concatenate([conv_in, z1], axis=3), jnp.concatenate([z1, flip_out], axis=3)], axis=2
    ).reshape(3, 384, 256)
    w2 = jnp.concatenate(
        [
            jnp.concatenate([conv_out, z2], axis=3).reshape(3, 384, 128),
            jnp.concatenate([z2, flip_in], axis=3).reshape(3, 384, 128),
        ],
        axis=1,
    )
    lat = jnp.stack([lax.axis_index("lat"), jnp.int32(bands * rows)]).astype(jnp.int32)
    inner = rows + 2
    plane = (inner, WIDE, channels)
    used = 18 * (channels // 2) + 2 * channels
    per = -(-used // (8 * bands)) * 8
    *pieces, grads = pl.pallas_call(
        tile_kernel,
        out_shape=[jax.ShapeDtypeStruct((rows, cols * mem_local, 128), BF)] * groups
        + [jax.ShapeDtypeStruct((bands * per, channels), BF)],
        in_specs=[sspec] + [vspec] * (groups + 5),
        out_specs=[vspec] * (groups + 1),
        scratch_shapes=[
            vm((groups, rows, width, 128), BF),
            vm((groups, rows, cols * mem_local, 128), BF),
            vm((groups,) + plane, F32),
            vm((groups,) + plane, F32),
            vm((groups,) + plane, F32),
            vm((groups, inner, cols * mem_local, 384), BF),
            vm((groups, inner, cols * mem_local, 384), BF),
            vm((groups, rows, cols * mem_local, channels), BF),
            vm(plane, F32),
            vm(plane, F32),
            vm(plane, F32),
            vm(plane, F32),
            vm(plane, F32),
        ],
        compiler_params=pltpu.CompilerParams(vmem_limit_bytes=56 * 1024 * 1024),
        name="tile",
    )(lat, *tiles, top, bot, w1, w2, pool_weight)

    def exchange(value, axis):
        return lax.all_to_all(value, axis, split_axis=0, concat_axis=0, tiled=True)

    def add_up(parts, copies, dtype):
        return pl.pallas_call(
            sum_kernel,
            out_shape=jax.ShapeDtypeStruct((copies,) + parts.shape[1:], dtype),
            in_specs=[vspec],
            out_specs=vspec,
            name="total",
        )(parts)

    pieces = [pieces[0]] + [swap(pieces[s], SLOTS[s], groups, -1) for s in range(1, groups)]
    parts = exchange(grads.reshape(bands, per, channels), "lat")
    parts, pieces = lax.optimization_barrier((parts, pieces))
    parts = exchange(add_up(parts, groups, F32), "member")
    full = exchange(add_up(parts, bands, BF), "lat").reshape(bands * per, channels)
    members = mem_local * groups
    scale = 1.0 / math.sqrt(members * bands * rows * lon)
    half = channels // 2
    grad_in, grad_out, grad_pool = pl.pallas_call(
        functools.partial(finish_kernel, scale),
        out_shape=[jax.ShapeDtypeStruct((n, channels), F32) for n in (9 * half, 9 * half, 2 * channels)],
        in_specs=[vspec],
        out_specs=[vspec] * 3,
        name="finish",
    )(full)
    grad_in = grad_in.reshape(3, 3, half, channels)
    grad_out = grad_out.reshape(3, 3, half, channels).transpose(0, 1, 3, 2)

    encoded, d_input = pl.pallas_call(
        unpack_kernel,
        out_shape=[jax.ShapeDtypeStruct(ensemble.shape, BF)] * 2,
        in_specs=[sspec] + [vspec] * groups,
        out_specs=[vspec] * 2,
        scratch_shapes=[vm((rows, 2 * lon, 128), F32)],
        name="unpack",
    )(me, *pieces)
    return encoded, d_input, grad_in, grad_pool, grad_out


def solution(mesh):
    return jax.shard_map(
        on_device,
        mesh=mesh,
        in_specs=(P("member", None, "lat", None), P("member", None, "lat", None), P(), P(), P()),
        out_specs=(P("member", None, "lat", None), P("member", None, "lat", None), P(), P(), P()),
        check_vma=False,
    )
```

```python
import functools
import math

import jax
import jax.numpy as jnp
from jax import lax
from jax.experimental import pallas as pl
from jax.experimental.pallas import tpu as pltpu
from jax.sharding import PartitionSpec as P

BF = jnp.bfloat16
F32 = jnp.float32
WIDE = 80


SLOTS = ((0, 0), (0, 1), (1, 0), (3, 0), (2, 0), (2, 1), (1, 1), (3, 1))
EARLY = 5


def peer(device, slot, groups, sign=1):
    step, core = slot
    chips = groups // 2
    return 2 * ((device // 2 + chips + sign * step) % chips) + (device % 2 + core) % 2


def swap(value, slot, groups, sign):
    pairs = [(i, peer(i, slot, groups, sign)) for i in range(groups)]
    return lax.ppermute(value, "member", pairs)


def near(*values):
    return [pltpu.with_memory_space_constraint(v, pltpu.VMEM) for v in values]


def sigmoid(v):
    return 1.0 / (1.0 + jnp.exp(-v))


def split3(v):
    a = v.astype(BF)
    r = v - a.astype(F32)
    b = r.astype(BF)
    c = (r - b.astype(F32)).astype(BF)
    return a, b, c


def dot(a, b):
    return jnp.dot(a, b, preferred_element_type=F32)


def dot_t(a, b, dims):
    return lax.dot_general(a, b, (dims, ((), ())), preferred_element_type=F32)


def dot_rows(a, b):
    return dot_t(a, b, ((0,), (0,)))


def pack_kernel(me_ref, ens_ref, cot_ref, *refs):
    outs, plane = refs[:-1], refs[-1]
    groups = len(outs)
    mem_local, _, rows, lon = ens_ref.shape
    width = outs[0].shape[1]
    for m in range(mem_local):
        for r in range(rows):
            both = jnp.concatenate([ens_ref[m, :, r, :], cot_ref[m, :, r, :]], axis=0).astype(F32).T
            plane[r, pl.ds(4 + m, lon, stride=2), :] = both
            plane[r, pl.ds(m, 2, stride=2), :] = both[lon - 2 :]
            plane[r, pl.ds(4 + 2 * lon + m, 2, stride=2), :] = both[:2]
    for s in range(groups):
        k = peer(me_ref[0], SLOTS[s], groups)
        for r in range(rows):
            outs[s][r] = plane[r, pl.ds(pl.multiple_of(k * (width - 8), 8), width), :].astype(BF)


def edges_kernel(*refs):
    tiles, (head_ref, tail_ref) = refs[:-2], refs[-2:]
    for s, tile in enumerate(tiles):
        head_ref[s] = tile[:2]
        tail_ref[s] = tile[tile.shape[0] - 2 :]


def unpack_kernel(me_ref, *refs):
    tiles, (enc_ref, din_ref, plane) = refs[:-3], refs[-3:]
    groups = len(tiles)
    mem_local, half, rows, lon = enc_ref.shape
    width = tiles[0].shape[1]
    for s in range(groups):
        k = peer(me_ref[0], SLOTS[s], groups)
        for r in range(rows):
            plane[r, pl.ds(pl.multiple_of(k * width, 8), width), :] = tiles[s][r].astype(F32)
    for m in range(mem_local):
        for r in range(rows):
            both = plane[r, pl.ds(m, lon, stride=2), :].T.astype(BF)
            enc_ref[m, :, r, :] = both[:half]
            din_ref[m, :, r, :] = both[half:]


def tile_kernel(
    lat_ref, t0, t1, t2, t3, t4, t5, t6, t7, top_ref, bot_ref, w1_ref, w2_ref, pool_ref,
    o0, o1, o2, o3, o4, o5, o6, o7, grads_ref,
    own_ref, out_ref, pre_s, dh_s, act_s, xo_s, hq_s, dpo_s, sum_s, var_s, shared_s, ca_s, cs_s,
):
    srcs, rows, width, _ = own_ref.shape
    inner = rows + 2
    cols = xo_s.shape[2]
    nlat = lat_ref[1]
    for s, tile in enumerate((t0, t1, t2, t3, t4, t5, t6, t7)):
        own_ref[s] = tile[...]
    members = 2 * srcs
    channels = pre_s.shape[-1]
    shape = (inner, WIDE, channels)

    def up(v, n):
        return pltpu.roll(v, WIDE - n, 1) if n else v

    parity = lax.broadcasted_iota(jnp.int32, shape, 1) % 2

    def pair_sum(v):
        return v + jnp.where(parity == 0, up(v, 1), pltpu.roll(v, 1, 1))

    row_id = lax.broadcasted_iota(jnp.int32, shape, 0) + lat_ref[0] * rows - 1
    inside = jnp.logical_and(row_id >= 0, row_id < nlat)

    sum_s[...] = jnp.zeros(shape, F32)

    def first(s, carry):
        x = jnp.concatenate([top_ref[s], own_ref[s], bot_ref[s]], axis=0).astype(F32)
        x = jnp.concatenate([x, jnp.zeros((rows + 4, WIDE - width, 128), F32)], axis=1)
        x1, x2, x3 = up(x, 2), up(x, 4), up(x, 6)
        xs = jnp.concatenate([x, x1, x2], axis=-1).astype(BF)
        xo_s[s] = jnp.concatenate([v[1 : 1 + inner, :cols] for v in (x1, x2, x3)], axis=-1).astype(BF)
        acc = dot(xs[0:inner].reshape(inner * WIDE, 384), w1_ref[0])
        acc += dot(xs[1 : 1 + inner].reshape(inner * WIDE, 384), w1_ref[1])
        acc += dot(xs[2 : 2 + inner].reshape(inner * WIDE, 384), w1_ref[2])
        pre = acc[:, :channels].reshape(shape)
        pre_s[s] = pre
        dh_s[s] = acc[:, channels:].reshape(shape)
        act = (pre * sigmoid(pre)).astype(BF).astype(F32)
        act_s[s] = act
        sum_s[...] += act
        return carry

    lax.fori_loop(0, srcs, first, 0)
    average = pair_sum(sum_s[...]) * (1.0 / members)
    sum_s[...] = average
    var_s[...] = jnp.zeros(shape, F32)

    def second(s, carry):
        d = act_s[s] - sum_s[...]
        var_s[...] += d * d
        return carry

    lax.fori_loop(0, srcs, second, 0)
    spread = jnp.sqrt(pair_sum(var_s[...]) * (1.0 / members) + 0.1)
    var_s[...] = spread
    stats = jnp.concatenate([sum_s[...], spread], axis=-1).reshape(inner * WIDE, 2 * channels)
    s1, s2, s3 = split3(stats)
    pool = pool_ref[...]
    shared_s[...] = (dot(s1, pool) + dot(s2, pool) + dot(s3, pool)).reshape(shape)
    ca_s[...] = jnp.zeros(shape, F32)

    def third(s, carry):
        zed = act_s[s] + shared_s[...]
        sig = sigmoid(zed)
        hid = jnp.where(inside, (zed * sig).astype(BF).astype(F32), 0.0)
        dz = (dh_s[s] * (sig * (1.0 + zed * (1.0 - sig)))).astype(BF).astype(F32)
        dh_s[s] = dz
        ca_s[...] += dz
        hq_s[s] = jnp.concatenate([up(hid, 2 * q)[:, :cols] for q in range(3)], axis=-1).astype(BF)
        return carry

    lax.fori_loop(0, srcs, third, 0)
    d_shared = pair_sum(ca_s[...])
    d1, d2, d3 = split3(d_shared.reshape(inner * WIDE, channels))
    last = ((1,), (1,))
    d_stats = dot_t(d1, pool, last) + dot_t(d2, pool, last) + dot_t(d3, pool, last)
    ca_s[...] = (d_stats[:, :channels] * (1.0 / members)).reshape(shape)
    cs_s[...] = d_stats[:, channels:].reshape(shape) / (members * var_s[...])
    r_id = lax.broadcasted_iota(jnp.int32, shape, 0)
    c_id = lax.broadcasted_iota(jnp.int32, shape, 1)
    mine = (r_id >= 1) & (r_id <= rows) & (c_id >= 2) & (c_id < 2 + cols) & (parity == 0)
    e1, e2, e3 = split3(jnp.where(mine, d_shared, 0.0).reshape(inner * WIDE, channels))
    g_pool = dot_rows(s1, e1) + dot_rows(s1, e2) + dot_rows(s2, e1) + dot_rows(s2, e2) + dot_rows(s1, e3) + dot_rows(s3, e1)

    def fourth(s, carry):
        pre = pre_s[s]
        sig = sigmoid(pre)
        d_act = dh_s[s] + ca_s[...] + cs_s[...] * (act_s[s] - sum_s[...])
        dp = jnp.where(inside, d_act * (sig * (1.0 + pre * (1.0 - sig))), 0.0).astype(BF).astype(F32)
        dq = jnp.concatenate([up(dp, 2 * q)[:, :cols] for q in range(3)], axis=-1).astype(BF)
        dpo_s[s] = dq[1 : 1 + rows, :, channels : 2 * channels]
        hq = hq_s[s]
        both = jnp.concatenate([hq, dq], axis=-1)
        acc = dot(both[0:rows].reshape(rows * cols, 6 * channels), w2_ref[0])
        acc += dot(both[1 : 1 + rows].reshape(rows * cols, 6 * channels), w2_ref[1])
        acc += dot(both[2 : 2 + rows].reshape(rows * cols, 6 * channels), w2_ref[2])
        own = xo_s[s, 1 : 1 + rows, :, 128:256].astype(F32)
        out_ref[s] = (own + acc.reshape(rows, cols, 128)).astype(BF)
        return carry

    lax.fori_loop(0, srcs, fourth, 0)
    for s, piece in enumerate((o0, o1, o2, o3, o4, o5, o6, o7)):
        piece[...] = out_ref[s]

    total = srcs * rows * cols
    dpo = dpo_s[...].reshape(total, channels)
    own = xo_s[:, 1 : 1 + rows, :, 128:256].reshape(total, 128)
    half = channels // 2
    for p in range(3):
        g_in = dot_rows(dpo, xo_s[:, p : p + rows].reshape(total, 384))
        g_out = dot_rows(own, hq_s[:, p : p + rows].reshape(total, 384))
        for q in range(3):
            t = 3 * p + q
            grads_ref[t * half : (t + 1) * half, :] = g_in[:, q * 128 : (q + 1) * 128].T[:half].astype(BF)
            grads_ref[(9 + t) * half : (10 + t) * half, :] = g_out[half:, q * 128 : (q + 1) * 128].astype(BF)
    used = 18 * half + 2 * channels
    grads_ref[18 * half : used, :] = g_pool.astype(BF)
    if used < grads_ref.shape[0]:
        grads_ref[used:, :] = jnp.zeros((grads_ref.shape[0] - used, 128), BF)


def sum_kernel(parts_ref, out_ref):
    total = jnp.sum(parts_ref[...].astype(F32), axis=0)
    out_ref[...] = jnp.broadcast_to(total[None], out_ref.shape).astype(out_ref.dtype)


def finish_kernel(scale, full_ref, in_ref, out_ref, pool_ref):
    start = 0
    for ref in (in_ref, out_ref, pool_ref):
        size = ref.shape[0]
        ref[...] = full_ref[start : start + size].astype(F32) * scale
        start += size


def on_device(ensemble, cotangent, conv_in, pool_weight, conv_out):
    mem_local, var_count, rows, lon = ensemble.shape
    groups = lax.axis_size("member")
    bands = lax.axis_size("lat")
    channels = conv_in.shape[-1]
    cols = lon // groups
    width = (cols + 4) * mem_local
    vspec = pl.BlockSpec(memory_space=pltpu.VMEM)
    sspec = pl.BlockSpec(memory_space=pltpu.SMEM)
    vm = pltpu.VMEM
    me = lax.axis_index("member").astype(jnp.int32).reshape(1)
    tiles = pl.pallas_call(
        pack_kernel,
        out_shape=[vm((rows, width, 128), BF)] * groups,
        in_specs=[sspec, vspec, vspec],
        out_specs=[vspec] * groups,
        scratch_shapes=[vm((rows, 2 * lon + 8, 128), F32)],
        name="pack",
    )(me, ensemble, cotangent)
    tiles = [tiles[0]] + [swap(tiles[s], SLOTS[s], groups, 1) for s in range(1, groups)]
    head, tail = pl.pallas_call(
        edges_kernel,
        out_shape=[vm((groups, 2, width, 128), BF)] * 2,
        in_specs=[vspec] * groups,
        out_specs=[vspec] * 2,
        name="edges",
    )(*near(*tiles))
    top = lax.ppermute(tail, "lat", [(i, i + 1) for i in range(bands - 1)])
    bot = lax.ppermute(head, "lat", [(i + 1, i) for i in range(bands - 1)])

    flip_in = jnp.transpose(conv_in[::-1, ::-1], (0, 1, 3, 2))
    flip_out = jnp.transpose(conv_out[::-1, ::-1], (0, 1, 3, 2))
    z1 = jnp.zeros_like(conv_in)
    z2 = jnp.zeros_like(conv_out)
    w1 = jnp.concatenate(
        [jnp.concatenate([conv_in, z1], axis=3), jnp.concatenate([z1, flip_out], axis=3)], axis=2
    ).reshape(3, 384, 256)
    w2 = jnp.concatenate(
        [
            jnp.concatenate([conv_out, z2], axis=3).reshape(3, 384, 128),
            jnp.concatenate([z2, flip_in], axis=3).reshape(3, 384, 128),
        ],
        axis=1,
    )
    lat = jnp.stack([lax.axis_index("lat"), jnp.int32(bands * rows)]).astype(jnp.int32)
    inner = rows + 2
    plane = (inner, WIDE, channels)
    used = 18 * (channels // 2) + 2 * channels
    per = -(-used // (8 * bands)) * 8
    *pieces, grads = pl.pallas_call(
        tile_kernel,
        out_shape=[vm((rows, cols * mem_local, 128), BF)] * groups
        + [vm((bands * per, channels), BF)],
        in_specs=[sspec] + [vspec] * (groups + 5),
        out_specs=[vspec] * (groups + 1),
        scratch_shapes=[
            vm((groups, rows, width, 128), BF),
            vm((groups, rows, cols * mem_local, 128), BF),
            vm((groups,) + plane, F32),
            vm((groups,) + plane, F32),
            vm((groups,) + plane, F32),
            vm((groups, inner, cols * mem_local, 384), BF),
            vm((groups, inner, cols * mem_local, 384), BF),
            vm((groups, rows, cols * mem_local, channels), BF),
            vm(plane, F32),
            vm(plane, F32),
            vm(plane, F32),
            vm(plane, F32),
            vm(plane, F32),
        ],
        compiler_params=pltpu.CompilerParams(vmem_limit_bytes=56 * 1024 * 1024),
        name="tile",
    )(lat, *near(*tiles, top, bot, w1, w2, pool_weight))

    def exchange(value, axis):
        return lax.all_to_all(value, axis, split_axis=0, concat_axis=0, tiled=True)

    def add_up(parts, copies, dtype):
        return pl.pallas_call(
            sum_kernel,
            out_shape=vm((copies,) + parts.shape[1:], dtype),
            in_specs=[vspec],
            out_specs=vspec,
            name="total",
        )(*near(parts))

    early = [pieces[0]] + [swap(pieces[s], SLOTS[s], groups, -1) for s in range(1, EARLY)]
    parts = exchange(grads.reshape(bands, per, channels), "lat")
    parts, early, late = lax.optimization_barrier((parts, early, pieces[EARLY:]))
    late = [swap(piece, SLOTS[s], groups, -1) for s, piece in enumerate(late, EARLY)]
    parts = exchange(add_up(parts, groups, F32), "member")
    parts, late = lax.optimization_barrier((parts, late))
    full = exchange(add_up(parts, bands, BF), "lat").reshape(bands * per, channels)
    members = mem_local * groups
    scale = 1.0 / math.sqrt(members * bands * rows * lon)
    half = channels // 2
    grad_in, grad_out, grad_pool = pl.pallas_call(
        functools.partial(finish_kernel, scale),
        out_shape=[jax.ShapeDtypeStruct((n, channels), F32) for n in (9 * half, 9 * half, 2 * channels)],
        in_specs=[vspec],
        out_specs=[vspec] * 3,
        name="finish",
    )(*near(full))
    grad_in = grad_in.reshape(3, 3, half, channels)
    grad_out = grad_out.reshape(3, 3, half, channels).transpose(0, 1, 3, 2)

    encoded, d_input = pl.pallas_call(
        unpack_kernel,
        out_shape=[jax.ShapeDtypeStruct(ensemble.shape, BF)] * 2,
        in_specs=[sspec] + [vspec] * groups,
        out_specs=[vspec] * 2,
        scratch_shapes=[vm((rows, 2 * lon, 128), F32)],
        name="unpack",
    )(me, *near(*early, *late))
    return encoded, d_input, grad_in, grad_pool, grad_out


def solution(mesh):
    return jax.shard_map(
        on_device,
        mesh=mesh,
        in_specs=(P("member", None, "lat", None), P("member", None, "lat", None), P(), P(), P()),
        out_specs=(P("member", None, "lat", None), P("member", None, "lat", None), P(), P(), P()),
        check_vma=False,
    )
```

```python
import functools
import math

import jax
import jax.numpy as jnp
from jax import lax
from jax.experimental import pallas as pl
from jax.experimental.pallas import tpu as pltpu
from jax.sharding import PartitionSpec as P

BF = jnp.bfloat16
F32 = jnp.float32
WIDE = 80


def swap(value, steps, cross, groups):
    chips = groups // 2
    pairs = [
        (2 * z + c, 2 * ((z + steps) % chips) + (c + cross) % 2) for z in range(chips) for c in range(2)
    ]
    return lax.ppermute(value, "member", pairs)


def column_block(device, steps, cross, groups):
    chips = groups // 2
    return 2 * lax.rem(device // 2 + steps, chips) + lax.rem(device + cross, 2)


def near(*values):
    return [pltpu.with_memory_space_constraint(v, pltpu.VMEM) for v in values]


def sigmoid(v):
    return 1.0 / (1.0 + jnp.exp(-v))


def split3(v):
    a = v.astype(BF)
    r = v - a.astype(F32)
    b = r.astype(BF)
    c = (r - b.astype(F32)).astype(BF)
    return a, b, c


def dot(a, b):
    return jnp.dot(a, b, preferred_element_type=F32)


def dot_t(a, b, dims):
    return lax.dot_general(a, b, (dims, ((), ())), preferred_element_type=F32)


def dot_rows(a, b):
    return dot_t(a, b, ((0,), (0,)))


def pack_kernel(me_ref, ens_ref, cot_ref, keep_ref, give_ref, plane):
    chips, _, width, _ = keep_ref.shape
    mem_local, _, rows, lon = ens_ref.shape
    for m in range(mem_local):
        for r in range(rows):
            both = jnp.concatenate([ens_ref[m, :, r, :], cot_ref[m, :, r, :]], axis=0).astype(F32).T
            plane[r, pl.ds(4 + m, lon, stride=2), :] = both
            plane[r, pl.ds(m, 2, stride=2), :] = both[lon - 2 :]
            plane[r, pl.ds(4 + 2 * lon + m, 2, stride=2), :] = both[:2]
    for d in range(chips):
        for cross, ref in enumerate((keep_ref, give_ref)):
            k = column_block(me_ref[0], d, cross, 2 * chips)
            for r in range(rows):
                ref[d, r] = plane[r, pl.ds(pl.multiple_of(k * (width - 8), 8), width), :].astype(BF)


def pair_kernel(keep_ref, got_ref, *out_refs):
    for d, ref in enumerate(out_refs):
        ref[0] = keep_ref[d]
        ref[1] = got_ref[d]


def edges_kernel(*refs):
    tiles, (head_ref, tail_ref) = refs[:-2], refs[-2:]
    rows = tiles[0].shape[1]
    for d, tile in enumerate(tiles):
        head_ref[2 * d : 2 * d + 2] = tile[:, :2]
        tail_ref[2 * d : 2 * d + 2] = tile[:, rows - 2 :]


def other_kernel(*refs):
    for d, tile in enumerate(refs[:-1]):
        refs[-1][d] = tile[1]


def unpack_kernel(me_ref, *refs):
    tiles, (theirs_ref, enc_ref, din_ref, plane) = refs[:-4], refs[-4:]
    chips = len(tiles)
    mem_local, half, rows, lon = enc_ref.shape
    width = theirs_ref.shape[2]
    for d in range(chips):
        for cross in range(2):
            k = column_block(me_ref[0], d, cross, 2 * chips)
            for r in range(rows):
                piece = theirs_ref[d, r] if cross else tiles[d][0, r]
                plane[r, pl.ds(pl.multiple_of(k * width, 8), width), :] = piece.astype(F32)
    for m in range(mem_local):
        for r in range(rows):
            both = plane[r, pl.ds(m, lon, stride=2), :].T.astype(BF)
            enc_ref[m, :, r, :] = both[:half]
            din_ref[m, :, r, :] = both[half:]


def tile_kernel(
    lat_ref, t0, t1, t2, t3, top_ref, bot_ref, w1_ref, pool_ref,
    grads_ref, hid_ref, dpre_ref,
    own_ref, pre_s, dh_s, act_s, xo_s, hq_s, dpo_s, hid_s, dpre_s, sum_s, var_s, shared_s, ca_s, cs_s, sems,
):
    srcs, rows, width, _ = own_ref.shape
    inner = rows + 2
    cols = xo_s.shape[2]
    nlat = lat_ref[1]
    for d, tile in enumerate((t0, t1, t2, t3)):
        own_ref[2 * d : 2 * d + 2] = tile[...]
    members = 2 * srcs
    channels = pre_s.shape[-1]
    shape = (inner, WIDE, channels)

    def up(v, n):
        return pltpu.roll(v, WIDE - n, 1) if n else v

    parity = lax.broadcasted_iota(jnp.int32, shape, 1) % 2

    def pair_sum(v):
        return v + jnp.where(parity == 0, up(v, 1), pltpu.roll(v, 1, 1))

    row_id = lax.broadcasted_iota(jnp.int32, shape, 0) + lat_ref[0] * rows - 1
    inside = jnp.logical_and(row_id >= 0, row_id < nlat)

    sum_s[...] = jnp.zeros(shape, F32)

    def first(s, carry):
        x = jnp.concatenate([top_ref[s], own_ref[s], bot_ref[s]], axis=0).astype(F32)
        x = jnp.concatenate([x, jnp.zeros((rows + 4, WIDE - width, 128), F32)], axis=1)
        x1, x2, x3 = up(x, 2), up(x, 4), up(x, 6)
        xs = jnp.concatenate([x, x1, x2], axis=-1).astype(BF)
        xo_s[s] = jnp.concatenate([v[1 : 1 + inner, :cols] for v in (x1, x2, x3)], axis=-1).astype(BF)
        acc = dot(xs[0:inner].reshape(inner * WIDE, 384), w1_ref[0])
        acc += dot(xs[1 : 1 + inner].reshape(inner * WIDE, 384), w1_ref[1])
        acc += dot(xs[2 : 2 + inner].reshape(inner * WIDE, 384), w1_ref[2])
        pre = acc[:, :channels].reshape(shape)
        pre_s[s] = pre
        dh_s[s] = acc[:, channels:].reshape(shape)
        act = (pre * sigmoid(pre)).astype(BF).astype(F32)
        act_s[s] = act
        sum_s[...] += act
        return carry

    lax.fori_loop(0, srcs, first, 0)
    average = pair_sum(sum_s[...]) * (1.0 / members)
    sum_s[...] = average
    var_s[...] = jnp.zeros(shape, F32)

    def second(s, carry):
        d = act_s[s] - sum_s[...]
        var_s[...] += d * d
        return carry

    lax.fori_loop(0, srcs, second, 0)
    spread = jnp.sqrt(pair_sum(var_s[...]) * (1.0 / members) + 0.1)
    var_s[...] = spread
    stats = jnp.concatenate([sum_s[...], spread], axis=-1).reshape(inner * WIDE, 2 * channels)
    s1, s2, s3 = split3(stats)
    pool = pool_ref[...]
    shared_s[...] = (dot(s1, pool) + dot(s2, pool) + dot(s3, pool)).reshape(shape)
    ca_s[...] = jnp.zeros(shape, F32)

    def third(s, carry):
        zed = act_s[s] + shared_s[...]
        sig = sigmoid(zed)
        hid = jnp.where(inside, (zed * sig).astype(BF).astype(F32), 0.0)
        dz = (dh_s[s] * (sig * (1.0 + zed * (1.0 - sig)))).astype(BF).astype(F32)
        dh_s[s] = dz
        ca_s[...] += dz
        hid_s[s] = hid[:, :width].astype(BF)
        hq_s[s] = jnp.concatenate([up(hid, 2 * q)[:, :cols] for q in range(3)], axis=-1).astype(BF)
        return carry

    lax.fori_loop(0, srcs, third, 0)
    hid_copy = pltpu.make_async_copy(hid_s, hid_ref, sems.at[0])
    hid_copy.start()
    d_shared = pair_sum(ca_s[...])
    d1, d2, d3 = split3(d_shared.reshape(inner * WIDE, channels))
    last = ((1,), (1,))
    d_stats = dot_t(d1, pool, last) + dot_t(d2, pool, last) + dot_t(d3, pool, last)
    ca_s[...] = (d_stats[:, :channels] * (1.0 / members)).reshape(shape)
    cs_s[...] = d_stats[:, channels:].reshape(shape) / (members * var_s[...])
    r_id = lax.broadcasted_iota(jnp.int32, shape, 0)
    c_id = lax.broadcasted_iota(jnp.int32, shape, 1)
    mine = (r_id >= 1) & (r_id <= rows) & (c_id >= 2) & (c_id < 2 + cols) & (parity == 0)
    e1, e2, e3 = split3(jnp.where(mine, d_shared, 0.0).reshape(inner * WIDE, channels))
    g_pool = dot_rows(s1, e1) + dot_rows(s1, e2) + dot_rows(s2, e1) + dot_rows(s2, e2) + dot_rows(s1, e3) + dot_rows(s3, e1)

    def fourth(s, carry):
        pre = pre_s[s]
        sig = sigmoid(pre)
        d_act = dh_s[s] + ca_s[...] + cs_s[...] * (act_s[s] - sum_s[...])
        dp = jnp.where(inside, d_act * (sig * (1.0 + pre * (1.0 - sig))), 0.0).astype(BF).astype(F32)
        dpre_s[s] = dp[:, :width].astype(BF)
        dpo_s[s] = up(dp, 2)[1 : 1 + rows, :cols].astype(BF)
        return carry

    lax.fori_loop(0, srcs, fourth, 0)
    dpre_copy = pltpu.make_async_copy(dpre_s, dpre_ref, sems.at[1])
    dpre_copy.start()

    total = srcs * rows * cols
    dpo = dpo_s[...].reshape(total, channels)
    own = xo_s[:, 1 : 1 + rows, :, 128:256].reshape(total, 128)
    half = channels // 2
    for p in range(3):
        g_in = dot_rows(dpo, xo_s[:, p : p + rows].reshape(total, 384))
        g_out = dot_rows(own, hq_s[:, p : p + rows].reshape(total, 384))
        for q in range(3):
            t = 3 * p + q
            grads_ref[t * half : (t + 1) * half, :] = g_in[:, q * 128 : (q + 1) * 128].T[:half].astype(BF)
            grads_ref[(9 + t) * half : (10 + t) * half, :] = g_out[half:, q * 128 : (q + 1) * 128].astype(BF)
    used = 18 * half + 2 * channels
    grads_ref[18 * half : used, :] = g_pool.astype(BF)
    if used < grads_ref.shape[0]:
        grads_ref[used:, :] = jnp.zeros((grads_ref.shape[0] - used, 128), BF)
    hid_copy.wait()
    dpre_copy.wait()


def output_kernel(t0, t1, t2, t3, hid_ref, dpre_ref, w2_ref, *out_refs):
    _, inner, width, _ = hid_ref.shape
    rows = inner - 2
    cols = out_refs[0].shape[2]

    def shifts(ref, s):
        v = ref[s].astype(F32)
        return [(pltpu.roll(v, width - 2 * q, 1) if q else v)[:, :cols] for q in range(3)]

    for d, (tile, out_ref) in enumerate(zip((t0, t1, t2, t3), out_refs)):

        def piece(j, carry):
            both = jnp.concatenate(shifts(hid_ref, 2 * d + j) + shifts(dpre_ref, 2 * d + j), axis=-1).astype(BF)
            depth = both.shape[-1]
            acc = dot(both[0:rows].reshape(rows * cols, depth), w2_ref[0])
            acc += dot(both[1 : 1 + rows].reshape(rows * cols, depth), w2_ref[1])
            acc += dot(both[2 : 2 + rows].reshape(rows * cols, depth), w2_ref[2])
            own = pltpu.roll(tile[j].astype(F32), width - 4, 1)[:, :cols]
            out_ref[j] = (own + acc.reshape(rows, cols, 128)).astype(BF)
            return carry

        lax.fori_loop(0, 2, piece, 0)


def sum_kernel(parts_ref, out_ref):
    total = jnp.sum(parts_ref[...].astype(F32), axis=0)
    out_ref[...] = jnp.broadcast_to(total[None], out_ref.shape).astype(out_ref.dtype)


def finish_kernel(scale, full_ref, in_ref, out_ref, pool_ref):
    start = 0
    for ref in (in_ref, out_ref, pool_ref):
        size = ref.shape[0]
        ref[...] = full_ref[start : start + size].astype(F32) * scale
        start += size


def on_device(ensemble, cotangent, conv_in, pool_weight, conv_out):
    mem_local, var_count, rows, lon = ensemble.shape
    groups = lax.axis_size("member")
    bands = lax.axis_size("lat")
    channels = conv_in.shape[-1]
    cols = lon // groups
    width = (cols + 4) * mem_local
    vspec = pl.BlockSpec(memory_space=pltpu.VMEM)
    sspec = pl.BlockSpec(memory_space=pltpu.SMEM)
    vm = pltpu.VMEM
    me = lax.axis_index("member").astype(jnp.int32).reshape(1)
    chips = groups // 2
    keep, give = pl.pallas_call(
        pack_kernel,
        out_shape=[vm((chips, rows, width, 128), BF)] * 2,
        in_specs=[sspec, vspec, vspec],
        out_specs=[vspec] * 2,
        scratch_shapes=[vm((rows, 2 * lon + 8, 128), F32)],
        name="pack",
    )(me, ensemble, cotangent)
    got = swap(give, 0, 1, groups)
    tiles = pl.pallas_call(
        pair_kernel,
        out_shape=[vm((2, rows, width, 128), BF)] * chips,
        in_specs=[vspec] * 2,
        out_specs=[vspec] * chips,
        name="pair",
    )(*near(keep, got))
    tiles = [tiles[0]] + [swap(tiles[d], d, 0, groups) for d in range(1, chips)]
    head, tail = pl.pallas_call(
        edges_kernel,
        out_shape=[vm((groups, 2, width, 128), BF)] * 2,
        in_specs=[vspec] * chips,
        out_specs=[vspec] * 2,
        name="edges",
    )(*near(*tiles))
    top = lax.ppermute(tail, "lat", [(i, i + 1) for i in range(bands - 1)])
    bot = lax.ppermute(head, "lat", [(i + 1, i) for i in range(bands - 1)])

    flip_in = jnp.transpose(conv_in[::-1, ::-1], (0, 1, 3, 2))
    flip_out = jnp.transpose(conv_out[::-1, ::-1], (0, 1, 3, 2))
    z1 = jnp.zeros_like(conv_in)
    z2 = jnp.zeros_like(conv_out)
    w1 = jnp.concatenate(
        [jnp.concatenate([conv_in, z1], axis=3), jnp.concatenate([z1, flip_out], axis=3)], axis=2
    ).reshape(3, 384, 256)
    w2 = jnp.concatenate(
        [
            jnp.concatenate([conv_out, z2], axis=3).reshape(3, 384, 128),
            jnp.concatenate([z2, flip_in], axis=3).reshape(3, 384, 128),
        ],
        axis=1,
    )
    lat = jnp.stack([lax.axis_index("lat"), jnp.int32(bands * rows)]).astype(jnp.int32)
    inner = rows + 2
    plane = (inner, WIDE, channels)
    used = 18 * (channels // 2) + 2 * channels
    per = -(-used // (8 * bands)) * 8
    shifted = (groups, inner, cols * mem_local, 384)
    compact = pltpu.HBM((groups, inner, width, channels), BF)
    hspec = pl.BlockSpec(memory_space=pltpu.HBM)
    grads, hid, dpre = pl.pallas_call(
        tile_kernel,
        out_shape=[vm((bands * per, channels), BF), compact, compact],
        in_specs=[sspec] + [vspec] * (chips + 4),
        out_specs=[vspec, hspec, hspec],
        scratch_shapes=[
            vm((groups, rows, width, 128), BF),
            vm((groups,) + plane, F32),
            vm((groups,) + plane, F32),
            vm((groups,) + plane, F32),
            vm(shifted, BF),
            vm(shifted, BF),
            vm((groups, rows, cols * mem_local, channels), BF),
            vm(compact.shape, BF),
            vm(compact.shape, BF),
            vm(plane, F32),
            vm(plane, F32),
            vm(plane, F32),
            vm(plane, F32),
            vm(plane, F32),
            pltpu.SemaphoreType.DMA((2,)),
        ],
        compiler_params=pltpu.CompilerParams(vmem_limit_bytes=48 * 1024 * 1024),
        name="tile",
    )(lat, *near(*tiles, top, bot, w1, pool_weight))
    pieces = pl.pallas_call(
        output_kernel,
        out_shape=[vm((2, rows, cols * mem_local, 128), BF)] * chips,
        in_specs=[vspec] * (chips + 3),
        out_specs=[vspec] * chips,
        name="output",
    )(*near(*tiles), hid, dpre, w2)

    def exchange(value, axis):
        return lax.all_to_all(value, axis, split_axis=0, concat_axis=0, tiled=True)

    def add_up(parts, copies, dtype):
        return pl.pallas_call(
            sum_kernel,
            out_shape=vm((copies,) + parts.shape[1:], dtype),
            in_specs=[vspec],
            out_specs=vspec,
            name="total",
        )(*near(parts))

    near_by = [swap(pieces[d], chips - d, 0, groups) for d in (1, chips - 1)]
    parts = exchange(grads.reshape(bands, per, channels), "lat")
    parts, near_by, middle = lax.optimization_barrier((parts, near_by, pieces[2]))
    middle = swap(middle, chips - 2, 0, groups)
    parts = exchange(add_up(parts, groups, F32), "member")
    parts, middle = lax.optimization_barrier((parts, middle))
    pieces = [pieces[0], near_by[0], middle, near_by[1]]
    other = pl.pallas_call(
        other_kernel,
        out_shape=vm((chips, rows, cols * mem_local, 128), BF),
        in_specs=[vspec] * chips,
        out_specs=vspec,
        name="other",
    )(*near(*pieces))
    theirs = swap(other, 0, 1, groups)
    full = exchange(add_up(parts, bands, BF), "lat").reshape(bands * per, channels)
    members = mem_local * groups
    scale = 1.0 / math.sqrt(members * bands * rows * lon)
    half = channels // 2
    grad_in, grad_out, grad_pool = pl.pallas_call(
        functools.partial(finish_kernel, scale),
        out_shape=[jax.ShapeDtypeStruct((n, channels), F32) for n in (9 * half, 9 * half, 2 * channels)],
        in_specs=[vspec],
        out_specs=[vspec] * 3,
        name="finish",
    )(*near(full))
    grad_in = grad_in.reshape(3, 3, half, channels)
    grad_out = grad_out.reshape(3, 3, half, channels).transpose(0, 1, 3, 2)

    encoded, d_input = pl.pallas_call(
        unpack_kernel,
        out_shape=[jax.ShapeDtypeStruct(ensemble.shape, BF)] * 2,
        in_specs=[sspec] + [vspec] * (chips + 1),
        out_specs=[vspec] * 2,
        scratch_shapes=[vm((rows, 2 * lon, 128), F32)],
        name="unpack",
    )(me, *near(*pieces, theirs))
    return encoded, d_input, grad_in, grad_pool, grad_out


def solution(mesh):
    return jax.shard_map(
        on_device,
        mesh=mesh,
        in_specs=(P("member", None, "lat", None), P("member", None, "lat", None), P(), P(), P()),
        out_specs=(P("member", None, "lat", None), P("member", None, "lat", None), P(), P(), P()),
        check_vma=False,
    )
```

```python
import functools
import math

import jax
import jax.numpy as jnp
from jax import lax
from jax.experimental import pallas as pl
from jax.experimental.pallas import tpu as pltpu
from jax.sharding import PartitionSpec as P


BF = jnp.bfloat16
F32 = jnp.float32
WIDE = 80


def swap(value, steps, cross, groups):
    chips = groups // 2
    pairs = [
        (2 * z + c, 2 * ((z + steps) % chips) + (c + cross) % 2) for z in range(chips) for c in range(2)
    ]
    return lax.ppermute(value, "member", pairs)


def column_block(device, steps, cross, groups):
    chips = groups // 2
    return 2 * lax.rem(device // 2 + steps, chips) + lax.rem(device + cross, 2)


def near(*values):
    return [pltpu.with_memory_space_constraint(v, pltpu.VMEM) for v in values]


def sigmoid(v):
    return 1.0 / (1.0 + jnp.exp(-v))


def split3(v):
    a = v.astype(BF)
    r = v - a.astype(F32)
    b = r.astype(BF)
    c = (r - b.astype(F32)).astype(BF)
    return a, b, c


def dot(a, b):
    return jnp.dot(a, b, preferred_element_type=F32)


def dot_t(a, b, dims):
    return lax.dot_general(a, b, (dims, ((), ())), preferred_element_type=F32)


def dot_rows(a, b):
    return dot_t(a, b, ((0,), (0,)))


def pack_kernel(me_ref, ens_ref, cot_ref, keep_ref, give_ref, plane):
    chips, _, width, _ = keep_ref.shape
    mem_local, _, rows, lon = ens_ref.shape
    for m in range(mem_local):
        for r in range(rows):
            both = jnp.concatenate([ens_ref[m, :, r, :], cot_ref[m, :, r, :]], axis=0).astype(F32).T
            plane[r, pl.ds(4 + m, lon, stride=2), :] = both
            plane[r, pl.ds(m, 2, stride=2), :] = both[lon - 2 :]
            plane[r, pl.ds(4 + 2 * lon + m, 2, stride=2), :] = both[:2]
    for d in range(chips):
        for cross, ref in enumerate((keep_ref, give_ref)):
            k = column_block(me_ref[0], d, cross, 2 * chips)
            for r in range(rows):
                ref[d, r] = plane[r, pl.ds(pl.multiple_of(k * (width - 8), 8), width), :].astype(BF)


def pair_kernel(keep_ref, got_ref, *out_refs):
    for d, ref in enumerate(out_refs):
        ref[0] = keep_ref[d]
        ref[1] = got_ref[d]


def edges_kernel(*refs):
    tiles, (head_ref, tail_ref) = refs[:-2], refs[-2:]
    rows = tiles[0].shape[1]
    for d, tile in enumerate(tiles):
        head_ref[2 * d : 2 * d + 2] = tile[:, :2]
        tail_ref[2 * d : 2 * d + 2] = tile[:, rows - 2 :]


def other_kernel(*refs):
    for d, tile in enumerate(refs[:-1]):
        refs[-1][d] = tile[1]


def unpack_kernel(me_ref, *refs):
    tiles, (theirs_ref, enc_ref, din_ref, plane) = refs[:-4], refs[-4:]
    chips = len(tiles)
    mem_local, half, rows, lon = enc_ref.shape
    width = theirs_ref.shape[2]
    for d in range(chips):
        for cross in range(2):
            k = column_block(me_ref[0], d, cross, 2 * chips)
            for r in range(rows):
                piece = theirs_ref[d, r] if cross else tiles[d][0, r]
                plane[r, pl.ds(pl.multiple_of(k * width, 8), width), :] = piece.astype(F32)
    for m in range(mem_local):
        for r in range(rows):
            both = plane[r, pl.ds(m, lon, stride=2), :].T.astype(BF)
            enc_ref[m, :, r, :] = both[:half]
            din_ref[m, :, r, :] = both[half:]


def tile_kernel(
    lat_ref, t0, t1, t2, t3, top_ref, bot_ref, w1_ref, pool_ref, _,
    grads_ref, hid_ref, dpre_ref,
    own_ref, pre_s, dh_s, act_s, xo_s, hq_s, dpo_s, hid_s, dpre_s, sum_s, var_s, shared_s, ca_s, cs_s, sems,
):
    srcs, rows, width, _ = own_ref.shape
    inner = rows + 2
    cols = xo_s.shape[2]
    nlat = lat_ref[1]
    for d, tile in enumerate((t0, t1, t2, t3)):
        own_ref[2 * d : 2 * d + 2] = tile[...]
    members = 2 * srcs
    channels = pre_s.shape[-1]
    shape = (inner, WIDE, channels)

    def up(v, n):
        return pltpu.roll(v, WIDE - n, 1) if n else v

    parity = lax.broadcasted_iota(jnp.int32, shape, 1) % 2

    def pair_sum(v):
        return v + jnp.where(parity == 0, up(v, 1), pltpu.roll(v, 1, 1))

    row_id = lax.broadcasted_iota(jnp.int32, shape, 0) + lat_ref[0] * rows - 1
    inside = jnp.logical_and(row_id >= 0, row_id < nlat)

    sum_s[...] = jnp.zeros(shape, F32)

    def first(s, carry):
        x = jnp.concatenate([top_ref[s], own_ref[s], bot_ref[s]], axis=0).astype(F32)
        x = jnp.concatenate([x, jnp.zeros((rows + 4, WIDE - width, 128), F32)], axis=1)
        x1, x2, x3 = up(x, 2), up(x, 4), up(x, 6)
        xs = jnp.concatenate([x, x1, x2], axis=-1).astype(BF)
        xo_s[s] = jnp.concatenate([v[1 : 1 + inner, :cols] for v in (x1, x2, x3)], axis=-1).astype(BF)
        acc = dot(xs[0:inner].reshape(inner * WIDE, 384), w1_ref[0])
        acc += dot(xs[1 : 1 + inner].reshape(inner * WIDE, 384), w1_ref[1])
        acc += dot(xs[2 : 2 + inner].reshape(inner * WIDE, 384), w1_ref[2])
        pre = acc[:, :channels].reshape(shape)
        pre_s[s] = pre
        dh_s[s] = acc[:, channels:].reshape(shape)
        act = (pre * sigmoid(pre)).astype(BF).astype(F32)
        act_s[s] = act
        sum_s[...] += act
        return carry

    lax.fori_loop(0, srcs, first, 0)
    average = pair_sum(sum_s[...]) * (1.0 / members)
    sum_s[...] = average
    var_s[...] = jnp.zeros(shape, F32)

    def second(s, carry):
        d = act_s[s] - sum_s[...]
        var_s[...] += d * d
        return carry

    lax.fori_loop(0, srcs, second, 0)
    spread = jnp.sqrt(pair_sum(var_s[...]) * (1.0 / members) + 0.1)
    var_s[...] = spread
    stats = jnp.concatenate([sum_s[...], spread], axis=-1).reshape(inner * WIDE, 2 * channels)
    s1, s2, s3 = split3(stats)
    pool = pool_ref[...]
    shared_s[...] = (dot(s1, pool) + dot(s2, pool) + dot(s3, pool)).reshape(shape)
    ca_s[...] = jnp.zeros(shape, F32)

    def third(s, carry):
        zed = act_s[s] + shared_s[...]
        sig = sigmoid(zed)
        hid = jnp.where(inside, (zed * sig).astype(BF).astype(F32), 0.0)
        dz = (dh_s[s] * (sig * (1.0 + zed * (1.0 - sig)))).astype(BF).astype(F32)
        dh_s[s] = dz
        ca_s[...] += dz
        hid_s[s] = hid[:, :width].astype(BF)
        hq_s[s] = jnp.concatenate([up(hid, 2 * q)[:, :cols] for q in range(3)], axis=-1).astype(BF)
        return carry

    lax.fori_loop(0, srcs, third, 0)
    hid_copy = pltpu.make_async_copy(hid_s, hid_ref, sems.at[0])
    hid_copy.start()
    d_shared = pair_sum(ca_s[...])
    d1, d2, d3 = split3(d_shared.reshape(inner * WIDE, channels))
    last = ((1,), (1,))
    d_stats = dot_t(d1, pool, last) + dot_t(d2, pool, last) + dot_t(d3, pool, last)
    ca_s[...] = (d_stats[:, :channels] * (1.0 / members)).reshape(shape)
    cs_s[...] = d_stats[:, channels:].reshape(shape) / (members * var_s[...])
    r_id = lax.broadcasted_iota(jnp.int32, shape, 0)
    c_id = lax.broadcasted_iota(jnp.int32, shape, 1)
    mine = (r_id >= 1) & (r_id <= rows) & (c_id >= 2) & (c_id < 2 + cols) & (parity == 0)
    e1, e2, e3 = split3(jnp.where(mine, d_shared, 0.0).reshape(inner * WIDE, channels))
    g_pool = dot_rows(s1, e1) + dot_rows(s1, e2) + dot_rows(s2, e1) + dot_rows(s2, e2) + dot_rows(s1, e3) + dot_rows(s3, e1)

    def fourth(s, carry):
        pre = pre_s[s]
        sig = sigmoid(pre)
        d_act = dh_s[s] + ca_s[...] + cs_s[...] * (act_s[s] - sum_s[...])
        dp = jnp.where(inside, d_act * (sig * (1.0 + pre * (1.0 - sig))), 0.0).astype(BF).astype(F32)
        dpre_s[s] = dp[:, :width].astype(BF)
        dpo_s[s] = up(dp, 2)[1 : 1 + rows, :cols].astype(BF)
        return carry

    lax.fori_loop(0, srcs, fourth, 0)
    dpre_copy = pltpu.make_async_copy(dpre_s, dpre_ref, sems.at[1])
    dpre_copy.start()

    total = srcs * rows * cols
    dpo = dpo_s[...].reshape(total, channels)
    own = xo_s[:, 1 : 1 + rows, :, 128:256].reshape(total, 128)
    half = channels // 2
    for p in range(3):
        g_in = dot_rows(dpo, xo_s[:, p : p + rows].reshape(total, 384))
        g_out = dot_rows(own, hq_s[:, p : p + rows].reshape(total, 384))
        for q in range(3):
            t = 3 * p + q
            grads_ref[t * half : (t + 1) * half, :] = g_in[:, q * 128 : (q + 1) * 128].T[:half].astype(BF)
            grads_ref[(9 + t) * half : (10 + t) * half, :] = g_out[half:, q * 128 : (q + 1) * 128].astype(BF)
    used = 18 * half + 2 * channels
    grads_ref[18 * half : used, :] = g_pool.astype(BF)
    if used < grads_ref.shape[0]:
        grads_ref[used:, :] = jnp.zeros((grads_ref.shape[0] - used, 128), BF)
    hid_copy.wait()
    dpre_copy.wait()


def output_kernel(t0, t1, t2, t3, hid_ref, dpre_ref, w2_ref, *out_refs):
    _, inner, width, _ = hid_ref.shape
    rows = inner - 2
    cols = out_refs[0].shape[2]

    def shifts(ref, s):
        v = ref[s].astype(F32)
        return [(pltpu.roll(v, width - 2 * q, 1) if q else v)[:, :cols] for q in range(3)]

    for d, (tile, out_ref) in enumerate(zip((t0, t1, t2, t3), out_refs)):

        def piece(j, carry):
            both = jnp.concatenate(shifts(hid_ref, 2 * d + j) + shifts(dpre_ref, 2 * d + j), axis=-1).astype(BF)
            depth = both.shape[-1]
            acc = dot(both[0:rows].reshape(rows * cols, depth), w2_ref[0])
            acc += dot(both[1 : 1 + rows].reshape(rows * cols, depth), w2_ref[1])
            acc += dot(both[2 : 2 + rows].reshape(rows * cols, depth), w2_ref[2])
            own = pltpu.roll(tile[j].astype(F32), width - 4, 1)[:, :cols]
            out_ref[j] = (own + acc.reshape(rows, cols, 128)).astype(BF)
            return carry

        lax.fori_loop(0, 2, piece, 0)


def sum_kernel(parts_ref, out_ref):
    total = jnp.sum(parts_ref[...].astype(F32), axis=0)
    out_ref[...] = jnp.broadcast_to(total[None], out_ref.shape).astype(out_ref.dtype)


def finish_kernel(scale, full_ref, in_ref, out_ref, pool_ref):
    start = 0
    for ref in (in_ref, out_ref, pool_ref):
        size = ref.shape[0]
        ref[...] = full_ref[start : start + size].astype(F32) * scale
        start += size


def block(ensemble, cotangent, conv_in, pool_weight, conv_out):
    mem_local, _, rows, lon = ensemble.shape
    groups = lax.axis_size("member")
    bands = lax.axis_size("lat")
    channels = conv_in.shape[-1]
    cols = lon // groups
    width = (cols + 4) * mem_local
    vspec = pl.BlockSpec(memory_space=pltpu.VMEM)
    sspec = pl.BlockSpec(memory_space=pltpu.SMEM)
    vm = pltpu.VMEM
    me = lax.axis_index("member").astype(jnp.int32).reshape(1)
    chips = groups // 2
    keep, give = pl.pallas_call(
        pack_kernel,
        out_shape=[vm((chips, rows, width, 128), BF)] * 2,
        in_specs=[sspec, vspec, vspec],
        out_specs=[vspec] * 2,
        scratch_shapes=[vm((rows, 2 * lon + 8, 128), F32)],
        name="pack",
    )(me, ensemble, cotangent)
    got = swap(give, 0, 1, groups)
    tiles = pl.pallas_call(
        pair_kernel,
        out_shape=[vm((2, rows, width, 128), BF)] * chips,
        in_specs=[vspec] * 2,
        out_specs=[vspec] * chips,
        name="pair",
    )(*near(keep, got))
    tiles = [tiles[0]] + [swap(tiles[d], d, 0, groups) for d in range(1, chips)]
    head, tail = pl.pallas_call(
        edges_kernel,
        out_shape=[vm((groups, 2, width, 128), BF)] * 2,
        in_specs=[vspec] * chips,
        out_specs=[vspec] * 2,
        name="edges",
    )(*near(*tiles))
    top = lax.ppermute(tail, "lat", [(i, i + 1) for i in range(bands - 1)])
    bot = lax.ppermute(head, "lat", [(i + 1, i) for i in range(bands - 1)])

    flip_in = jnp.transpose(conv_in[::-1, ::-1], (0, 1, 3, 2))
    flip_out = jnp.transpose(conv_out[::-1, ::-1], (0, 1, 3, 2))
    z1 = jnp.zeros_like(conv_in)
    z2 = jnp.zeros_like(conv_out)
    w1 = jnp.concatenate(
        [jnp.concatenate([conv_in, z1], axis=3), jnp.concatenate([z1, flip_out], axis=3)], axis=2
    ).reshape(3, 384, 256)
    w2 = jnp.concatenate(
        [
            jnp.concatenate([conv_out, z2], axis=3).reshape(3, 384, 128),
            jnp.concatenate([z2, flip_in], axis=3).reshape(3, 384, 128),
        ],
        axis=1,
    )
    lat = jnp.stack([lax.axis_index("lat"), jnp.int32(bands * rows)]).astype(jnp.int32)
    inner = rows + 2
    plane = (inner, WIDE, channels)
    used = 18 * (channels // 2) + 2 * channels
    per = -(-used // (8 * bands)) * 8
    shifted = (groups, inner, cols * mem_local, 384)
    compact = pltpu.HBM((groups, inner, width, channels), BF)
    hspec = pl.BlockSpec(memory_space=pltpu.HBM)
    grads, hid, dpre = pl.pallas_call(
        tile_kernel,
        out_shape=[vm((bands * per, channels), BF), compact, compact],
        in_specs=[sspec] + [vspec] * (chips + 4) + [hspec],
        out_specs=[vspec, hspec, hspec],
        scratch_shapes=[
            vm((groups, rows, width, 128), BF),
            vm((groups,) + plane, F32),
            vm((groups,) + plane, F32),
            vm((groups,) + plane, F32),
            vm(shifted, BF),
            vm(shifted, BF),
            vm((groups, rows, cols * mem_local, channels), BF),
            vm(compact.shape, BF),
            vm(compact.shape, BF),
            vm(plane, F32),
            vm(plane, F32),
            vm(plane, F32),
            vm(plane, F32),
            vm(plane, F32),
            pltpu.SemaphoreType.DMA((2,)),
        ],
        compiler_params=pltpu.CompilerParams(vmem_limit_bytes=48 * 1024 * 1024),
        name="tile",
    )(lat, *near(*tiles, top, bot, w1, pool_weight), w2)
    pieces = list(pl.pallas_call(
        output_kernel,
        out_shape=[vm((2, rows, cols * mem_local, 128), BF)] * chips,
        in_specs=[vspec] * (chips + 3),
        out_specs=[vspec] * chips,
        name="output",
    )(*near(*tiles), hid, dpre, w2))

    def exchange(value, axis):
        return lax.all_to_all(value, axis, split_axis=0, concat_axis=0, tiled=True)

    def add_up(parts, copies, dtype):
        return pl.pallas_call(
            sum_kernel,
            out_shape=vm((copies,) + parts.shape[1:], dtype),
            in_specs=[vspec],
            out_specs=vspec,
            name="total",
        )(*near(parts))

    parts = exchange(grads.reshape(bands, per, channels), "lat")
    far = swap(pieces[2], chips - 2, 0, groups)
    parts, pieces[1], pieces[3] = lax.optimization_barrier((parts, pieces[1], pieces[3]))
    pieces = [pieces[0]] + [far if d == 2 else swap(pieces[d], chips - d, 0, groups) for d in range(1, chips)]
    parts = add_up(parts, groups, F32)
    parts = exchange(parts, "member")
    parts, pieces[1], pieces[3] = lax.optimization_barrier((parts, pieces[1], pieces[3]))
    other = pl.pallas_call(
        other_kernel,
        out_shape=vm((chips, rows, cols * mem_local, 128), BF),
        in_specs=[vspec] * chips,
        out_specs=vspec,
        name="other",
    )(*near(*pieces))
    theirs = swap(other, 0, 1, groups)
    full = exchange(add_up(parts, bands, BF), "lat").reshape(bands * per, channels)
    members = mem_local * groups
    scale = 1.0 / math.sqrt(members * bands * rows * lon)
    half = channels // 2
    grad_in, grad_out, grad_pool = pl.pallas_call(
        functools.partial(finish_kernel, scale),
        out_shape=[jax.ShapeDtypeStruct((n, channels), F32) for n in (9 * half, 9 * half, 2 * channels)],
        in_specs=[vspec],
        out_specs=[vspec] * 3,
        name="finish",
    )(*near(full))
    grad_in = grad_in.reshape(3, 3, half, channels)
    grad_out = grad_out.reshape(3, 3, half, channels).transpose(0, 1, 3, 2)

    encoded, d_input = pl.pallas_call(
        unpack_kernel,
        out_shape=[jax.ShapeDtypeStruct(ensemble.shape, BF)] * 2,
        in_specs=[sspec] + [vspec] * (chips + 1),
        out_specs=[vspec] * 2,
        scratch_shapes=[vm((rows, 2 * lon, 128), F32)],
        name="unpack",
    )(me, *near(*pieces, theirs))
    return encoded, d_input, grad_in, grad_pool, grad_out


def solution(mesh):
    return jax.shard_map(
        block,
        mesh=mesh,
        in_specs=(P("member", None, "lat", None), P("member", None, "lat", None), P(), P(), P()),
        out_specs=(P("member", None, "lat", None), P("member", None, "lat", None), P(), P(), P()),
        check_vma=False,
    )
```

```python
import functools
import math

import jax
import jax.numpy as jnp
from jax import lax
from jax.experimental import pallas as pl
from jax.experimental.pallas import tpu as pltpu
from jax.sharding import PartitionSpec as P


BF = jnp.bfloat16
F32 = jnp.float32
WIDE = 80


ORDER = (0, 1, 3, 2)


def swap(value, steps, cross, groups):
    chips = groups // 2
    pairs = [
        (2 * z + c, 2 * ((z + steps) % chips) + (c + cross) % 2) for z in range(chips) for c in range(2)
    ]
    return lax.ppermute(value, "member", pairs)


def column_block(device, steps, cross, groups):
    chips = groups // 2
    return 2 * lax.rem(device // 2 + steps, chips) + lax.rem(device + cross, 2)


def near(*values):
    return [pltpu.with_memory_space_constraint(v, pltpu.VMEM) for v in values]


def sigmoid(v):
    return 1.0 / (1.0 + jnp.exp(-v))


def split3(v):
    a = v.astype(BF)
    r = v - a.astype(F32)
    b = r.astype(BF)
    c = (r - b.astype(F32)).astype(BF)
    return a, b, c


def dot(a, b):
    return jnp.dot(a, b, preferred_element_type=F32)


def dot_t(a, b, dims):
    return lax.dot_general(a, b, (dims, ((), ())), preferred_element_type=F32)


def dot_rows(a, b):
    return dot_t(a, b, ((0,), (0,)))


def pack_kernel(me_ref, ens_ref, cot_ref, keep_ref, give_ref, plane):
    chips, _, width, _ = keep_ref.shape
    mem_local, _, rows, lon = ens_ref.shape
    for m in range(mem_local):
        for r in range(rows):
            both = jnp.concatenate([ens_ref[m, :, r, :], cot_ref[m, :, r, :]], axis=0).astype(F32).T
            plane[r, pl.ds(4 + m, lon, stride=2), :] = both
            plane[r, pl.ds(m, 2, stride=2), :] = both[lon - 2 :]
            plane[r, pl.ds(4 + 2 * lon + m, 2, stride=2), :] = both[:2]
    for d in range(chips):
        for cross, ref in enumerate((keep_ref, give_ref)):
            k = column_block(me_ref[0], ORDER[d], cross, 2 * chips)
            for r in range(rows):
                ref[d, r] = plane[r, pl.ds(pl.multiple_of(k * (width - 8), 8), width), :].astype(BF)


def pair_kernel(keep_ref, got_ref, *out_refs):
    for d, ref in enumerate(out_refs):
        ref[0] = keep_ref[d]
        ref[1] = got_ref[d]


def edges_kernel(*refs):
    tiles, (head_ref, tail_ref) = refs[:-2], refs[-2:]
    rows = tiles[0].shape[1]
    for d, tile in enumerate(tiles):
        head_ref[2 * d : 2 * d + 2] = tile[:, :2]
        tail_ref[2 * d : 2 * d + 2] = tile[:, rows - 2 :]


def other_kernel(*refs):
    for d, tile in enumerate(refs[:-1]):
        refs[-1][d] = tile[1]


def unpack_kernel(me_ref, *refs):
    tiles, (theirs_ref, enc_ref, din_ref, plane) = refs[:-4], refs[-4:]
    chips = len(tiles)
    mem_local, half, rows, lon = enc_ref.shape
    width = theirs_ref.shape[2]
    for d in range(chips):
        for cross in range(2):
            k = column_block(me_ref[0], ORDER[d], cross, 2 * chips)
            for r in range(rows):
                piece = theirs_ref[d, r] if cross else tiles[d][0, r]
                plane[r, pl.ds(pl.multiple_of(k * width, 8), width), :] = piece.astype(F32)
    for m in range(mem_local):
        for r in range(rows):
            both = plane[r, pl.ds(m, lon, stride=2), :].T.astype(BF)
            enc_ref[m, :, r, :] = both[:half]
            din_ref[m, :, r, :] = both[half:]


def tile_kernel(
    lat_ref, t0, t1, t2, t3, top0, top1, bot0, bot1, w1_ref, pool_ref, _,
    grads_ref, hid_ref, dpre_ref,
    own_ref, top_ref, bot_ref, pre_s, dh_s, act_s, xo_s, oc_s, hq_s, dpo_s, hid_s, dpre_s, sum_s, var_s, shared_s, ca_s, cs_s, sems,
):
    srcs, rows, width, _ = own_ref.shape
    inner = rows + 2
    cols = xo_s.shape[2]
    nlat = lat_ref[1]
    for d, tile in enumerate((t0, t1, t2, t3)):
        own_ref[2 * d : 2 * d + 2] = tile[...]
    split = top0.shape[0]
    top_ref[:split] = top0[...]
    top_ref[split:] = top1[...]
    bot_ref[:split] = bot0[...]
    bot_ref[split:] = bot1[...]
    members = 2 * srcs
    channels = pre_s.shape[-1]
    shape = (inner, WIDE, channels)

    def up(v, n):
        return pltpu.roll(v, WIDE - n, 1) if n else v

    parity = lax.broadcasted_iota(jnp.int32, shape, 1) % 2

    def pair_sum(v):
        return v + jnp.where(parity == 0, up(v, 1), pltpu.roll(v, 1, 1))

    row_id = lax.broadcasted_iota(jnp.int32, shape, 0) + lat_ref[0] * rows - 1
    inside = jnp.logical_and(row_id >= 0, row_id < nlat)

    sum_s[...] = jnp.zeros(shape, F32)

    def first(s, carry):
        x = jnp.concatenate([top_ref[s], own_ref[s], bot_ref[s]], axis=0).astype(F32)
        x = jnp.concatenate([x, jnp.zeros((rows + 4, WIDE - width, 128), F32)], axis=1)
        x1, x2, x3 = up(x, 2), up(x, 4), up(x, 6)
        xs = jnp.concatenate([x, x1, x2], axis=-1).astype(BF)
        own = [v[1 : 1 + inner, :cols] for v in (x1, x2, x3)]
        half = channels // 2
        xo_s[s] = jnp.concatenate([v[..., :half] for v in own], axis=-1).astype(BF)
        oc_s[s] = own[1][1 : 1 + rows].astype(BF)
        xs = jnp.concatenate([xs[p : p + inner] for p in range(3)], axis=-1)
        acc = dot(xs.reshape(inner * WIDE, 1152), w1_ref[...])
        pre = acc[:, :channels].reshape(shape)
        pre_s[s] = pre
        dh_s[s] = acc[:, channels:].reshape(shape)
        act = (pre * sigmoid(pre)).astype(BF).astype(F32)
        act_s[s] = act
        sum_s[...] += act
        return carry

    lax.fori_loop(0, srcs, first, 0)
    average = pair_sum(sum_s[...]) * (1.0 / members)
    sum_s[...] = average
    var_s[...] = jnp.zeros(shape, F32)

    def second(s, carry):
        d = act_s[s] - sum_s[...]
        var_s[...] += d * d
        return carry

    lax.fori_loop(0, srcs, second, 0)
    spread = jnp.sqrt(pair_sum(var_s[...]) * (1.0 / members) + 0.1)
    var_s[...] = spread
    stats = jnp.concatenate([sum_s[...], spread], axis=-1).reshape(inner * WIDE, 2 * channels)
    s1, s2, s3 = split3(stats)
    pool = pool_ref[...]
    shared_s[...] = (dot(s1, pool) + dot(s2, pool) + dot(s3, pool)).reshape(shape)
    ca_s[...] = jnp.zeros(shape, F32)

    def third(s, carry):
        zed = act_s[s] + shared_s[...]
        sig = sigmoid(zed)
        hid = jnp.where(inside, (zed * sig).astype(BF).astype(F32), 0.0)
        dz = (dh_s[s] * (sig * (1.0 + zed * (1.0 - sig)))).astype(BF).astype(F32)
        dh_s[s] = dz
        ca_s[...] += dz
        hid_s[s] = hid[:, :width].astype(BF)
        hq_s[s] = jnp.concatenate([up(hid, 2 * q)[:, :cols] for q in range(3)], axis=-1).astype(BF)
        return carry

    lax.fori_loop(0, srcs, third, 0)
    hid_copy = pltpu.make_async_copy(hid_s, hid_ref, sems.at[0])
    hid_copy.start()
    d_shared = pair_sum(ca_s[...])
    d1, d2, d3 = split3(d_shared.reshape(inner * WIDE, channels))
    last = ((1,), (1,))
    d_stats = dot_t(d1, pool, last) + dot_t(d2, pool, last) + dot_t(d3, pool, last)
    ca_s[...] = (d_stats[:, :channels] * (1.0 / members)).reshape(shape)
    cs_s[...] = d_stats[:, channels:].reshape(shape) / (members * var_s[...])
    r_id = lax.broadcasted_iota(jnp.int32, shape, 0)
    c_id = lax.broadcasted_iota(jnp.int32, shape, 1)
    mine = (r_id >= 1) & (r_id <= rows) & (c_id >= 2) & (c_id < 2 + cols) & (parity == 0)
    e1, e2, e3 = split3(jnp.where(mine, d_shared, 0.0).reshape(inner * WIDE, channels))
    g_pool = dot_rows(s1, e1) + dot_rows(s1, e2) + dot_rows(s2, e1) + dot_rows(s2, e2) + dot_rows(s1, e3) + dot_rows(s3, e1)

    def fourth(s, carry):
        pre = pre_s[s]
        sig = sigmoid(pre)
        d_act = dh_s[s] + ca_s[...] + cs_s[...] * (act_s[s] - sum_s[...])
        dp = jnp.where(inside, d_act * (sig * (1.0 + pre * (1.0 - sig))), 0.0).astype(BF).astype(F32)
        dpre_s[s] = dp[:, :width].astype(BF)
        dpo_s[s] = up(dp, 2)[1 : 1 + rows, :cols].astype(BF)
        return carry

    lax.fori_loop(0, srcs, fourth, 0)
    dpre_copy = pltpu.make_async_copy(dpre_s, dpre_ref, sems.at[1])
    dpre_copy.start()

    total = srcs * rows * cols
    dpo = dpo_s[...].reshape(total, channels)
    own = oc_s[...].reshape(total, 128)
    half = channels // 2
    taps = 3 * half
    for p in range(3):
        g_in = dot_rows(dpo, xo_s[:, p : p + rows].reshape(total, taps))
        grads_ref[p * taps : (p + 1) * taps, :] = g_in.T.astype(BF)
    hqs = jnp.concatenate([hq_s[:, p : p + rows].reshape(total, 384) for p in range(3)], axis=-1)
    g_out = dot_rows(own, hqs)
    for t in range(9):
        grads_ref[(9 + t) * half : (10 + t) * half, :] = g_out[half:, t * 128 : (t + 1) * 128].astype(BF)
    used = 18 * half + 2 * channels
    grads_ref[18 * half : used, :] = g_pool.astype(BF)
    if used < grads_ref.shape[0]:
        grads_ref[used:, :] = jnp.zeros((grads_ref.shape[0] - used, 128), BF)
    hid_copy.wait()
    dpre_copy.wait()


def output_kernel(t0, t1, t2, t3, hid_ref, dpre_ref, w2_ref, *out_refs):
    _, inner, width, _ = hid_ref.shape
    rows = inner - 2
    cols = out_refs[0].shape[2]

    def shifts(ref, s):
        v = ref[s].astype(F32)
        return [(pltpu.roll(v, width - 2 * q, 1) if q else v)[:, :cols] for q in range(3)]

    for d, (tile, out_ref) in enumerate(zip((t0, t1, t2, t3), out_refs)):

        def piece(j, carry):
            both = jnp.concatenate(shifts(hid_ref, 2 * d + j) + shifts(dpre_ref, 2 * d + j), axis=-1).astype(BF)
            depth = both.shape[-1]
            acc = dot(both[0:rows].reshape(rows * cols, depth), w2_ref[0])
            acc += dot(both[1 : 1 + rows].reshape(rows * cols, depth), w2_ref[1])
            acc += dot(both[2 : 2 + rows].reshape(rows * cols, depth), w2_ref[2])
            own = pltpu.roll(tile[j].astype(F32), width - 4, 1)[:, :cols]
            out_ref[j] = (own + acc.reshape(rows, cols, 128)).astype(BF)
            return carry

        lax.fori_loop(0, 2, piece, 0)


def sum_kernel(parts_ref, out_ref):
    total = jnp.sum(parts_ref[...].astype(F32), axis=0)
    out_ref[...] = jnp.broadcast_to(total[None], out_ref.shape).astype(out_ref.dtype)


def finish_kernel(scale, full_ref, in_ref, out_ref, pool_ref):
    start = 0
    for ref in (in_ref, out_ref, pool_ref):
        size = ref.shape[0]
        ref[...] = full_ref[start : start + size].astype(F32) * scale
        start += size


def block(ensemble, cotangent, conv_in, pool_weight, conv_out):
    mem_local, _, rows, lon = ensemble.shape
    groups = lax.axis_size("member")
    bands = lax.axis_size("lat")
    channels = conv_in.shape[-1]
    cols = lon // groups
    width = (cols + 4) * mem_local
    vspec = pl.BlockSpec(memory_space=pltpu.VMEM)
    sspec = pl.BlockSpec(memory_space=pltpu.SMEM)
    vm = pltpu.VMEM
    me = lax.axis_index("member").astype(jnp.int32).reshape(1)
    chips = groups // 2
    keep, give = pl.pallas_call(
        pack_kernel,
        out_shape=[vm((chips, rows, width, 128), BF)] * 2,
        in_specs=[sspec, vspec, vspec],
        out_specs=[vspec] * 2,
        scratch_shapes=[vm((rows, 2 * lon + 8, 128), F32)],
        name="pack",
    )(me, ensemble, cotangent)
    got = swap(give, 0, 1, groups)
    tiles = pl.pallas_call(
        pair_kernel,
        out_shape=[vm((2, rows, width, 128), BF)] * chips,
        in_specs=[vspec] * 2,
        out_specs=[vspec] * chips,
        name="pair",
    )(*near(keep, got))
    tiles = [tiles[0]] + [swap(tiles[i], ORDER[i], 0, groups) for i in range(1, chips)]

    def edges(*sources):
        return pl.pallas_call(
            edges_kernel,
            out_shape=[vm((2 * len(sources), 2, width, 128), BF)] * 2,
            in_specs=[vspec] * len(sources),
            out_specs=[vspec] * 2,
            name="edges",
        )(*near(*sources))

    def to_bands(head, tail):
        top = lax.ppermute(tail, "lat", [(i, i + 1) for i in range(bands - 1)])
        bot = lax.ppermute(head, "lat", [(i + 1, i) for i in range(bands - 1)])
        return top, bot

    first_edges = edges(*tiles[:3])
    top0, bot0 = to_bands(*first_edges)
    last_edges = edges(*tiles[3:])
    top1, bot1 = to_bands(*last_edges)

    flip_in = jnp.transpose(conv_in[::-1, ::-1], (0, 1, 3, 2))
    flip_out = jnp.transpose(conv_out[::-1, ::-1], (0, 1, 3, 2))
    z1 = jnp.zeros_like(conv_in)
    z2 = jnp.zeros_like(conv_out)
    w1 = jnp.concatenate(
        [jnp.concatenate([conv_in, z1], axis=3), jnp.concatenate([z1, flip_out], axis=3)], axis=2
    ).reshape(1152, 256)
    w2 = jnp.concatenate(
        [
            jnp.concatenate([conv_out, z2], axis=3).reshape(3, 384, 128),
            jnp.concatenate([z2, flip_in], axis=3).reshape(3, 384, 128),
        ],
        axis=1,
    )
    lat = jnp.stack([lax.axis_index("lat"), jnp.int32(bands * rows)]).astype(jnp.int32)
    inner = rows + 2
    plane = (inner, WIDE, channels)
    used = 18 * (channels // 2) + 2 * channels
    per = -(-used // (8 * bands)) * 8
    shifted = (groups, inner, cols * mem_local, 384)
    compact = pltpu.HBM((groups, inner, width, channels), BF)
    hspec = pl.BlockSpec(memory_space=pltpu.HBM)
    grads, hid, dpre = pl.pallas_call(
        tile_kernel,
        out_shape=[vm((bands * per, channels), BF), compact, compact],
        in_specs=[sspec] + [vspec] * (chips + 6) + [hspec],
        out_specs=[vspec, hspec, hspec],
        scratch_shapes=[
            vm((groups, rows, width, 128), BF),
            vm((groups, 2, width, 128), BF),
            vm((groups, 2, width, 128), BF),
            vm((groups,) + plane, F32),
            vm((groups,) + plane, F32),
            vm((groups,) + plane, F32),
            vm(shifted[:3] + (192,), BF),
            vm((groups, rows, cols * mem_local, 128), BF),
            vm(shifted, BF),
            vm((groups, rows, cols * mem_local, channels), BF),
            vm(compact.shape, BF),
            vm(compact.shape, BF),
            vm(plane, F32),
            vm(plane, F32),
            vm(plane, F32),
            vm(plane, F32),
            vm(plane, F32),
            pltpu.SemaphoreType.DMA((2,)),
        ],
        compiler_params=pltpu.CompilerParams(vmem_limit_bytes=48 * 1024 * 1024),
        name="tile",
    )(lat, *near(*tiles, top0, top1, bot0, bot1, w1, pool_weight), w2)
    pieces = list(pl.pallas_call(
        output_kernel,
        out_shape=[vm((2, rows, cols * mem_local, 128), BF)] * chips,
        in_specs=[vspec] * (chips + 3),
        out_specs=[vspec] * chips,
        name="output",
    )(*near(*tiles), hid, dpre, w2))

    def exchange(value, axis):
        return lax.all_to_all(value, axis, split_axis=0, concat_axis=0, tiled=True)

    def add_up(parts, copies, dtype):
        return pl.pallas_call(
            sum_kernel,
            out_shape=vm((copies,) + parts.shape[1:], dtype),
            in_specs=[vspec],
            out_specs=vspec,
            name="total",
        )(*near(parts))

    parts = exchange(grads.reshape(bands, per, channels), "lat")
    far = swap(pieces[3], chips - ORDER[3], 0, groups)
    parts, pieces[1], pieces[2] = lax.optimization_barrier((parts, pieces[1], pieces[2]))
    pieces[1:3] = [swap(piece, chips - d, 0, groups) for d, piece in zip(ORDER[1:3], pieces[1:3])]
    pieces[3] = far
    parts = add_up(parts, groups, F32)
    parts = exchange(parts, "member")
    parts = add_up(parts, bands, BF)
    other = pl.pallas_call(
        other_kernel,
        out_shape=vm((chips, rows, cols * mem_local, 128), BF),
        in_specs=[vspec] * chips,
        out_specs=vspec,
        name="other",
    )(*near(*pieces))
    theirs = swap(other, 0, 1, groups)
    full = exchange(parts, "lat").reshape(bands * per, channels)
    members = mem_local * groups
    scale = 1.0 / math.sqrt(members * bands * rows * lon)
    half = channels // 2
    grad_in, grad_out, grad_pool = pl.pallas_call(
        functools.partial(finish_kernel, scale),
        out_shape=[jax.ShapeDtypeStruct((n, channels), F32) for n in (9 * half, 9 * half, 2 * channels)],
        in_specs=[vspec],
        out_specs=[vspec] * 3,
        name="finish",
    )(*near(full))
    grad_in = grad_in.reshape(3, 3, half, channels)
    grad_out = grad_out.reshape(3, 3, half, channels).transpose(0, 1, 3, 2)

    encoded, d_input = pl.pallas_call(
        unpack_kernel,
        out_shape=[jax.ShapeDtypeStruct(ensemble.shape, BF)] * 2,
        in_specs=[sspec] + [vspec] * (chips + 1),
        out_specs=[vspec] * 2,
        scratch_shapes=[vm((rows, 2 * lon, 128), F32)],
        name="unpack",
    )(me, *near(*pieces, theirs))
    return encoded, d_input, grad_in, grad_pool, grad_out


def solution(mesh):
    return jax.shard_map(
        block,
        mesh=mesh,
        in_specs=(P("member", None, "lat", None), P("member", None, "lat", None), P(), P(), P()),
        out_specs=(P("member", None, "lat", None), P("member", None, "lat", None), P(), P(), P()),
        check_vma=False,
    )
```

```python
import functools
import math

import jax
import jax.numpy as jnp
from jax import lax
from jax.experimental import pallas as pl
from jax.experimental.pallas import tpu as pltpu
from jax.sharding import Mesh
from jax.sharding import PartitionSpec as P


BF = jnp.bfloat16
F32 = jnp.float32
WIDE = 80


MEMBER = ("zh", "core")
LAT = ("y", "zl", "x")
PLANE = ("y", "x")
REST = ("zh", "core", "zl")
ORDER = (0, 1, 3, 2)


def swap(value, steps, cross, groups):
    chips = groups // 2
    pairs = [
        (2 * z + c, 2 * ((z + steps) % chips) + (c + cross) % 2) for z in range(chips) for c in range(2)
    ]
    return lax.ppermute(value, MEMBER, pairs)


def column_block(device, steps, cross, groups):
    chips = groups // 2
    return 2 * lax.rem(device // 2 + steps, chips) + lax.rem(device + cross, 2)


def near(*values):
    return [pltpu.with_memory_space_constraint(v, pltpu.VMEM) for v in values]


def sigmoid(v):
    return 1.0 / (1.0 + jnp.exp(-v))


def split3(v):
    a = v.astype(BF)
    r = v - a.astype(F32)
    b = r.astype(BF)
    c = (r - b.astype(F32)).astype(BF)
    return a, b, c


def dot(a, b):
    return jnp.dot(a, b, preferred_element_type=F32)


def dot_t(a, b, dims):
    return lax.dot_general(a, b, (dims, ((), ())), preferred_element_type=F32)


def dot_rows(a, b):
    return dot_t(a, b, ((0,), (0,)))


def pack_kernel(me_ref, ens_ref, cot_ref, keep_ref, give_ref, plane):
    chips, _, width, _ = keep_ref.shape
    mem_local, _, rows, lon = ens_ref.shape
    for m in range(mem_local):
        for r in range(rows):
            both = jnp.concatenate([ens_ref[m, :, r, :], cot_ref[m, :, r, :]], axis=0).astype(F32).T
            plane[r, pl.ds(4 + m, lon, stride=2), :] = both
            plane[r, pl.ds(m, 2, stride=2), :] = both[lon - 2 :]
            plane[r, pl.ds(4 + 2 * lon + m, 2, stride=2), :] = both[:2]
    for d in range(chips):
        for cross, ref in enumerate((keep_ref, give_ref)):
            k = column_block(me_ref[0], ORDER[d], cross, 2 * chips)
            for r in range(rows):
                ref[d, r] = plane[r, pl.ds(pl.multiple_of(k * (width - 8), 8), width), :].astype(BF)


def pair_kernel(keep_ref, got_ref, *out_refs):
    for d, ref in enumerate(out_refs):
        ref[0] = keep_ref[d]
        ref[1] = got_ref[d]


def edges_kernel(*refs):
    tiles, (head_ref, tail_ref) = refs[:-2], refs[-2:]
    rows = tiles[0].shape[1]
    for d, tile in enumerate(tiles):
        head_ref[2 * d : 2 * d + 2] = tile[:, :2]
        tail_ref[2 * d : 2 * d + 2] = tile[:, rows - 2 :]


def other_kernel(*refs):
    for d, tile in enumerate(refs[:-1]):
        refs[-1][d] = tile[1]


def unpack_kernel(me_ref, *refs):
    tiles, (theirs_ref, enc_ref, din_ref, plane) = refs[:-4], refs[-4:]
    chips = len(tiles)
    mem_local, half, rows, lon = enc_ref.shape
    width = theirs_ref.shape[2]
    for d in range(chips):
        for cross in range(2):
            k = column_block(me_ref[0], ORDER[d], cross, 2 * chips)
            for r in range(rows):
                piece = theirs_ref[d, r] if cross else tiles[d][0, r]
                plane[r, pl.ds(pl.multiple_of(k * width, 8), width), :] = piece.astype(F32)
    for m in range(mem_local):
        for r in range(rows):
            both = plane[r, pl.ds(m, lon, stride=2), :].T.astype(BF)
            enc_ref[m, :, r, :] = both[:half]
            din_ref[m, :, r, :] = both[half:]


def tile_kernel(
    lat_ref, t0, t1, t2, t3, top_ref, bot_ref, w1_ref, pool_ref, _,
    grads_ref, hid_ref, dpre_ref,
    own_ref, pre_s, dh_s, act_s, xo_s, oc_s, hq_s, dpo_s, hid_s, dpre_s, sum_s, var_s, shared_s, ca_s, cs_s, sems,
):
    srcs, rows, width, _ = own_ref.shape
    inner = rows + 2
    cols = xo_s.shape[2]
    nlat = lat_ref[1]
    for d, tile in enumerate((t0, t1, t2, t3)):
        own_ref[2 * d : 2 * d + 2] = tile[...]
    members = 2 * srcs
    channels = pre_s.shape[-1]
    shape = (inner, WIDE, channels)

    def up(v, n):
        return pltpu.roll(v, WIDE - n, 1) if n else v

    parity = lax.broadcasted_iota(jnp.int32, shape, 1) % 2

    def pair_sum(v):
        return v + jnp.where(parity == 0, up(v, 1), pltpu.roll(v, 1, 1))

    row_id = lax.broadcasted_iota(jnp.int32, shape, 0) + lat_ref[0] * rows - 1
    inside = jnp.logical_and(row_id >= 0, row_id < nlat)

    sum_s[...] = jnp.zeros(shape, F32)

    def first(s, carry):
        x = jnp.concatenate([top_ref[s], own_ref[s], bot_ref[s]], axis=0).astype(F32)
        x = jnp.concatenate([x, jnp.zeros((rows + 4, WIDE - width, 128), F32)], axis=1)
        x1, x2, x3 = up(x, 2), up(x, 4), up(x, 6)
        xs = jnp.concatenate([x, x1, x2], axis=-1).astype(BF)
        own = [v[1 : 1 + inner, :cols] for v in (x1, x2, x3)]
        half = channels // 2
        xo_s[s] = jnp.concatenate([v[..., :half] for v in own], axis=-1).astype(BF)
        oc_s[s] = own[1][1 : 1 + rows].astype(BF)
        xs = jnp.concatenate([xs[p : p + inner] for p in range(3)], axis=-1)
        acc = dot(xs.reshape(inner * WIDE, 1152), w1_ref[...])
        pre = acc[:, :channels].reshape(shape)
        pre_s[s] = pre
        dh_s[s] = acc[:, channels:].reshape(shape)
        act = (pre * sigmoid(pre)).astype(BF).astype(F32)
        act_s[s] = act
        sum_s[...] += act
        return carry

    lax.fori_loop(0, srcs, first, 0)
    average = pair_sum(sum_s[...]) * (1.0 / members)
    sum_s[...] = average
    var_s[...] = jnp.zeros(shape, F32)

    def second(s, carry):
        d = act_s[s] - sum_s[...]
        var_s[...] += d * d
        return carry

    lax.fori_loop(0, srcs, second, 0)
    spread = jnp.sqrt(pair_sum(var_s[...]) * (1.0 / members) + 0.1)
    var_s[...] = spread
    stats = jnp.concatenate([sum_s[...], spread], axis=-1).reshape(inner * WIDE, 2 * channels)
    s1, s2, s3 = split3(stats)
    pool = pool_ref[...]
    shared_s[...] = (dot(s1, pool) + dot(s2, pool) + dot(s3, pool)).reshape(shape)
    ca_s[...] = jnp.zeros(shape, F32)

    def third(s, carry):
        zed = act_s[s] + shared_s[...]
        sig = sigmoid(zed)
        hid = jnp.where(inside, (zed * sig).astype(BF).astype(F32), 0.0)
        dz = (dh_s[s] * (sig * (1.0 + zed * (1.0 - sig)))).astype(BF).astype(F32)
        dh_s[s] = dz
        ca_s[...] += dz
        hid_s[s] = hid[:, :width].astype(BF)
        hq_s[s] = jnp.concatenate([up(hid, 2 * q)[:, :cols] for q in range(3)], axis=-1).astype(BF)
        return carry

    lax.fori_loop(0, srcs, third, 0)
    hid_copy = pltpu.make_async_copy(hid_s, hid_ref, sems.at[0])
    hid_copy.start()
    d_shared = pair_sum(ca_s[...])
    d1, d2, d3 = split3(d_shared.reshape(inner * WIDE, channels))
    last = ((1,), (1,))
    d_stats = dot_t(d1, pool, last) + dot_t(d2, pool, last) + dot_t(d3, pool, last)
    ca_s[...] = (d_stats[:, :channels] * (1.0 / members)).reshape(shape)
    cs_s[...] = d_stats[:, channels:].reshape(shape) / (members * var_s[...])
    r_id = lax.broadcasted_iota(jnp.int32, shape, 0)
    c_id = lax.broadcasted_iota(jnp.int32, shape, 1)
    mine = (r_id >= 1) & (r_id <= rows) & (c_id >= 2) & (c_id < 2 + cols) & (parity == 0)
    e1, e2, e3 = split3(jnp.where(mine, d_shared, 0.0).reshape(inner * WIDE, channels))
    g_pool = dot_rows(s1, e1) + dot_rows(s1, e2) + dot_rows(s2, e1) + dot_rows(s2, e2) + dot_rows(s1, e3) + dot_rows(s3, e1)

    def fourth(s, carry):
        pre = pre_s[s]
        sig = sigmoid(pre)
        d_act = dh_s[s] + ca_s[...] + cs_s[...] * (act_s[s] - sum_s[...])
        dp = jnp.where(inside, d_act * (sig * (1.0 + pre * (1.0 - sig))), 0.0).astype(BF).astype(F32)
        dpre_s[s] = dp[:, :width].astype(BF)
        dpo_s[s] = up(dp, 2)[1 : 1 + rows, :cols].astype(BF)
        return carry

    lax.fori_loop(0, srcs, fourth, 0)
    dpre_copy = pltpu.make_async_copy(dpre_s, dpre_ref, sems.at[1])
    dpre_copy.start()

    total = srcs * rows * cols
    dpo = dpo_s[...].reshape(total, channels)
    own = oc_s[...].reshape(total, 128)
    half = channels // 2
    taps = 3 * half
    for p in range(3):
        g_in = dot_rows(dpo, xo_s[:, p : p + rows].reshape(total, taps))
        grads_ref[p * taps : (p + 1) * taps, :] = g_in.T.astype(BF)
    hqs = jnp.concatenate([hq_s[:, p : p + rows].reshape(total, 384) for p in range(3)], axis=-1)
    g_out = dot_rows(own, hqs)
    for t in range(9):
        grads_ref[(9 + t) * half : (10 + t) * half, :] = g_out[half:, t * 128 : (t + 1) * 128].astype(BF)
    used = 18 * half + 2 * channels
    grads_ref[18 * half : used, :] = g_pool.astype(BF)
    if used < grads_ref.shape[0]:
        grads_ref[used:, :] = jnp.zeros((grads_ref.shape[0] - used, 128), BF)
    hid_copy.wait()
    dpre_copy.wait()


def output_kernel(t0, t1, t2, t3, hid_ref, dpre_ref, w2_ref, *out_refs):
    _, inner, width, _ = hid_ref.shape
    rows = inner - 2
    cols = out_refs[0].shape[2]

    def shifts(ref, s):
        v = ref[s].astype(F32)
        return [(pltpu.roll(v, width - 2 * q, 1) if q else v)[:, :cols] for q in range(3)]

    for d, (tile, out_ref) in enumerate(zip((t0, t1, t2, t3), out_refs)):

        def piece(j, carry):
            both = jnp.concatenate(shifts(hid_ref, 2 * d + j) + shifts(dpre_ref, 2 * d + j), axis=-1).astype(BF)
            depth = both.shape[-1]
            acc = dot(both[0:rows].reshape(rows * cols, depth), w2_ref[0])
            acc += dot(both[1 : 1 + rows].reshape(rows * cols, depth), w2_ref[1])
            acc += dot(both[2 : 2 + rows].reshape(rows * cols, depth), w2_ref[2])
            own = pltpu.roll(tile[j].astype(F32), width - 4, 1)[:, :cols]
            out_ref[j] = (own + acc.reshape(rows, cols, 128)).astype(BF)
            return carry

        lax.fori_loop(0, 2, piece, 0)


def sum_kernel(parts_ref, out_ref):
    total = jnp.sum(parts_ref[...].astype(F32), axis=0)
    out_ref[...] = jnp.broadcast_to(total[None], out_ref.shape).astype(out_ref.dtype)


def finish_kernel(scale, full_ref, in_ref, out_ref, pool_ref):
    start = 0
    for ref in (in_ref, out_ref, pool_ref):
        size = ref.shape[0]
        ref[...] = full_ref[start : start + size].astype(F32) * scale
        start += size


def block(ensemble, cotangent, conv_in, pool_weight, conv_out):
    mem_local, _, rows, lon = ensemble.shape
    groups = lax.axis_size(MEMBER)
    bands = lax.axis_size(LAT)
    channels = conv_in.shape[-1]
    cols = lon // groups
    width = (cols + 4) * mem_local
    vspec = pl.BlockSpec(memory_space=pltpu.VMEM)
    sspec = pl.BlockSpec(memory_space=pltpu.SMEM)
    vm = pltpu.VMEM
    me = lax.axis_index(MEMBER).astype(jnp.int32).reshape(1)
    chips = groups // 2
    keep, give = pl.pallas_call(
        pack_kernel,
        out_shape=[vm((chips, rows, width, 128), BF)] * 2,
        in_specs=[sspec, vspec, vspec],
        out_specs=[vspec] * 2,
        scratch_shapes=[vm((rows, 2 * lon + 8, 128), F32)],
        name="pack",
    )(me, ensemble, cotangent)
    got = swap(give, 0, 1, groups)
    tiles = pl.pallas_call(
        pair_kernel,
        out_shape=[vm((2, rows, width, 128), BF)] * chips,
        in_specs=[vspec] * 2,
        out_specs=[vspec] * chips,
        name="pair",
    )(*near(keep, got))
    tiles = [tiles[0]] + [swap(tiles[i], ORDER[i], 0, groups) for i in range(1, chips)]
    head, tail = pl.pallas_call(
        edges_kernel,
        out_shape=[vm((groups, 2, width, 128), BF)] * 2,
        in_specs=[vspec] * chips,
        out_specs=[vspec] * 2,
        name="edges",
    )(*near(*tiles))
    top = lax.ppermute(tail, LAT, [(i, i + 1) for i in range(bands - 1)])
    bot = lax.ppermute(head, LAT, [(i + 1, i) for i in range(bands - 1)])

    flip_in = jnp.transpose(conv_in[::-1, ::-1], (0, 1, 3, 2))
    flip_out = jnp.transpose(conv_out[::-1, ::-1], (0, 1, 3, 2))
    z1 = jnp.zeros_like(conv_in)
    z2 = jnp.zeros_like(conv_out)
    w1 = jnp.concatenate(
        [jnp.concatenate([conv_in, z1], axis=3), jnp.concatenate([z1, flip_out], axis=3)], axis=2
    ).reshape(1152, 256)
    w2 = jnp.concatenate(
        [
            jnp.concatenate([conv_out, z2], axis=3).reshape(3, 384, 128),
            jnp.concatenate([z2, flip_in], axis=3).reshape(3, 384, 128),
        ],
        axis=1,
    )
    lat = jnp.stack([lax.axis_index(LAT), jnp.int32(bands * rows)]).astype(jnp.int32)
    inner = rows + 2
    plane = (inner, WIDE, channels)
    used = 18 * (channels // 2) + 2 * channels
    slices, copies = lax.axis_size(PLANE), lax.axis_size(REST)
    per = -(-used // (8 * slices)) * 8
    shifted = (groups, inner, cols * mem_local, 384)
    compact = pltpu.HBM((groups, inner, width, channels), BF)
    hspec = pl.BlockSpec(memory_space=pltpu.HBM)
    grads, hid, dpre = pl.pallas_call(
        tile_kernel,
        out_shape=[vm((slices * per, channels), BF), compact, compact],
        in_specs=[sspec] + [vspec] * (chips + 4) + [hspec],
        out_specs=[vspec, hspec, hspec],
        scratch_shapes=[
            vm((groups, rows, width, 128), BF),
            vm((groups,) + plane, F32),
            vm((groups,) + plane, F32),
            vm((groups,) + plane, F32),
            vm(shifted[:3] + (192,), BF),
            vm((groups, rows, cols * mem_local, 128), BF),
            vm(shifted, BF),
            vm((groups, rows, cols * mem_local, channels), BF),
            vm(compact.shape, BF),
            vm(compact.shape, BF),
            vm(plane, F32),
            vm(plane, F32),
            vm(plane, F32),
            vm(plane, F32),
            vm(plane, F32),
            pltpu.SemaphoreType.DMA((2,)),
        ],
        compiler_params=pltpu.CompilerParams(vmem_limit_bytes=48 * 1024 * 1024),
        name="tile",
    )(lat, *near(*tiles, top, bot, w1, pool_weight), w2)
    pieces = list(pl.pallas_call(
        output_kernel,
        out_shape=[vm((2, rows, cols * mem_local, 128), BF)] * chips,
        in_specs=[vspec] * (chips + 3),
        out_specs=[vspec] * chips,
        name="output",
    )(*near(*tiles), hid, dpre, w2))

    def exchange(value, axis):
        return lax.all_to_all(value, axis, split_axis=0, concat_axis=0, tiled=True)

    def add_up(parts, count):
        return pl.pallas_call(
            sum_kernel,
            out_shape=vm((count,) + parts.shape[1:], BF),
            in_specs=[vspec],
            out_specs=vspec,
            name="total",
        )(*near(parts))

    parts = exchange(grads.reshape(slices, per, channels), PLANE)
    far = swap(pieces[3], chips - ORDER[3], 0, groups)
    parts, pieces[1], pieces[2] = lax.optimization_barrier((parts, pieces[1], pieces[2]))
    pieces[1:3] = [swap(piece, chips - d, 0, groups) for d, piece in zip(ORDER[1:3], pieces[1:3])]
    pieces[3] = far
    parts = add_up(parts, copies)
    parts = exchange(parts, REST)
    parts = add_up(parts, slices)
    other = pl.pallas_call(
        other_kernel,
        out_shape=vm((chips, rows, cols * mem_local, 128), BF),
        in_specs=[vspec] * chips,
        out_specs=vspec,
        name="other",
    )(*near(*pieces))
    theirs = swap(other, 0, 1, groups)
    full = exchange(parts, PLANE).reshape(slices * per, channels)
    members = mem_local * groups
    scale = 1.0 / math.sqrt(members * bands * rows * lon)
    half = channels // 2
    grad_in, grad_out, grad_pool = pl.pallas_call(
        functools.partial(finish_kernel, scale),
        out_shape=[jax.ShapeDtypeStruct((n, channels), F32) for n in (9 * half, 9 * half, 2 * channels)],
        in_specs=[vspec],
        out_specs=[vspec] * 3,
        name="finish",
    )(*near(full))
    grad_in = grad_in.reshape(3, 3, half, channels)
    grad_out = grad_out.reshape(3, 3, half, channels).transpose(0, 1, 3, 2)

    encoded, d_input = pl.pallas_call(
        unpack_kernel,
        out_shape=[jax.ShapeDtypeStruct(ensemble.shape, BF)] * 2,
        in_specs=[sspec] + [vspec] * (chips + 1),
        out_specs=[vspec] * 2,
        scratch_shapes=[vm((rows, 2 * lon, 128), F32)],
        name="unpack",
    )(me, *near(*pieces, theirs))
    return encoded, d_input, grad_in, grad_pool, grad_out


def solution(mesh):
    groups, bands = mesh.devices.shape
    lat = (4, 2, 4) if bands == 32 else (1, bands, 1)
    fine = Mesh(mesh.devices.reshape((groups // 2, 2) + lat), MEMBER + LAT)
    fields = P(MEMBER, None, LAT, None)
    return jax.shard_map(
        block,
        mesh=fine,
        in_specs=(fields, fields, P(), P(), P()),
        out_specs=(fields, fields, P(), P(), P()),
        check_vma=False,
    )
```

```python
import functools
import math

import jax
import jax.numpy as jnp
from jax import lax
from jax.experimental import pallas as pl
from jax.experimental.pallas import tpu as pltpu
from jax.sharding import Mesh
from jax.sharding import PartitionSpec as P


BF = jnp.bfloat16
F32 = jnp.float32
WIDE = 80


MEMBER = ("zh", "core")
LAT = ("y", "zl", "x")
PLANE = ("y", "x")
REST = ("zh", "core", "zl")
ORDER = (0, 1, 3, 2)


def swap(value, steps, cross, groups):
    chips = groups // 2
    pairs = [
        (2 * z + c, 2 * ((z + steps) % chips) + (c + cross) % 2) for z in range(chips) for c in range(2)
    ]
    return lax.ppermute(value, MEMBER, pairs)


def column_block(device, steps, cross, groups):
    chips = groups // 2
    return 2 * lax.rem(device // 2 + steps, chips) + lax.rem(device + cross, 2)


def near(*values):
    return [pltpu.with_memory_space_constraint(v, pltpu.VMEM) for v in values]


def sigmoid(v):
    return 1.0 / (1.0 + jnp.exp(-v))


def split3(v):
    a = v.astype(BF)
    r = v - a.astype(F32)
    b = r.astype(BF)
    c = (r - b.astype(F32)).astype(BF)
    return a, b, c


def dot(a, b):
    return jnp.dot(a, b, preferred_element_type=F32)


def dot_t(a, b, dims):
    return lax.dot_general(a, b, (dims, ((), ())), preferred_element_type=F32)


def dot_rows(a, b):
    return dot_t(a, b, ((0,), (0,)))


def pack_kernel(me_ref, ens_ref, cot_ref, keep_ref, give_ref, plane):
    chips, _, width, _ = keep_ref.shape
    mem_local, _, rows, lon = ens_ref.shape
    for m in range(mem_local):
        for r in range(rows):
            both = jnp.concatenate([ens_ref[m, :, r, :], cot_ref[m, :, r, :]], axis=0).astype(F32).T
            plane[r, pl.ds(4 + m, lon, stride=2), :] = both
            plane[r, pl.ds(m, 2, stride=2), :] = both[lon - 2 :]
            plane[r, pl.ds(4 + 2 * lon + m, 2, stride=2), :] = both[:2]
    for d in range(chips):
        for cross, ref in enumerate((keep_ref, give_ref)):
            k = column_block(me_ref[0], ORDER[d], cross, 2 * chips)
            for r in range(rows):
                ref[d, r] = plane[r, pl.ds(pl.multiple_of(k * (width - 8), 8), width), :].astype(BF)


def pair_kernel(keep_ref, got_ref, *out_refs):
    last = keep_ref.shape[0] - 1
    for d, ref in enumerate(out_refs[:last]):
        ref[0] = keep_ref[d]
        ref[1] = got_ref[d]
    out_refs[last][0] = keep_ref[last]
    out_refs[last + 1][0] = got_ref[last]


def edges_kernel(*refs):
    tiles, (head_ref, tail_ref) = refs[:-2], refs[-2:]
    rows = tiles[0].shape[1]
    at = 0
    for tile in tiles:
        n = tile.shape[0]
        head_ref[at : at + n] = tile[:, :2]
        tail_ref[at : at + n] = tile[:, rows - 2 :]
        at += n


def other_kernel(*refs):
    for d, tile in enumerate(refs[:-1]):
        refs[-1][d] = tile[tile.shape[0] - 1]


def unpack_kernel(me_ref, *refs):
    tiles, (theirs_ref, enc_ref, din_ref, plane) = refs[:-4], refs[-4:]
    chips = len(tiles)
    mem_local, half, rows, lon = enc_ref.shape
    width = theirs_ref.shape[2]
    for d in range(chips):
        for cross in range(2):
            k = column_block(me_ref[0], ORDER[d], cross, 2 * chips)
            for r in range(rows):
                piece = theirs_ref[d, r] if cross else tiles[d][0, r]
                plane[r, pl.ds(pl.multiple_of(k * width, 8), width), :] = piece.astype(F32)
    for m in range(mem_local):
        for r in range(rows):
            both = plane[r, pl.ds(m, lon, stride=2), :].T.astype(BF)
            enc_ref[m, :, r, :] = both[:half]
            din_ref[m, :, r, :] = both[half:]


def tile_kernel(
    lat_ref, t0, t1, t2, t3, t4, top_ref, bot_ref, w1_ref, pool_ref, _,
    grads_ref, hid_ref, dpre_ref,
    own_ref, pre_s, dh_s, act_s, xo_s, oc_s, hq_s, dpo_s, hid_s, dpre_s, sum_s, var_s, shared_s, ca_s, cs_s, sems,
):
    srcs, rows, width, _ = own_ref.shape
    inner = rows + 2
    cols = xo_s.shape[2]
    nlat = lat_ref[1]
    at = 0
    for tile in (t0, t1, t2, t3, t4):
        own_ref[at : at + tile.shape[0]] = tile[...]
        at += tile.shape[0]
    members = 2 * srcs
    channels = pre_s.shape[-1]
    shape = (inner, WIDE, channels)

    def up(v, n):
        return pltpu.roll(v, WIDE - n, 1) if n else v

    parity = lax.broadcasted_iota(jnp.int32, shape, 1) % 2

    def pair_sum(v):
        return v + jnp.where(parity == 0, up(v, 1), pltpu.roll(v, 1, 1))

    row_id = lax.broadcasted_iota(jnp.int32, shape, 0) + lat_ref[0] * rows - 1
    inside = jnp.logical_and(row_id >= 0, row_id < nlat)

    sum_s[...] = jnp.zeros(shape, F32)

    def first(s, carry):
        x = jnp.concatenate([top_ref[s], own_ref[s], bot_ref[s]], axis=0).astype(F32)
        x = jnp.concatenate([x, jnp.zeros((rows + 4, WIDE - width, 128), F32)], axis=1)
        x1, x2, x3 = up(x, 2), up(x, 4), up(x, 6)
        xs = jnp.concatenate([x, x1, x2], axis=-1).astype(BF)
        own = [v[1 : 1 + inner, :cols] for v in (x1, x2, x3)]
        half = channels // 2
        xo_s[s] = jnp.concatenate([v[..., :half] for v in own], axis=-1).astype(BF)
        oc_s[s] = own[1][1 : 1 + rows].astype(BF)
        xs = jnp.concatenate([xs[p : p + inner] for p in range(3)], axis=-1)
        acc = dot(xs.reshape(inner * WIDE, 1152), w1_ref[...])
        pre = acc[:, :channels].reshape(shape)
        pre_s[s] = pre
        dh_s[s] = acc[:, channels:].reshape(shape)
        act = (pre * sigmoid(pre)).astype(BF).astype(F32)
        act_s[s] = act
        sum_s[...] += act
        return carry

    lax.fori_loop(0, srcs, first, 0)
    average = pair_sum(sum_s[...]) * (1.0 / members)
    sum_s[...] = average
    var_s[...] = jnp.zeros(shape, F32)

    def second(s, carry):
        d = act_s[s] - sum_s[...]
        var_s[...] += d * d
        return carry

    lax.fori_loop(0, srcs, second, 0)
    spread = jnp.sqrt(pair_sum(var_s[...]) * (1.0 / members) + 0.1)
    var_s[...] = spread
    stats = jnp.concatenate([sum_s[...], spread], axis=-1).reshape(inner * WIDE, 2 * channels)
    s1, s2, s3 = split3(stats)
    pool = pool_ref[...]
    shared_s[...] = (dot(s1, pool) + dot(s2, pool) + dot(s3, pool)).reshape(shape)
    ca_s[...] = jnp.zeros(shape, F32)

    def third(s, carry):
        zed = act_s[s] + shared_s[...]
        sig = sigmoid(zed)
        hid = jnp.where(inside, (zed * sig).astype(BF).astype(F32), 0.0)
        dz = (dh_s[s] * (sig * (1.0 + zed * (1.0 - sig)))).astype(BF).astype(F32)
        dh_s[s] = dz
        ca_s[...] += dz
        hid_s[s] = hid[:, :width].astype(BF)
        hq_s[s] = jnp.concatenate([up(hid, 2 * q)[:, :cols] for q in range(3)], axis=-1).astype(BF)
        return carry

    lax.fori_loop(0, srcs, third, 0)
    hid_copy = pltpu.make_async_copy(hid_s, hid_ref, sems.at[0])
    hid_copy.start()
    d_shared = pair_sum(ca_s[...])
    d1, d2, d3 = split3(d_shared.reshape(inner * WIDE, channels))
    last = ((1,), (1,))
    d_stats = dot_t(d1, pool, last) + dot_t(d2, pool, last) + dot_t(d3, pool, last)
    ca_s[...] = (d_stats[:, :channels] * (1.0 / members)).reshape(shape)
    cs_s[...] = d_stats[:, channels:].reshape(shape) / (members * var_s[...])
    r_id = lax.broadcasted_iota(jnp.int32, shape, 0)
    c_id = lax.broadcasted_iota(jnp.int32, shape, 1)
    mine = (r_id >= 1) & (r_id <= rows) & (c_id >= 2) & (c_id < 2 + cols) & (parity == 0)
    e1, e2, e3 = split3(jnp.where(mine, d_shared, 0.0).reshape(inner * WIDE, channels))
    g_pool = dot_rows(s1, e1) + dot_rows(s1, e2) + dot_rows(s2, e1) + dot_rows(s2, e2) + dot_rows(s1, e3) + dot_rows(s3, e1)

    def fourth(s, carry):
        pre = pre_s[s]
        sig = sigmoid(pre)
        d_act = dh_s[s] + ca_s[...] + cs_s[...] * (act_s[s] - sum_s[...])
        dp = jnp.where(inside, d_act * (sig * (1.0 + pre * (1.0 - sig))), 0.0).astype(BF).astype(F32)
        dpre_s[s] = dp[:, :width].astype(BF)
        dpo_s[s] = up(dp, 2)[1 : 1 + rows, :cols].astype(BF)
        return carry

    lax.fori_loop(0, srcs, fourth, 0)
    dpre_copy = pltpu.make_async_copy(dpre_s, dpre_ref, sems.at[1])
    dpre_copy.start()

    total = srcs * rows * cols
    dpo = dpo_s[...].reshape(total, channels)
    own = oc_s[...].reshape(total, 128)
    half = channels // 2
    taps = 3 * half
    for p in range(3):
        g_in = dot_rows(dpo, xo_s[:, p : p + rows].reshape(total, taps))
        grads_ref[p * taps : (p + 1) * taps, :] = g_in.T.astype(BF)
    hqs = jnp.concatenate([hq_s[:, p : p + rows].reshape(total, 384) for p in range(3)], axis=-1)
    g_out = dot_rows(own, hqs)
    for t in range(9):
        grads_ref[(9 + t) * half : (10 + t) * half, :] = g_out[half:, t * 128 : (t + 1) * 128].astype(BF)
    used = 18 * half + 2 * channels
    grads_ref[18 * half : used, :] = g_pool.astype(BF)
    if used < grads_ref.shape[0]:
        grads_ref[used:, :] = jnp.zeros((grads_ref.shape[0] - used, 128), BF)
    hid_copy.wait()
    dpre_copy.wait()


def output_kernel(t0, t1, t2, t3, t4, hid_ref, dpre_ref, w2_ref, *out_refs):
    _, inner, width, _ = hid_ref.shape
    rows = inner - 2
    cols = out_refs[0].shape[2]

    def shifts(ref, s):
        v = ref[s].astype(F32)
        return [(pltpu.roll(v, width - 2 * q, 1) if q else v)[:, :cols] for q in range(3)]

    def piece(at, tile, out_ref, j, carry):
        both = jnp.concatenate(shifts(hid_ref, at + j) + shifts(dpre_ref, at + j), axis=-1).astype(BF)
        depth = both.shape[-1]
        acc = dot(both[0:rows].reshape(rows * cols, depth), w2_ref[0])
        acc += dot(both[1 : 1 + rows].reshape(rows * cols, depth), w2_ref[1])
        acc += dot(both[2 : 2 + rows].reshape(rows * cols, depth), w2_ref[2])
        own = pltpu.roll(tile[j].astype(F32), width - 4, 1)[:, :cols]
        out_ref[j] = (own + acc.reshape(rows, cols, 128)).astype(BF)
        return carry

    at = 0
    for tile, out_ref in zip((t0, t1, t2, t3, t4), out_refs):
        lax.fori_loop(0, tile.shape[0], functools.partial(piece, at, tile, out_ref), 0)
        at += tile.shape[0]


def sum_kernel(parts_ref, out_ref):
    total = jnp.sum(parts_ref[...].astype(F32), axis=0)
    out_ref[...] = jnp.broadcast_to(total[None], out_ref.shape).astype(out_ref.dtype)


def finish_kernel(scale, full_ref, in_ref, out_ref, pool_ref):
    start = 0
    for ref in (in_ref, out_ref, pool_ref):
        size = ref.shape[0]
        ref[...] = full_ref[start : start + size].astype(F32) * scale
        start += size


def block(ensemble, cotangent, conv_in, pool_weight, conv_out):
    mem_local, _, rows, lon = ensemble.shape
    groups = lax.axis_size(MEMBER)
    bands = lax.axis_size(LAT)
    channels = conv_in.shape[-1]
    cols = lon // groups
    width = (cols + 4) * mem_local
    vspec = pl.BlockSpec(memory_space=pltpu.VMEM)
    sspec = pl.BlockSpec(memory_space=pltpu.SMEM)
    vm = pltpu.VMEM
    me = lax.axis_index(MEMBER).astype(jnp.int32).reshape(1)
    chips = groups // 2
    keep, give = pl.pallas_call(
        pack_kernel,
        out_shape=[vm((chips, rows, width, 128), BF)] * 2,
        in_specs=[sspec, vspec, vspec],
        out_specs=[vspec] * 2,
        scratch_shapes=[vm((rows, 2 * lon + 8, 128), F32)],
        name="pack",
    )(me, ensemble, cotangent)
    got = swap(give, 0, 1, groups)
    sizes = [2] * (chips - 1) + [1, 1]
    tiles = pl.pallas_call(
        pair_kernel,
        out_shape=[vm((n, rows, width, 128), BF) for n in sizes],
        in_specs=[vspec] * 2,
        out_specs=[vspec] * len(sizes),
        name="pair",
    )(*near(keep, got))
    back = chips - 1
    relay = swap(tiles[4], back, 0, groups)
    far = swap(tiles[3], 2, 0, groups)
    beside = [swap(tiles[i], ORDER[i], 0, groups) for i in (2, 1)]
    relay = swap(relay, back, 0, groups)
    tiles = [tiles[0], beside[1], beside[0], far, relay]
    head, tail = pl.pallas_call(
        edges_kernel,
        out_shape=[vm((groups, 2, width, 128), BF)] * 2,
        in_specs=[vspec] * len(sizes),
        out_specs=[vspec] * 2,
        name="edges",
    )(*near(*tiles))
    top = lax.ppermute(tail, LAT, [(i, i + 1) for i in range(bands - 1)])
    bot = lax.ppermute(head, LAT, [(i + 1, i) for i in range(bands - 1)])

    flip_in = jnp.transpose(conv_in[::-1, ::-1], (0, 1, 3, 2))
    flip_out = jnp.transpose(conv_out[::-1, ::-1], (0, 1, 3, 2))
    z1 = jnp.zeros_like(conv_in)
    z2 = jnp.zeros_like(conv_out)
    w1 = jnp.concatenate(
        [jnp.concatenate([conv_in, z1], axis=3), jnp.concatenate([z1, flip_out], axis=3)], axis=2
    ).reshape(1152, 256)
    w2 = jnp.concatenate(
        [
            jnp.concatenate([conv_out, z2], axis=3).reshape(3, 384, 128),
            jnp.concatenate([z2, flip_in], axis=3).reshape(3, 384, 128),
        ],
        axis=1,
    )
    lat = jnp.stack([lax.axis_index(LAT), jnp.int32(bands * rows)]).astype(jnp.int32)
    inner = rows + 2
    plane = (inner, WIDE, channels)
    used = 18 * (channels // 2) + 2 * channels
    slices, copies = lax.axis_size(PLANE), lax.axis_size(REST)
    per = -(-used // (8 * slices)) * 8
    shifted = (groups, inner, cols * mem_local, 384)
    compact = pltpu.HBM((groups, inner, width, channels), BF)
    hspec = pl.BlockSpec(memory_space=pltpu.HBM)
    grads, hid, dpre = pl.pallas_call(
        tile_kernel,
        out_shape=[vm((slices * per, channels), BF), compact, compact],
        in_specs=[sspec] + [vspec] * (len(sizes) + 4) + [hspec],
        out_specs=[vspec, hspec, hspec],
        scratch_shapes=[
            vm((groups, rows, width, 128), BF),
            vm((groups,) + plane, F32),
            vm((groups,) + plane, F32),
            vm((groups,) + plane, F32),
            vm(shifted[:3] + (192,), BF),
            vm((groups, rows, cols * mem_local, 128), BF),
            vm(shifted, BF),
            vm((groups, rows, cols * mem_local, channels), BF),
            vm(compact.shape, BF),
            vm(compact.shape, BF),
            vm(plane, F32),
            vm(plane, F32),
            vm(plane, F32),
            vm(plane, F32),
            vm(plane, F32),
            pltpu.SemaphoreType.DMA((2,)),
        ],
        compiler_params=pltpu.CompilerParams(vmem_limit_bytes=48 * 1024 * 1024),
        name="tile",
    )(lat, *near(*tiles, top, bot, w1, pool_weight), w2)
    pieces = list(pl.pallas_call(
        output_kernel,
        out_shape=[vm((n, rows, cols * mem_local, 128), BF) for n in sizes],
        in_specs=[vspec] * (len(sizes) + 3),
        out_specs=[vspec] * len(sizes),
        name="output",
    )(*near(*tiles), hid, dpre, w2))

    def exchange(value, axis):
        return lax.all_to_all(value, axis, split_axis=0, concat_axis=0, tiled=True)

    def add_up(parts, count):
        return pl.pallas_call(
            sum_kernel,
            out_shape=vm((count,) + parts.shape[1:], BF),
            in_specs=[vspec],
            out_specs=vspec,
            name="total",
        )(*near(parts))

    parts = exchange(grads.reshape(slices, per, channels), PLANE)
    relay = swap(pieces[4], back, 0, groups)
    far = swap(pieces[3], 2, 0, groups)
    parts, pieces[1], pieces[2] = lax.optimization_barrier((parts, pieces[1], pieces[2]))
    beside = [swap(pieces[i], chips - ORDER[i], 0, groups) for i in (1, 2)]
    relay = swap(relay, back, 0, groups)
    pieces = [pieces[0], *beside, far]
    parts = add_up(parts, copies)
    parts = exchange(parts, REST)
    parts = add_up(parts, slices)
    other = pl.pallas_call(
        other_kernel,
        out_shape=vm((chips, rows, cols * mem_local, 128), BF),
        in_specs=[vspec] * chips,
        out_specs=vspec,
        name="other",
    )(*near(*pieces[:3], relay))
    theirs = swap(other, 0, 1, groups)
    full = exchange(parts, PLANE).reshape(slices * per, channels)
    members = mem_local * groups
    scale = 1.0 / math.sqrt(members * bands * rows * lon)
    half = channels // 2
    grad_in, grad_out, grad_pool = pl.pallas_call(
        functools.partial(finish_kernel, scale),
        out_shape=[jax.ShapeDtypeStruct((n, channels), F32) for n in (9 * half, 9 * half, 2 * channels)],
        in_specs=[vspec],
        out_specs=[vspec] * 3,
        name="finish",
    )(*near(full))
    grad_in = grad_in.reshape(3, 3, half, channels)
    grad_out = grad_out.reshape(3, 3, half, channels).transpose(0, 1, 3, 2)

    encoded, d_input = pl.pallas_call(
        unpack_kernel,
        out_shape=[jax.ShapeDtypeStruct(ensemble.shape, BF)] * 2,
        in_specs=[sspec] + [vspec] * (chips + 1),
        out_specs=[vspec] * 2,
        scratch_shapes=[vm((rows, 2 * lon, 128), F32)],
        name="unpack",
    )(me, *near(*pieces, theirs))
    return encoded, d_input, grad_in, grad_pool, grad_out


def solution(mesh):
    groups, bands = mesh.devices.shape
    lat = (4, 2, 4) if bands == 32 else (1, bands, 1)
    fine = Mesh(mesh.devices.reshape((groups // 2, 2) + lat), MEMBER + LAT)
    fields = P(MEMBER, None, LAT, None)
    return jax.shard_map(
        block,
        mesh=fine,
        in_specs=(fields, fields, P(), P(), P()),
        out_specs=(fields, fields, P(), P(), P()),
        check_vma=False,
    )
```

```python
import functools
import math

import jax
import jax.numpy as jnp
from jax import lax
from jax.experimental import pallas as pl
from jax.experimental.pallas import tpu as pltpu
from jax.sharding import Mesh
from jax.sharding import PartitionSpec as P


BF = jnp.bfloat16
F32 = jnp.float32
WIDE = 80


MEMBER = ("zh", "core")
LAT = ("y", "zl", "x")
LINE = ("zh", "core", "zl")
REST = ("y", "x")
ORDER = (0, 1, 3, 2)


def swap(value, steps, cross, groups):
    chips = groups // 2
    pairs = [
        (2 * z + c, 2 * ((z + steps) % chips) + (c + cross) % 2) for z in range(chips) for c in range(2)
    ]
    return lax.ppermute(value, MEMBER, pairs)


def column_block(device, steps, cross, groups):
    chips = groups // 2
    return 2 * lax.rem(device // 2 + steps, chips) + lax.rem(device + cross, 2)


def near(*values):
    return [pltpu.with_memory_space_constraint(v, pltpu.VMEM) for v in values]


def sigmoid(v):
    return 1.0 / (1.0 + jnp.exp(-v))


def split3(v):
    a = v.astype(BF)
    r = v - a.astype(F32)
    b = r.astype(BF)
    c = (r - b.astype(F32)).astype(BF)
    return a, b, c


def dot(a, b):
    return jnp.dot(a, b, preferred_element_type=F32)


def dot_t(a, b, dims):
    return lax.dot_general(a, b, (dims, ((), ())), preferred_element_type=F32)


def dot_rows(a, b):
    return dot_t(a, b, ((0,), (0,)))


def pack_kernel(me_ref, ens_ref, cot_ref, keep_ref, give_ref, plane):
    chips, _, width, _ = keep_ref.shape
    mem_local, _, rows, lon = ens_ref.shape
    for m in range(mem_local):
        for r in range(rows):
            both = jnp.concatenate([ens_ref[m, :, r, :], cot_ref[m, :, r, :]], axis=0).astype(F32).T
            plane[r, pl.ds(4 + m, lon, stride=2), :] = both
            plane[r, pl.ds(m, 2, stride=2), :] = both[lon - 2 :]
            plane[r, pl.ds(4 + 2 * lon + m, 2, stride=2), :] = both[:2]
    for d in range(chips):
        for cross, ref in enumerate((keep_ref, give_ref)):
            k = column_block(me_ref[0], ORDER[d], cross, 2 * chips)
            for r in range(rows):
                ref[d, r] = plane[r, pl.ds(pl.multiple_of(k * (width - 8), 8), width), :].astype(BF)


def pair_kernel(keep_ref, got_ref, *out_refs):
    for d, ref in enumerate(out_refs):
        ref[0] = keep_ref[d]
        ref[1] = got_ref[d]


def edges_kernel(*refs):
    tiles, (head_ref, tail_ref) = refs[:-2], refs[-2:]
    rows = tiles[0].shape[1]
    for d, tile in enumerate(tiles):
        head_ref[2 * d : 2 * d + 2] = tile[:, :2]
        tail_ref[2 * d : 2 * d + 2] = tile[:, rows - 2 :]


def other_kernel(*refs):
    for d, tile in enumerate(refs[:-1]):
        refs[-1][d] = tile[1]


def unpack_kernel(me_ref, *refs):
    tiles, (theirs_ref, enc_ref, din_ref, plane) = refs[:-4], refs[-4:]
    chips = len(tiles)
    mem_local, half, rows, lon = enc_ref.shape
    width = theirs_ref.shape[2]
    for d in range(chips):
        for cross in range(2):
            k = column_block(me_ref[0], ORDER[d], cross, 2 * chips)
            for r in range(rows):
                piece = theirs_ref[d, r] if cross else tiles[d][0, r]
                plane[r, pl.ds(pl.multiple_of(k * width, 8), width), :] = piece.astype(F32)
    for m in range(mem_local):
        for r in range(rows):
            both = plane[r, pl.ds(m, lon, stride=2), :].T.astype(BF)
            enc_ref[m, :, r, :] = both[:half]
            din_ref[m, :, r, :] = both[half:]


def tile_kernel(
    lat_ref, t0, t1, t2, t3, top_ref, bot_ref, w1_ref, pool_ref, _,
    grads_ref, hid_ref, dpre_ref,
    own_ref, pre_s, dh_s, act_s, xo_s, oc_s, hq_s, dpo_s, hid_s, dpre_s, sum_s, var_s, shared_s, ca_s, cs_s, sems,
):
    srcs, rows, width, _ = own_ref.shape
    inner = rows + 2
    cols = xo_s.shape[2]
    nlat = lat_ref[1]
    for d, tile in enumerate((t0, t1, t2, t3)):
        own_ref[2 * d : 2 * d + 2] = tile[...]
    members = 2 * srcs
    channels = pre_s.shape[-1]
    shape = (inner, WIDE, channels)

    def up(v, n):
        return pltpu.roll(v, WIDE - n, 1) if n else v

    parity = lax.broadcasted_iota(jnp.int32, shape, 1) % 2

    def pair_sum(v):
        return v + jnp.where(parity == 0, up(v, 1), pltpu.roll(v, 1, 1))

    row_id = lax.broadcasted_iota(jnp.int32, shape, 0) + lat_ref[0] * rows - 1
    inside = jnp.logical_and(row_id >= 0, row_id < nlat)

    sum_s[...] = jnp.zeros(shape, F32)

    def first(s, carry):
        x = jnp.concatenate([top_ref[s], own_ref[s], bot_ref[s]], axis=0).astype(F32)
        x = jnp.concatenate([x, jnp.zeros((rows + 4, WIDE - width, 128), F32)], axis=1)
        x1, x2, x3 = up(x, 2), up(x, 4), up(x, 6)
        xs = jnp.concatenate([x, x1, x2], axis=-1).astype(BF)
        own = [v[1 : 1 + inner, :cols] for v in (x1, x2, x3)]
        half = channels // 2
        xo_s[s] = jnp.concatenate([v[..., :half] for v in own], axis=-1).astype(BF)
        oc_s[s] = own[1][1 : 1 + rows].astype(BF)
        xs = jnp.concatenate([xs[p : p + inner] for p in range(3)], axis=-1)
        acc = dot(xs.reshape(inner * WIDE, 1152), w1_ref[...])
        pre = acc[:, :channels].reshape(shape)
        pre_s[s] = pre
        dh_s[s] = acc[:, channels:].reshape(shape)
        act = (pre * sigmoid(pre)).astype(BF).astype(F32)
        act_s[s] = act
        sum_s[...] += act
        return carry

    lax.fori_loop(0, srcs, first, 0)
    average = pair_sum(sum_s[...]) * (1.0 / members)
    sum_s[...] = average
    var_s[...] = jnp.zeros(shape, F32)

    def second(s, carry):
        d = act_s[s] - sum_s[...]
        var_s[...] += d * d
        return carry

    lax.fori_loop(0, srcs, second, 0)
    spread = jnp.sqrt(pair_sum(var_s[...]) * (1.0 / members) + 0.1)
    var_s[...] = spread
    stats = jnp.concatenate([sum_s[...], spread], axis=-1).reshape(inner * WIDE, 2 * channels)
    s1, s2, s3 = split3(stats)
    pool = pool_ref[...]
    shared_s[...] = (dot(s1, pool) + dot(s2, pool) + dot(s3, pool)).reshape(shape)
    ca_s[...] = jnp.zeros(shape, F32)

    def third(s, carry):
        zed = act_s[s] + shared_s[...]
        sig = sigmoid(zed)
        hid = jnp.where(inside, (zed * sig).astype(BF).astype(F32), 0.0)
        dz = (dh_s[s] * (sig * (1.0 + zed * (1.0 - sig)))).astype(BF).astype(F32)
        dh_s[s] = dz
        ca_s[...] += dz
        hid_s[s] = hid[:, :width].astype(BF)
        hq_s[s] = jnp.concatenate([up(hid, 2 * q)[:, :cols] for q in range(3)], axis=-1).astype(BF)
        return carry

    lax.fori_loop(0, srcs, third, 0)
    hid_copy = pltpu.make_async_copy(hid_s, hid_ref, sems.at[0])
    hid_copy.start()
    d_shared = pair_sum(ca_s[...])
    d1, d2, d3 = split3(d_shared.reshape(inner * WIDE, channels))
    last = ((1,), (1,))
    d_stats = dot_t(d1, pool, last) + dot_t(d2, pool, last) + dot_t(d3, pool, last)
    ca_s[...] = (d_stats[:, :channels] * (1.0 / members)).reshape(shape)
    cs_s[...] = d_stats[:, channels:].reshape(shape) / (members * var_s[...])
    r_id = lax.broadcasted_iota(jnp.int32, shape, 0)
    c_id = lax.broadcasted_iota(jnp.int32, shape, 1)
    mine = (r_id >= 1) & (r_id <= rows) & (c_id >= 2) & (c_id < 2 + cols) & (parity == 0)
    e1, e2, e3 = split3(jnp.where(mine, d_shared, 0.0).reshape(inner * WIDE, channels))
    g_pool = dot_rows(s1, e1) + dot_rows(s1, e2) + dot_rows(s2, e1) + dot_rows(s2, e2) + dot_rows(s1, e3) + dot_rows(s3, e1)

    def fourth(s, carry):
        pre = pre_s[s]
        sig = sigmoid(pre)
        d_act = dh_s[s] + ca_s[...] + cs_s[...] * (act_s[s] - sum_s[...])
        dp = jnp.where(inside, d_act * (sig * (1.0 + pre * (1.0 - sig))), 0.0).astype(BF).astype(F32)
        dpre_s[s] = dp[:, :width].astype(BF)
        dpo_s[s] = up(dp, 2)[1 : 1 + rows, :cols].astype(BF)
        return carry

    lax.fori_loop(0, srcs, fourth, 0)
    dpre_copy = pltpu.make_async_copy(dpre_s, dpre_ref, sems.at[1])
    dpre_copy.start()

    total = srcs * rows * cols
    dpo = dpo_s[...].reshape(total, channels)
    own = oc_s[...].reshape(total, 128)
    half = channels // 2
    taps = 3 * half
    for p in range(3):
        g_in = dot_rows(dpo, xo_s[:, p : p + rows].reshape(total, taps))
        grads_ref[p * taps : (p + 1) * taps, :] = g_in.T.astype(BF)
    hqs = jnp.concatenate([hq_s[:, p : p + rows].reshape(total, 384) for p in range(3)], axis=-1)
    g_out = dot_rows(own, hqs)
    for t in range(9):
        grads_ref[(9 + t) * half : (10 + t) * half, :] = g_out[half:, t * 128 : (t + 1) * 128].astype(BF)
    used = 18 * half + 2 * channels
    grads_ref[18 * half : used, :] = g_pool.astype(BF)
    if used < grads_ref.shape[0]:
        grads_ref[used:, :] = jnp.zeros((grads_ref.shape[0] - used, 128), BF)
    hid_copy.wait()
    dpre_copy.wait()


def output_kernel(t0, t1, t2, t3, hid_ref, dpre_ref, w2_ref, *out_refs):
    _, inner, width, _ = hid_ref.shape
    rows = inner - 2
    cols = out_refs[0].shape[2]

    def shifts(ref, s):
        v = ref[s].astype(F32)
        return [(pltpu.roll(v, width - 2 * q, 1) if q else v)[:, :cols] for q in range(3)]

    for d, (tile, out_ref) in enumerate(zip((t0, t1, t2, t3), out_refs)):

        def piece(j, carry):
            both = jnp.concatenate(shifts(hid_ref, 2 * d + j) + shifts(dpre_ref, 2 * d + j), axis=-1).astype(BF)
            depth = both.shape[-1]
            acc = dot(both[0:rows].reshape(rows * cols, depth), w2_ref[0])
            acc += dot(both[1 : 1 + rows].reshape(rows * cols, depth), w2_ref[1])
            acc += dot(both[2 : 2 + rows].reshape(rows * cols, depth), w2_ref[2])
            own = pltpu.roll(tile[j].astype(F32), width - 4, 1)[:, :cols]
            out_ref[j] = (own + acc.reshape(rows, cols, 128)).astype(BF)
            return carry

        lax.fori_loop(0, 2, piece, 0)


def sum_kernel(parts_ref, out_ref):
    total = jnp.sum(parts_ref[...].astype(F32), axis=0)
    out_ref[...] = jnp.broadcast_to(total[None], out_ref.shape).astype(out_ref.dtype)


def finish_kernel(scale, full_ref, in_ref, out_ref, pool_ref):
    start = 0
    for ref in (in_ref, out_ref, pool_ref):
        size = ref.shape[0]
        ref[...] = full_ref[start : start + size].astype(F32) * scale
        start += size


def block(ensemble, cotangent, conv_in, pool_weight, conv_out):
    mem_local, _, rows, lon = ensemble.shape
    groups = lax.axis_size(MEMBER)
    bands = lax.axis_size(LAT)
    channels = conv_in.shape[-1]
    cols = lon // groups
    width = (cols + 4) * mem_local
    vspec = pl.BlockSpec(memory_space=pltpu.VMEM)
    sspec = pl.BlockSpec(memory_space=pltpu.SMEM)
    vm = pltpu.VMEM
    me = lax.axis_index(MEMBER).astype(jnp.int32).reshape(1)
    chips = groups // 2
    keep, give = pl.pallas_call(
        pack_kernel,
        out_shape=[vm((chips, rows, width, 128), BF)] * 2,
        in_specs=[sspec, vspec, vspec],
        out_specs=[vspec] * 2,
        scratch_shapes=[vm((rows, 2 * lon + 8, 128), F32)],
        name="pack",
    )(me, ensemble, cotangent)
    got = swap(give, 0, 1, groups)
    tiles = pl.pallas_call(
        pair_kernel,
        out_shape=[vm((2, rows, width, 128), BF)] * chips,
        in_specs=[vspec] * 2,
        out_specs=[vspec] * chips,
        name="pair",
    )(*near(keep, got))
    tiles = [tiles[0]] + [swap(tiles[i], ORDER[i], 0, groups) for i in range(1, chips)]
    head, tail = pl.pallas_call(
        edges_kernel,
        out_shape=[vm((groups, 2, width, 128), BF)] * 2,
        in_specs=[vspec] * chips,
        out_specs=[vspec] * 2,
        name="edges",
    )(*near(*tiles))
    top = lax.ppermute(tail, LAT, [(i, i + 1) for i in range(bands - 1)])
    bot = lax.ppermute(head, LAT, [(i + 1, i) for i in range(bands - 1)])

    flip_in = jnp.transpose(conv_in[::-1, ::-1], (0, 1, 3, 2))
    flip_out = jnp.transpose(conv_out[::-1, ::-1], (0, 1, 3, 2))
    z1 = jnp.zeros_like(conv_in)
    z2 = jnp.zeros_like(conv_out)
    w1 = jnp.concatenate(
        [jnp.concatenate([conv_in, z1], axis=3), jnp.concatenate([z1, flip_out], axis=3)], axis=2
    ).reshape(1152, 256)
    w2 = jnp.concatenate(
        [
            jnp.concatenate([conv_out, z2], axis=3).reshape(3, 384, 128),
            jnp.concatenate([z2, flip_in], axis=3).reshape(3, 384, 128),
        ],
        axis=1,
    )
    lat = jnp.stack([lax.axis_index(LAT), jnp.int32(bands * rows)]).astype(jnp.int32)
    inner = rows + 2
    plane = (inner, WIDE, channels)
    used = 18 * (channels // 2) + 2 * channels
    slices, copies = lax.axis_size(LINE), lax.axis_size(REST)
    per = -(-used // (8 * slices)) * 8
    shifted = (groups, inner, cols * mem_local, 384)
    compact = pltpu.HBM((groups, inner, width, channels), BF)
    hspec = pl.BlockSpec(memory_space=pltpu.HBM)
    grads, hid, dpre = pl.pallas_call(
        tile_kernel,
        out_shape=[vm((slices * per, channels), BF), compact, compact],
        in_specs=[sspec] + [vspec] * (chips + 4) + [hspec],
        out_specs=[vspec, hspec, hspec],
        scratch_shapes=[
            vm((groups, rows, width, 128), BF),
            vm((groups,) + plane, F32),
            vm((groups,) + plane, F32),
            vm((groups,) + plane, F32),
            vm(shifted[:3] + (192,), BF),
            vm((groups, rows, cols * mem_local, 128), BF),
            vm(shifted, BF),
            vm((groups, rows, cols * mem_local, channels), BF),
            vm(compact.shape, BF),
            vm(compact.shape, BF),
            vm(plane, F32),
            vm(plane, F32),
            vm(plane, F32),
            vm(plane, F32),
            vm(plane, F32),
            pltpu.SemaphoreType.DMA((2,)),
        ],
        compiler_params=pltpu.CompilerParams(vmem_limit_bytes=48 * 1024 * 1024),
        name="tile",
    )(lat, *near(*tiles, top, bot, w1, pool_weight), w2)
    pieces = list(pl.pallas_call(
        output_kernel,
        out_shape=[vm((2, rows, cols * mem_local, 128), BF)] * chips,
        in_specs=[vspec] * (chips + 3),
        out_specs=[vspec] * chips,
        name="output",
    )(*near(*tiles), hid, dpre, w2))

    def exchange(value, axis):
        return lax.all_to_all(value, axis, split_axis=0, concat_axis=0, tiled=True)

    def add_up(parts, count):
        return pl.pallas_call(
            sum_kernel,
            out_shape=vm((count,) + parts.shape[1:], BF),
            in_specs=[vspec],
            out_specs=vspec,
            name="total",
        )(*near(parts))

    parts = exchange(grads.reshape(slices, per, channels), LINE)
    far = swap(pieces[3], chips - ORDER[3], 0, groups)
    parts, pieces[1], pieces[2] = lax.optimization_barrier((parts, pieces[1], pieces[2]))
    pieces[1:3] = [swap(piece, chips - d, 0, groups) for d, piece in zip(ORDER[1:3], pieces[1:3])]
    pieces[3] = far
    parts = add_up(parts, copies)
    parts = exchange(parts, REST)
    parts = add_up(parts, slices)
    other = pl.pallas_call(
        other_kernel,
        out_shape=vm((chips, rows, cols * mem_local, 128), BF),
        in_specs=[vspec] * chips,
        out_specs=vspec,
        name="other",
    )(*near(*pieces))
    theirs = swap(other, 0, 1, groups)
    full = exchange(parts, LINE).reshape(slices * per, channels)
    members = mem_local * groups
    scale = 1.0 / math.sqrt(members * bands * rows * lon)
    half = channels // 2
    grad_in, grad_out, grad_pool = pl.pallas_call(
        functools.partial(finish_kernel, scale),
        out_shape=[jax.ShapeDtypeStruct((n, channels), F32) for n in (9 * half, 9 * half, 2 * channels)],
        in_specs=[vspec],
        out_specs=[vspec] * 3,
        name="finish",
    )(*near(full))
    grad_in = grad_in.reshape(3, 3, half, channels)
    grad_out = grad_out.reshape(3, 3, half, channels).transpose(0, 1, 3, 2)

    encoded, d_input = pl.pallas_call(
        unpack_kernel,
        out_shape=[jax.ShapeDtypeStruct(ensemble.shape, BF)] * 2,
        in_specs=[sspec] + [vspec] * (chips + 1),
        out_specs=[vspec] * 2,
        scratch_shapes=[vm((rows, 2 * lon, 128), F32)],
        name="unpack",
    )(me, *near(*pieces, theirs))
    return encoded, d_input, grad_in, grad_pool, grad_out


def solution(mesh):
    groups, bands = mesh.devices.shape
    lat = (4, 2, 4) if bands == 32 else (1, bands, 1)
    fine = Mesh(mesh.devices.reshape((groups // 2, 2) + lat), MEMBER + LAT)
    fields = P(MEMBER, None, LAT, None)
    return jax.shard_map(
        block,
        mesh=fine,
        in_specs=(fields, fields, P(), P(), P()),
        out_specs=(fields, fields, P(), P(), P()),
        check_vma=False,
    )
```

```python
import functools
import math

import jax
import jax.numpy as jnp
from jax import lax
from jax.experimental import pallas as pl
from jax.experimental.pallas import tpu as pltpu
from jax.sharding import Mesh
from jax.sharding import PartitionSpec as P


BF = jnp.bfloat16
F32 = jnp.float32
WIDE = 80


MEMBER = ("zh", "core")
LAT = ("y", "zl", "x")
PLANE = ("y", "x")
REST = ("zh", "core", "zl")
ORDER = (0, 1, 3, 2)


def swap(value, steps, cross, groups):
    chips = groups // 2
    pairs = [
        (2 * z + c, 2 * ((z + steps) % chips) + (c + cross) % 2) for z in range(chips) for c in range(2)
    ]
    return lax.ppermute(value, MEMBER, pairs)


def column_block(device, steps, cross, groups):
    chips = groups // 2
    return 2 * lax.rem(device // 2 + steps, chips) + lax.rem(device + cross, 2)


def near(*values):
    return [pltpu.with_memory_space_constraint(v, pltpu.VMEM) for v in values]


def sigmoid(v):
    return 1.0 / (1.0 + jnp.exp(-v))


def split3(v):
    a = v.astype(BF)
    r = v - a.astype(F32)
    b = r.astype(BF)
    c = (r - b.astype(F32)).astype(BF)
    return a, b, c


def dot(a, b):
    return jnp.dot(a, b, preferred_element_type=F32)


def dot_t(a, b, dims):
    return lax.dot_general(a, b, (dims, ((), ())), preferred_element_type=F32)


def dot_rows(a, b):
    return dot_t(a, b, ((0,), (0,)))


def pack_kernel(me_ref, ens_ref, cot_ref, keep_ref, give_ref, plane):
    chips, _, width, _ = keep_ref.shape
    mem_local, _, rows, lon = ens_ref.shape
    for m in range(mem_local):
        for r in range(rows):
            both = jnp.concatenate([ens_ref[m, :, r, :], cot_ref[m, :, r, :]], axis=0).astype(F32).T
            plane[r, pl.ds(4 + m, lon, stride=2), :] = both
            plane[r, pl.ds(m, 2, stride=2), :] = both[lon - 2 :]
            plane[r, pl.ds(4 + 2 * lon + m, 2, stride=2), :] = both[:2]
    for d in range(chips):
        for cross, ref in enumerate((keep_ref, give_ref)):
            k = column_block(me_ref[0], ORDER[d], cross, 2 * chips)
            for r in range(rows):
                ref[d, r] = plane[r, pl.ds(pl.multiple_of(k * (width - 8), 8), width), :].astype(BF)


def pair_kernel(keep_ref, got_ref, *out_refs):
    for d, ref in enumerate(out_refs):
        ref[0] = keep_ref[d]
        ref[1] = got_ref[d]


def edges_kernel(*refs):
    tiles, (head_ref, tail_ref) = refs[:-2], refs[-2:]
    rows = tiles[0].shape[1]
    for d, tile in enumerate(tiles):
        head_ref[2 * d : 2 * d + 2] = tile[:, :2]
        tail_ref[2 * d : 2 * d + 2] = tile[:, rows - 2 :]


def other_kernel(*refs):
    for d, tile in enumerate(refs[:-1]):
        refs[-1][d] = tile[1]


def unpack_kernel(me_ref, *refs):
    tiles, (theirs_ref, enc_ref, din_ref, plane) = refs[:-4], refs[-4:]
    chips = len(tiles)
    mem_local, half, rows, lon = enc_ref.shape
    width = theirs_ref.shape[2]
    for d in range(chips):
        for cross in range(2):
            k = column_block(me_ref[0], ORDER[d], cross, 2 * chips)
            for r in range(rows):
                piece = theirs_ref[d, r] if cross else tiles[d][0, r]
                plane[r, pl.ds(pl.multiple_of(k * width, 8), width), :] = piece.astype(F32)
    for m in range(mem_local):
        for r in range(rows):
            both = plane[r, pl.ds(m, lon, stride=2), :].T.astype(BF)
            enc_ref[m, :, r, :] = both[:half]
            din_ref[m, :, r, :] = both[half:]


def tile_kernel(
    lat_ref, t0, t1, t2, t3, top_ref, bot_ref, w1_ref, pool_ref, _,
    grads_ref, hid_far, dpre_far, hid_ref, dpre_ref,
    own_ref, pre_s, dh_s, act_s, xo_s, oc_s, hq_s, dpo_s, hid_s, dpre_s, sum_s, var_s, shared_s, ca_s, cs_s, sems,
):
    srcs, rows, width, _ = own_ref.shape
    inner = rows + 2
    cols = xo_s.shape[2]
    nlat = lat_ref[1]
    for d, tile in enumerate((t0, t1, t2, t3)):
        own_ref[2 * d : 2 * d + 2] = tile[...]
    members = 2 * srcs
    channels = pre_s.shape[-1]
    shape = (inner, WIDE, channels)

    def up(v, n):
        return pltpu.roll(v, WIDE - n, 1) if n else v

    parity = lax.broadcasted_iota(jnp.int32, shape, 1) % 2

    def pair_sum(v):
        return v + jnp.where(parity == 0, up(v, 1), pltpu.roll(v, 1, 1))

    row_id = lax.broadcasted_iota(jnp.int32, shape, 0) + lat_ref[0] * rows - 1
    inside = jnp.logical_and(row_id >= 0, row_id < nlat)

    sum_s[...] = jnp.zeros(shape, F32)

    def first(s, carry):
        x = jnp.concatenate([top_ref[s], own_ref[s], bot_ref[s]], axis=0).astype(F32)
        x = jnp.concatenate([x, jnp.zeros((rows + 4, WIDE - width, 128), F32)], axis=1)
        x1, x2, x3 = up(x, 2), up(x, 4), up(x, 6)
        xs = jnp.concatenate([x, x1, x2], axis=-1).astype(BF)
        own = [v[1 : 1 + inner, :cols] for v in (x1, x2, x3)]
        half = channels // 2
        xo_s[s] = jnp.concatenate([v[..., :half] for v in own], axis=-1).astype(BF)
        oc_s[s] = own[1][1 : 1 + rows].astype(BF)
        xs = jnp.concatenate([xs[p : p + inner] for p in range(3)], axis=-1)
        acc = dot(xs.reshape(inner * WIDE, 1152), w1_ref[...])
        pre = acc[:, :channels].reshape(shape)
        pre_s[s] = pre
        dh_s[s] = acc[:, channels:].reshape(shape)
        act = (pre * sigmoid(pre)).astype(BF).astype(F32)
        act_s[s] = act
        sum_s[...] += act
        return carry

    lax.fori_loop(0, srcs, first, 0)
    average = pair_sum(sum_s[...]) * (1.0 / members)
    sum_s[...] = average
    var_s[...] = jnp.zeros(shape, F32)

    def second(s, carry):
        d = act_s[s] - sum_s[...]
        var_s[...] += d * d
        return carry

    lax.fori_loop(0, srcs, second, 0)
    spread = jnp.sqrt(pair_sum(var_s[...]) * (1.0 / members) + 0.1)
    var_s[...] = spread
    stats = jnp.concatenate([sum_s[...], spread], axis=-1).reshape(inner * WIDE, 2 * channels)
    s1, s2, s3 = split3(stats)
    pool = pool_ref[...]
    shared_s[...] = (dot(s1, pool) + dot(s2, pool) + dot(s3, pool)).reshape(shape)
    ca_s[...] = jnp.zeros(shape, F32)

    def third(s, carry):
        zed = act_s[s] + shared_s[...]
        sig = sigmoid(zed)
        hid = jnp.where(inside, (zed * sig).astype(BF).astype(F32), 0.0)
        dz = (dh_s[s] * (sig * (1.0 + zed * (1.0 - sig)))).astype(BF).astype(F32)
        dh_s[s] = dz
        ca_s[...] += dz
        hid_s[s] = hid[:, :width].astype(BF)
        hq_s[s] = jnp.concatenate([up(hid, 2 * q)[:, :cols] for q in range(3)], axis=-1).astype(BF)
        return carry

    lax.fori_loop(0, srcs, third, 0)
    first = hid_ref.shape[0]
    hid_far[...] = hid_s[first:]
    hid_copy = pltpu.make_async_copy(hid_s.at[pl.ds(0, first)], hid_ref, sems.at[0])
    hid_copy.start()
    d_shared = pair_sum(ca_s[...])
    d1, d2, d3 = split3(d_shared.reshape(inner * WIDE, channels))
    last = ((1,), (1,))
    d_stats = dot_t(d1, pool, last) + dot_t(d2, pool, last) + dot_t(d3, pool, last)
    ca_s[...] = (d_stats[:, :channels] * (1.0 / members)).reshape(shape)
    cs_s[...] = d_stats[:, channels:].reshape(shape) / (members * var_s[...])
    r_id = lax.broadcasted_iota(jnp.int32, shape, 0)
    c_id = lax.broadcasted_iota(jnp.int32, shape, 1)
    mine = (r_id >= 1) & (r_id <= rows) & (c_id >= 2) & (c_id < 2 + cols) & (parity == 0)
    e1, e2, e3 = split3(jnp.where(mine, d_shared, 0.0).reshape(inner * WIDE, channels))
    g_pool = dot_rows(s1, e1) + dot_rows(s1, e2) + dot_rows(s2, e1) + dot_rows(s2, e2) + dot_rows(s1, e3) + dot_rows(s3, e1)

    def fourth(s, carry):
        pre = pre_s[s]
        sig = sigmoid(pre)
        d_act = dh_s[s] + ca_s[...] + cs_s[...] * (act_s[s] - sum_s[...])
        dp = jnp.where(inside, d_act * (sig * (1.0 + pre * (1.0 - sig))), 0.0).astype(BF).astype(F32)
        dpre_s[s] = dp[:, :width].astype(BF)
        dpo_s[s] = up(dp, 2)[1 : 1 + rows, :cols].astype(BF)
        return carry

    lax.fori_loop(0, srcs, fourth, 0)
    dpre_far[...] = dpre_s[first:]
    dpre_copy = pltpu.make_async_copy(dpre_s.at[pl.ds(0, first)], dpre_ref, sems.at[1])
    dpre_copy.start()

    total = srcs * rows * cols
    dpo = dpo_s[...].reshape(total, channels)
    own = oc_s[...].reshape(total, 128)
    half = channels // 2
    taps = 3 * half
    for p in range(3):
        g_in = dot_rows(dpo, xo_s[:, p : p + rows].reshape(total, taps))
        grads_ref[p * taps : (p + 1) * taps, :] = g_in.T.astype(BF)
    hqs = jnp.concatenate([hq_s[:, p : p + rows].reshape(total, 384) for p in range(3)], axis=-1)
    g_out = dot_rows(own, hqs)
    for t in range(9):
        grads_ref[(9 + t) * half : (10 + t) * half, :] = g_out[half:, t * 128 : (t + 1) * 128].astype(BF)
    used = 18 * half + 2 * channels
    grads_ref[18 * half : used, :] = g_pool.astype(BF)
    if used < grads_ref.shape[0]:
        grads_ref[used:, :] = jnp.zeros((grads_ref.shape[0] - used, 128), BF)
    hid_copy.wait()
    dpre_copy.wait()


def output_kernel(*refs):
    (hid_ref, dpre_ref, w2_ref), refs = refs[:3], refs[3:]
    tiles, out_refs = refs[: len(refs) // 2], refs[len(refs) // 2 :]
    _, inner, width, _ = hid_ref.shape
    rows = inner - 2
    cols = out_refs[0].shape[2]

    def shifts(ref, s):
        v = ref[s].astype(F32)
        return [(pltpu.roll(v, width - 2 * q, 1) if q else v)[:, :cols] for q in range(3)]

    for d, (tile, out_ref) in enumerate(zip(tiles, out_refs)):

        def piece(j, carry):
            s = 2 * d + j
            both = jnp.concatenate(shifts(hid_ref, s) + shifts(dpre_ref, s), axis=-1).astype(BF)
            depth = both.shape[-1]
            acc = dot(both[0:rows].reshape(rows * cols, depth), w2_ref[0])
            acc += dot(both[1 : 1 + rows].reshape(rows * cols, depth), w2_ref[1])
            acc += dot(both[2 : 2 + rows].reshape(rows * cols, depth), w2_ref[2])
            own = pltpu.roll(tile[j].astype(F32), width - 4, 1)[:, :cols]
            out_ref[j] = (own + acc.reshape(rows, cols, 128)).astype(BF)
            return carry

        lax.fori_loop(0, 2, piece, 0)


def sum_kernel(parts_ref, out_ref):
    total = jnp.sum(parts_ref[...].astype(F32), axis=0)
    out_ref[...] = jnp.broadcast_to(total[None], out_ref.shape).astype(out_ref.dtype)


def finish_kernel(scale, full_ref, in_ref, out_ref, pool_ref):
    start = 0
    for ref in (in_ref, out_ref, pool_ref):
        size = ref.shape[0]
        ref[...] = full_ref[start : start + size].astype(F32) * scale
        start += size


def block(ensemble, cotangent, conv_in, pool_weight, conv_out):
    mem_local, _, rows, lon = ensemble.shape
    groups = lax.axis_size(MEMBER)
    bands = lax.axis_size(LAT)
    channels = conv_in.shape[-1]
    cols = lon // groups
    width = (cols + 4) * mem_local
    vspec = pl.BlockSpec(memory_space=pltpu.VMEM)
    sspec = pl.BlockSpec(memory_space=pltpu.SMEM)
    vm = pltpu.VMEM
    me = lax.axis_index(MEMBER).astype(jnp.int32).reshape(1)
    chips = groups // 2
    keep, give = pl.pallas_call(
        pack_kernel,
        out_shape=[vm((chips, rows, width, 128), BF)] * 2,
        in_specs=[sspec, vspec, vspec],
        out_specs=[vspec] * 2,
        scratch_shapes=[vm((rows, 2 * lon + 8, 128), F32)],
        name="pack",
    )(me, ensemble, cotangent)
    got = swap(give, 0, 1, groups)
    tiles = pl.pallas_call(
        pair_kernel,
        out_shape=[vm((2, rows, width, 128), BF)] * chips,
        in_specs=[vspec] * 2,
        out_specs=[vspec] * chips,
        name="pair",
    )(*near(keep, got))
    tiles = [tiles[0]] + [swap(tiles[i], ORDER[i], 0, groups) for i in range(1, chips)]
    head, tail = pl.pallas_call(
        edges_kernel,
        out_shape=[vm((groups, 2, width, 128), BF)] * 2,
        in_specs=[vspec] * chips,
        out_specs=[vspec] * 2,
        name="edges",
    )(*near(*tiles))
    top = lax.ppermute(tail, LAT, [(i, i + 1) for i in range(bands - 1)])
    bot = lax.ppermute(head, LAT, [(i + 1, i) for i in range(bands - 1)])

    flip_in = jnp.transpose(conv_in[::-1, ::-1], (0, 1, 3, 2))
    flip_out = jnp.transpose(conv_out[::-1, ::-1], (0, 1, 3, 2))
    z1 = jnp.zeros_like(conv_in)
    z2 = jnp.zeros_like(conv_out)
    w1 = jnp.concatenate(
        [jnp.concatenate([conv_in, z1], axis=3), jnp.concatenate([z1, flip_out], axis=3)], axis=2
    ).reshape(1152, 256)
    w2 = jnp.concatenate(
        [
            jnp.concatenate([conv_out, z2], axis=3).reshape(3, 384, 128),
            jnp.concatenate([z2, flip_in], axis=3).reshape(3, 384, 128),
        ],
        axis=1,
    )
    lat = jnp.stack([lax.axis_index(LAT), jnp.int32(bands * rows)]).astype(jnp.int32)
    inner = rows + 2
    plane = (inner, WIDE, channels)
    used = 18 * (channels // 2) + 2 * channels
    slices, copies = lax.axis_size(PLANE), lax.axis_size(REST)
    per = -(-used // (8 * slices)) * 8
    shifted = (groups, inner, cols * mem_local, 384)
    compact = (groups, inner, width, channels)
    far_part = vm((2,) + compact[1:], BF)
    first_part = pltpu.HBM((groups - 2,) + compact[1:], BF)
    hspec = pl.BlockSpec(memory_space=pltpu.HBM)
    grads, hid_far, dpre_far, hid, dpre = pl.pallas_call(
        tile_kernel,
        out_shape=[vm((slices * per, channels), BF), far_part, far_part, first_part, first_part],
        in_specs=[sspec] + [vspec] * (chips + 4) + [hspec],
        out_specs=[vspec] * 3 + [hspec] * 2,
        scratch_shapes=[
            vm((groups, rows, width, 128), BF),
            vm((groups,) + plane, F32),
            vm((groups,) + plane, F32),
            vm((groups,) + plane, F32),
            vm(shifted[:3] + (192,), BF),
            vm((groups, rows, cols * mem_local, 128), BF),
            vm(shifted, BF),
            vm((groups, rows, cols * mem_local, channels), BF),
            vm(compact, BF),
            vm(compact, BF),
            vm(plane, F32),
            vm(plane, F32),
            vm(plane, F32),
            vm(plane, F32),
            vm(plane, F32),
            pltpu.SemaphoreType.DMA((2,)),
        ],
        compiler_params=pltpu.CompilerParams(vmem_limit_bytes=48 * 1024 * 1024),
        name="tile",
    )(lat, *near(*tiles, top, bot, w1, pool_weight), w2)

    def outputs(hid, dpre, *sources):
        n = len(sources)
        return pl.pallas_call(
            output_kernel,
            out_shape=[vm((2, rows, cols * mem_local, 128), BF)] * n,
            in_specs=[vspec] * (n + 3),
            out_specs=[vspec] * n,
            name="output",
        )(hid, dpre, w2, *near(*sources))

    far_piece = outputs(*near(hid_far, dpre_far), tiles[-1])
    pieces = [*outputs(hid, dpre, *tiles[:-1]), *far_piece]

    def exchange(value, axis):
        return lax.all_to_all(value, axis, split_axis=0, concat_axis=0, tiled=True)

    def add_up(parts, count):
        return pl.pallas_call(
            sum_kernel,
            out_shape=vm((count,) + parts.shape[1:], BF),
            in_specs=[vspec],
            out_specs=vspec,
            name="total",
        )(*near(parts))

    parts = exchange(grads.reshape(slices, per, channels), PLANE)
    far = swap(pieces[3], chips - ORDER[3], 0, groups)
    parts, pieces[1], pieces[2] = lax.optimization_barrier((parts, pieces[1], pieces[2]))
    pieces[1:3] = [swap(piece, chips - d, 0, groups) for d, piece in zip(ORDER[1:3], pieces[1:3])]
    pieces[3] = far
    parts = add_up(parts, copies)
    parts = exchange(parts, REST)
    parts = add_up(parts, slices)
    other = pl.pallas_call(
        other_kernel,
        out_shape=vm((chips, rows, cols * mem_local, 128), BF),
        in_specs=[vspec] * chips,
        out_specs=vspec,
        name="other",
    )(*near(*pieces))
    theirs = swap(other, 0, 1, groups)
    full = exchange(parts, PLANE).reshape(slices * per, channels)
    members = mem_local * groups
    scale = 1.0 / math.sqrt(members * bands * rows * lon)
    half = channels // 2
    grad_in, grad_out, grad_pool = pl.pallas_call(
        functools.partial(finish_kernel, scale),
        out_shape=[jax.ShapeDtypeStruct((n, channels), F32) for n in (9 * half, 9 * half, 2 * channels)],
        in_specs=[vspec],
        out_specs=[vspec] * 3,
        name="finish",
    )(*near(full))
    grad_in = grad_in.reshape(3, 3, half, channels)
    grad_out = grad_out.reshape(3, 3, half, channels).transpose(0, 1, 3, 2)

    encoded, d_input = pl.pallas_call(
        unpack_kernel,
        out_shape=[jax.ShapeDtypeStruct(ensemble.shape, BF)] * 2,
        in_specs=[sspec] + [vspec] * (chips + 1),
        out_specs=[vspec] * 2,
        scratch_shapes=[vm((rows, 2 * lon, 128), F32)],
        name="unpack",
    )(me, *near(*pieces, theirs))
    return encoded, d_input, grad_in, grad_pool, grad_out


def solution(mesh):
    groups, bands = mesh.devices.shape
    lat = (4, 2, 4) if bands == 32 else (1, bands, 1)
    fine = Mesh(mesh.devices.reshape((groups // 2, 2) + lat), MEMBER + LAT)
    fields = P(MEMBER, None, LAT, None)
    return jax.shard_map(
        block,
        mesh=fine,
        in_specs=(fields, fields, P(), P(), P()),
        out_specs=(fields, fields, P(), P(), P()),
        check_vma=False,
    )
```

```python
import functools
import math

import jax
import jax.numpy as jnp
from jax import lax
from jax.experimental import pallas as pl
from jax.experimental.pallas import tpu as pltpu
from jax.sharding import Mesh
from jax.sharding import PartitionSpec as P


BF = jnp.bfloat16
F32 = jnp.float32
WIDE = 80


MEMBER = ("zh", "core")
LAT = ("y", "zl", "x")
PLANE = ("y", "x")
REST = ("zh", "core", "zl")
ORDER = (0, 1, 3, 2)


def swap(value, steps, cross, groups):
    chips = groups // 2
    pairs = [
        (2 * z + c, 2 * ((z + steps) % chips) + (c + cross) % 2) for z in range(chips) for c in range(2)
    ]
    return lax.ppermute(value, MEMBER, pairs)


def column_block(device, steps, cross, groups):
    chips = groups // 2
    return 2 * lax.rem(device // 2 + steps, chips) + lax.rem(device + cross, 2)


def near(*values):
    return [pltpu.with_memory_space_constraint(v, pltpu.VMEM) for v in values]


def sigmoid(v):
    return 1.0 / (1.0 + jnp.exp(-v))


def split2(v):
    a = v.astype(BF)
    return a, (v - a.astype(F32)).astype(BF)


def dot(a, b):
    return jnp.dot(a, b, preferred_element_type=F32)


def dot_t(a, b, dims):
    return lax.dot_general(a, b, (dims, ((), ())), preferred_element_type=F32)


def dot_rows(a, b):
    return dot_t(a, b, ((0,), (0,)))


def pack_kernel(me_ref, ens_ref, cot_ref, keep_ref, give_ref, plane):
    chips, _, width, _ = keep_ref.shape
    mem_local, _, rows, lon = ens_ref.shape
    for m in range(mem_local):
        for r in range(rows):
            both = jnp.concatenate([ens_ref[m, :, r, :], cot_ref[m, :, r, :]], axis=0).astype(F32).T
            plane[r, pl.ds(4 + m, lon, stride=2), :] = both
            plane[r, pl.ds(m, 2, stride=2), :] = both[lon - 2 :]
            plane[r, pl.ds(4 + 2 * lon + m, 2, stride=2), :] = both[:2]
    for d in range(chips):
        for cross, ref in enumerate((keep_ref, give_ref)):
            k = column_block(me_ref[0], ORDER[d], cross, 2 * chips)
            for r in range(rows):
                ref[d, r] = plane[r, pl.ds(pl.multiple_of(k * (width - 8), 8), width), :].astype(BF)


def pair_kernel(keep_ref, got_ref, *out_refs):
    for d, ref in enumerate(out_refs):
        ref[0] = keep_ref[d]
        ref[1] = got_ref[d]


def edges_kernel(*refs):
    tiles, (head_ref, tail_ref) = refs[:-2], refs[-2:]
    rows = tiles[0].shape[1]
    for d, tile in enumerate(tiles):
        head_ref[2 * d : 2 * d + 2] = tile[:, :2]
        tail_ref[2 * d : 2 * d + 2] = tile[:, rows - 2 :]


def other_kernel(*refs):
    for d, tile in enumerate(refs[:-1]):
        refs[-1][d] = tile[1]


def unpack_kernel(me_ref, *refs):
    tiles, (theirs_ref, enc_ref, din_ref, plane) = refs[:-4], refs[-4:]
    chips = len(tiles)
    mem_local, half, rows, lon = enc_ref.shape
    width = theirs_ref.shape[2]
    for d in range(chips):
        for cross in range(2):
            k = column_block(me_ref[0], ORDER[d], cross, 2 * chips)
            for r in range(rows):
                piece = theirs_ref[d, r] if cross else tiles[d][0, r]
                plane[r, pl.ds(pl.multiple_of(k * width, 8), width), :] = piece.astype(F32)
    for m in range(mem_local):
        for r in range(rows):
            both = plane[r, pl.ds(m, lon, stride=2), :].T.astype(BF)
            enc_ref[m, :, r, :] = both[:half]
            din_ref[m, :, r, :] = both[half:]


def tile_kernel(
    lat_ref, t0, t1, t2, t3, top_ref, bot_ref, w1_ref, pool_ref, _,
    grads_ref, hid_ref, dpre_ref,
    own_ref, pre_s, dh_s, act_s, xo_s, oc_s, hq_s, dpo_s, hid_s, dpre_s, sum_s, var_s, shared_s, ca_s, cs_s, sems,
):
    srcs, rows, width, _ = own_ref.shape
    inner = rows + 2
    cols = xo_s.shape[2]
    nlat = lat_ref[1]
    for d, tile in enumerate((t0, t1, t2, t3)):
        own_ref[2 * d : 2 * d + 2] = tile[...]
    members = 2 * srcs
    channels = pre_s.shape[-1]
    shape = (inner, WIDE, channels)

    def up(v, n):
        return pltpu.roll(v, WIDE - n, 1) if n else v

    parity = lax.broadcasted_iota(jnp.int32, shape, 1) % 2

    def pair_sum(v):
        return v + jnp.where(parity == 0, up(v, 1), pltpu.roll(v, 1, 1))

    row_id = lax.broadcasted_iota(jnp.int32, shape, 0) + lat_ref[0] * rows - 1
    inside = jnp.logical_and(row_id >= 0, row_id < nlat)

    sum_s[...] = jnp.zeros(shape, F32)

    def first(s, carry):
        x = jnp.concatenate([top_ref[s], own_ref[s], bot_ref[s]], axis=0).astype(F32)
        x = jnp.concatenate([x, jnp.zeros((rows + 4, WIDE - width, 128), F32)], axis=1)
        x1, x2, x3 = up(x, 2), up(x, 4), up(x, 6)
        xs = jnp.concatenate([x, x1, x2], axis=-1).astype(BF)
        own = [v[1 : 1 + inner, :cols] for v in (x1, x2, x3)]
        half = channels // 2
        xo_s[s] = jnp.concatenate([v[..., :half] for v in own], axis=-1).astype(BF)
        oc_s[s] = own[1][1 : 1 + rows].astype(BF)
        xs = jnp.concatenate([xs[p : p + inner] for p in range(3)], axis=-1)
        acc = dot(xs.reshape(inner * WIDE, 1152), w1_ref[...])
        pre = acc[:, :channels].reshape(shape)
        pre_s[s] = pre
        dh_s[s] = acc[:, channels:].reshape(shape)
        act = (pre * sigmoid(pre)).astype(BF).astype(F32)
        act_s[s] = act
        sum_s[...] += act
        return carry

    lax.fori_loop(0, srcs, first, 0)
    average = pair_sum(sum_s[...]) * (1.0 / members)
    sum_s[...] = average
    var_s[...] = jnp.zeros(shape, F32)

    def second(s, carry):
        d = act_s[s] - sum_s[...]
        var_s[...] += d * d
        return carry

    lax.fori_loop(0, srcs, second, 0)
    spread = jnp.sqrt(pair_sum(var_s[...]) * (1.0 / members) + 0.1)
    var_s[...] = spread
    stats = jnp.concatenate([sum_s[...], spread], axis=-1).reshape(inner * WIDE, 2 * channels)
    s1, s2 = split2(stats)
    pool = pool_ref[...]
    shared_s[...] = (dot(s1, pool) + dot(s2, pool)).reshape(shape)
    ca_s[...] = jnp.zeros(shape, F32)

    def third(s, carry):
        zed = act_s[s] + shared_s[...]
        sig = sigmoid(zed)
        hid = jnp.where(inside, (zed * sig).astype(BF).astype(F32), 0.0)
        dz = (dh_s[s] * (sig * (1.0 + zed * (1.0 - sig)))).astype(BF).astype(F32)
        dh_s[s] = dz
        ca_s[...] += dz
        hid_s[s] = hid[:, :width].astype(BF)
        hq_s[s] = jnp.concatenate([up(hid, 2 * q)[:, :cols] for q in range(3)], axis=-1).astype(BF)
        return carry

    lax.fori_loop(0, srcs, third, 0)
    hid_copy = pltpu.make_async_copy(hid_s, hid_ref, sems.at[0])
    hid_copy.start()
    d_shared = pair_sum(ca_s[...])
    d1, d2 = split2(d_shared.reshape(inner * WIDE, channels))
    last = ((1,), (1,))
    d_stats = dot_t(d1, pool, last) + dot_t(d2, pool, last)
    ca_s[...] = (d_stats[:, :channels] * (1.0 / members)).reshape(shape)
    cs_s[...] = d_stats[:, channels:].reshape(shape) / (members * var_s[...])
    r_id = lax.broadcasted_iota(jnp.int32, shape, 0)
    c_id = lax.broadcasted_iota(jnp.int32, shape, 1)
    mine = (r_id >= 1) & (r_id <= rows) & (c_id >= 2) & (c_id < 2 + cols) & (parity == 0)
    e1, e2 = split2(jnp.where(mine, d_shared, 0.0).reshape(inner * WIDE, channels))
    g_pool = dot_rows(s1, e1) + dot_rows(s1, e2) + dot_rows(s2, e1)

    def fourth(s, carry):
        pre = pre_s[s]
        sig = sigmoid(pre)
        d_act = dh_s[s] + ca_s[...] + cs_s[...] * (act_s[s] - sum_s[...])
        dp = jnp.where(inside, d_act * (sig * (1.0 + pre * (1.0 - sig))), 0.0).astype(BF).astype(F32)
        dpre_s[s] = dp[:, :width].astype(BF)
        dpo_s[s] = up(dp, 2)[1 : 1 + rows, :cols].astype(BF)
        return carry

    lax.fori_loop(0, srcs, fourth, 0)
    dpre_copy = pltpu.make_async_copy(dpre_s, dpre_ref, sems.at[1])
    dpre_copy.start()

    total = srcs * rows * cols
    dpo = dpo_s[...].reshape(total, channels)
    own = oc_s[...].reshape(total, 128)
    half = channels // 2
    taps = 3 * half
    for p in range(3):
        g_in = dot_rows(dpo, xo_s[:, p : p + rows].reshape(total, taps))
        grads_ref[p * taps : (p + 1) * taps, :] = g_in.T.astype(BF)
    hqs = jnp.concatenate([hq_s[:, p : p + rows].reshape(total, 384) for p in range(3)], axis=-1)
    g_out = dot_rows(own, hqs)
    for t in range(9):
        grads_ref[(9 + t) * half : (10 + t) * half, :] = g_out[half:, t * 128 : (t + 1) * 128].astype(BF)
    used = 18 * half + 2 * channels
    grads_ref[18 * half : used, :] = g_pool.astype(BF)
    if used < grads_ref.shape[0]:
        grads_ref[used:, :] = jnp.zeros((grads_ref.shape[0] - used, 128), BF)
    hid_copy.wait()
    dpre_copy.wait()


def output_kernel(t0, t1, t2, t3, hid_ref, dpre_ref, w2_ref, *out_refs):
    _, inner, width, _ = hid_ref.shape
    rows = inner - 2
    cols = out_refs[0].shape[2]

    def shifts(ref, s):
        v = ref[s].astype(F32)
        return [(pltpu.roll(v, width - 2 * q, 1) if q else v)[:, :cols] for q in range(3)]

    for d, (tile, out_ref) in enumerate(zip((t0, t1, t2, t3), out_refs)):

        def piece(j, carry):
            both = jnp.concatenate(shifts(hid_ref, 2 * d + j) + shifts(dpre_ref, 2 * d + j), axis=-1).astype(BF)
            depth = both.shape[-1]
            acc = dot(both[0:rows].reshape(rows * cols, depth), w2_ref[0])
            acc += dot(both[1 : 1 + rows].reshape(rows * cols, depth), w2_ref[1])
            acc += dot(both[2 : 2 + rows].reshape(rows * cols, depth), w2_ref[2])
            own = pltpu.roll(tile[j].astype(F32), width - 4, 1)[:, :cols]
            out_ref[j] = (own + acc.reshape(rows, cols, 128)).astype(BF)
            return carry

        lax.fori_loop(0, 2, piece, 0)


def sum_kernel(parts_ref, out_ref):
    total = jnp.sum(parts_ref[...].astype(F32), axis=0)
    out_ref[...] = jnp.broadcast_to(total[None], out_ref.shape).astype(out_ref.dtype)


def finish_kernel(scale, full_ref, in_ref, out_ref, pool_ref):
    start = 0
    for ref in (in_ref, out_ref, pool_ref):
        size = ref.shape[0]
        ref[...] = full_ref[start : start + size].astype(F32) * scale
        start += size


def block(ensemble, cotangent, conv_in, pool_weight, conv_out):
    mem_local, _, rows, lon = ensemble.shape
    groups = lax.axis_size(MEMBER)
    bands = lax.axis_size(LAT)
    channels = conv_in.shape[-1]
    cols = lon // groups
    width = (cols + 4) * mem_local
    vspec = pl.BlockSpec(memory_space=pltpu.VMEM)
    sspec = pl.BlockSpec(memory_space=pltpu.SMEM)
    vm = pltpu.VMEM
    me = lax.axis_index(MEMBER).astype(jnp.int32).reshape(1)
    chips = groups // 2
    keep, give = pl.pallas_call(
        pack_kernel,
        out_shape=[vm((chips, rows, width, 128), BF)] * 2,
        in_specs=[sspec, vspec, vspec],
        out_specs=[vspec] * 2,
        scratch_shapes=[vm((rows, 2 * lon + 32, 128), F32)],
        name="pack",
    )(me, ensemble, cotangent)
    got = swap(give, 0, 1, groups)
    tiles = pl.pallas_call(
        pair_kernel,
        out_shape=[vm((2, rows, width, 128), BF)] * chips,
        in_specs=[vspec] * 2,
        out_specs=[vspec] * chips,
        name="pair",
    )(*near(keep, got))
    tiles = [tiles[0]] + [swap(tiles[i], ORDER[i], 0, groups) for i in range(1, chips)]
    head, tail = pl.pallas_call(
        edges_kernel,
        out_shape=[vm((groups, 2, width, 128), BF)] * 2,
        in_specs=[vspec] * chips,
        out_specs=[vspec] * 2,
        name="edges",
    )(*near(*tiles))
    top = lax.ppermute(tail, LAT, [(i, i + 1) for i in range(bands - 1)])
    bot = lax.ppermute(head, LAT, [(i + 1, i) for i in range(bands - 1)])

    flip_in = jnp.transpose(conv_in[::-1, ::-1], (0, 1, 3, 2))
    flip_out = jnp.transpose(conv_out[::-1, ::-1], (0, 1, 3, 2))
    z1 = jnp.zeros_like(conv_in)
    z2 = jnp.zeros_like(conv_out)
    w1 = jnp.concatenate(
        [jnp.concatenate([conv_in, z1], axis=3), jnp.concatenate([z1, flip_out], axis=3)], axis=2
    ).reshape(1152, 256)
    w2 = jnp.concatenate(
        [
            jnp.concatenate([conv_out, z2], axis=3).reshape(3, 384, 128),
            jnp.concatenate([z2, flip_in], axis=3).reshape(3, 384, 128),
        ],
        axis=1,
    )
    lat = jnp.stack([lax.axis_index(LAT), jnp.int32(bands * rows)]).astype(jnp.int32)
    inner = rows + 2
    plane = (inner, WIDE, channels)
    used = 18 * (channels // 2) + 2 * channels
    slices, copies = lax.axis_size(PLANE), lax.axis_size(REST)
    per = -(-used // (8 * slices)) * 8
    shifted = (groups, inner, cols * mem_local, 384)
    compact = pltpu.HBM((groups, inner, width, channels), BF)
    hspec = pl.BlockSpec(memory_space=pltpu.HBM)
    grads, hid, dpre = pl.pallas_call(
        tile_kernel,
        out_shape=[vm((slices * per, channels), BF), compact, compact],
        in_specs=[sspec] + [vspec] * (chips + 5),
        out_specs=[vspec, hspec, hspec],
        scratch_shapes=[
            vm((groups, rows, width, 128), BF),
            vm((groups,) + plane, F32),
            vm((groups,) + plane, F32),
            vm((groups,) + plane, F32),
            vm(shifted[:3] + (192,), BF),
            vm((groups, rows, cols * mem_local, 128), BF),
            vm(shifted, BF),
            vm((groups, rows, cols * mem_local, channels), BF),
            vm(compact.shape, BF),
            vm(compact.shape, BF),
            vm(plane, F32),
            vm(plane, F32),
            vm(plane, F32),
            vm(plane, F32),
            vm(plane, F32),
            pltpu.SemaphoreType.DMA((2,)),
        ],
        compiler_params=pltpu.CompilerParams(vmem_limit_bytes=48 * 1024 * 1024),
        name="tile",
    )(lat, *near(*tiles, top, bot, w1, pool_weight, w2))
    pieces = list(pl.pallas_call(
        output_kernel,
        out_shape=[vm((2, rows, cols * mem_local, 128), BF)] * chips,
        in_specs=[vspec] * (chips + 3),
        out_specs=[vspec] * chips,
        name="output",
    )(*near(*tiles), hid, dpre, *near(w2)))

    def exchange(value, axis):
        return lax.all_to_all(value, axis, split_axis=0, concat_axis=0, tiled=True)

    def add_up(parts, count):
        return pl.pallas_call(
            sum_kernel,
            out_shape=vm((count,) + parts.shape[1:], BF),
            in_specs=[vspec],
            out_specs=vspec,
            name="total",
        )(*near(parts))

    parts = exchange(grads.reshape(slices, per, channels), PLANE)
    far = swap(pieces[3], chips - ORDER[3], 0, groups)
    parts, pieces[1], pieces[2] = lax.optimization_barrier((parts, pieces[1], pieces[2]))
    pieces[1:3] = [swap(piece, chips - d, 0, groups) for d, piece in zip(ORDER[1:3], pieces[1:3])]
    pieces[3] = far
    parts = add_up(parts, copies)
    parts = exchange(parts, REST)
    parts = add_up(parts, slices)
    other = pl.pallas_call(
        other_kernel,
        out_shape=vm((chips, rows, cols * mem_local, 128), BF),
        in_specs=[vspec] * chips,
        out_specs=vspec,
        name="other",
    )(*near(*pieces))
    theirs = swap(other, 0, 1, groups)
    full = exchange(parts, PLANE).reshape(slices * per, channels)
    members = mem_local * groups
    scale = 1.0 / math.sqrt(members * bands * rows * lon)
    half = channels // 2
    grad_in, grad_out, grad_pool = pl.pallas_call(
        functools.partial(finish_kernel, scale),
        out_shape=[jax.ShapeDtypeStruct((n, channels), F32) for n in (9 * half, 9 * half, 2 * channels)],
        in_specs=[vspec],
        out_specs=[vspec] * 3,
        name="finish",
    )(*near(full))
    grad_in = grad_in.reshape(3, 3, half, channels)
    grad_out = grad_out.reshape(3, 3, half, channels).transpose(0, 1, 3, 2)

    encoded, d_input = pl.pallas_call(
        unpack_kernel,
        out_shape=[jax.ShapeDtypeStruct(ensemble.shape, BF)] * 2,
        in_specs=[sspec] + [vspec] * (chips + 1),
        out_specs=[vspec] * 2,
        scratch_shapes=[vm((rows, 2 * lon, 128), F32)],
        name="unpack",
    )(me, *near(*pieces, theirs))
    return encoded, d_input, grad_in, grad_pool, grad_out


def solution(mesh):
    groups, bands = mesh.devices.shape
    lat = (4, 2, 4) if bands == 32 else (1, bands, 1)
    fine = Mesh(mesh.devices.reshape((groups // 2, 2) + lat), MEMBER + LAT)
    fields = P(MEMBER, None, LAT, None)
    return jax.shard_map(
        block,
        mesh=fine,
        in_specs=(fields, fields, P(), P(), P()),
        out_specs=(fields, fields, P(), P(), P()),
        check_vma=False,
    )
```
